256 devices in a mesh: sub: 64 (over z, y, core), grp: 4 (over x).
Axes of the slice: x: 4, y: 4, z: 8, core: 2. Of those that a mesh axis runs over, the one named last changes fastest.
Arguments:
- residual: float32 [16, 64, 4, 512], P(None, 'sub', 'grp'), may hold values from -6 to 6
- bounds: float32 [2], replicated, may hold values from 0.2 to 14, as said below
- local_inverse: bfloat16 [64, 4, 1024, 1024], P('sub', 'grp'), may hold values from -1 to 2
- corner_basis: bfloat16 [64, 4, 24, 1024], P('sub', 'grp'), may hold values from -1 to 1
- corner_map: int32 [64, 4, 24], P('sub', 'grp'), may hold values from 0 to 255
- coarse_inverse: float32 [256, 256], P(('sub', 'grp')), may hold values from -1 to 2, as said below
Outputs:
- basis: float32 [5, 16, 64, 4, 512], P(None, None, 'sub', 'grp')
- gram: float32 [80, 80], replicated
The draws below stay inside these ranges and needn't reach their ends.
Inputs may be any that keep to these rules, and one draw needn't show every extreme that they name: bounds[0] lies in 0.2 to 0.4 and bounds[1] in 10 to 14. `coarse_inverse`: symmetric.
All inputs are finite; a program needn't handle non-finite values.
Results may differ from the reference program's by a relative error of at most 0.0022.
Values may be sent and summed in bfloat16 or wider, within the bound.
No kernel may reach another device: no remote copies, remote signals or barrier semaphores. Data moves between devices by JAX's collectives and lax.ppermute only.
A program may use at most 64 MiB of HBM per device.

```python
import jax
import jax.numpy as jnp
from jax import lax

FACE = 256
RHS = 16
S_STEP = 2
CORNERS = 24
CO_DEV = 1
NSUBS = 64
NGRPS = 4
NCO = 256
GRAM = 80


def draw_bounds(key, part):
    first, second = jax.random.split(jax.random.fold_in(key, 11))
    lower = jax.random.uniform(first, (), jnp.float32, 0.2, 0.4)
    upper = jax.random.uniform(second, (), jnp.float32, 10.0, 14.0)
    return jnp.stack([lower, upper])


def draw_local_inverse(key, part):
    width = 4 * FACE
    first, second = jax.random.split(jax.random.fold_in(key, 23))
    diagonal_part = jax.random.uniform(first, (NSUBS, NGRPS, width), jnp.float32, 0.5, 1.0)
    noise_part = jax.random.normal(second, (NSUBS, NGRPS, width, width), jnp.float32) * (0.35 / jnp.sqrt(1.0 * width))
    noise_part = jnp.clip(noise_part, -0.5, 0.5)
    whole = noise_part + diagonal_part[..., None] * jnp.eye(width, dtype=jnp.float32)
    return whole.astype(jnp.bfloat16)


def draw_corner_basis(key, part):
    width = 4 * FACE
    spread = jnp.sqrt(4.0 * CO_DEV / (1.0 * CORNERS * width))
    values = jax.random.normal(jax.random.fold_in(key, 53), (NSUBS, NGRPS, CORNERS, width), jnp.float32)
    values = jnp.clip(values, -4.0, 4.0) * spread
    return values.astype(jnp.bfloat16)


def draw_coarse_inverse(key, part):
    first, second = jax.random.split(jax.random.fold_in(key, 37))
    diagonal_part = jnp.exp(jax.random.uniform(first, (NCO,), jnp.float32, jnp.log(0.3), 0.0))
    noise_part = jax.random.normal(second, (NCO, NCO), jnp.float32) * (0.4 / jnp.sqrt(1.0 * NCO))
    noise_part = jnp.clip(0.5 * (noise_part + noise_part.T), -0.5, 0.5)
    return noise_part + diagonal_part[:, None] * jnp.eye(NCO, dtype=jnp.float32)


def touch_ends(array, own_key, smallest, high):
    longest = array.shape.index(max(array.shape))
    spots = []
    for shift in (0, 1):
        where = [jax.random.randint(jax.random.fold_in(own_key, axis), (), 0, length) for axis, length in enumerate(array.shape)]
        where[longest] = (where[longest] + shift) % array.shape[longest]
        spots.append(tuple(where))
    return array.at[spots[0]].set(smallest).at[spots[1]].set(high)


def levels(stream_key, extent, pieces, smallest, top_value):
    loudness, own = 1.0, jax.random.fold_in(stream_key, 6)
    for position, parts in pieces:
        steps = jnp.exp(jax.random.uniform(jax.random.fold_in(own, position), (parts,), jnp.float32, smallest / len(pieces), top_value / len(pieces)))
        loudness = loudness * jnp.repeat(steps, extent[position] // parts).reshape([-1 if axis == position else 1 for axis in range(len(extent))])
    return loudness


def scatter_about(rng, shape, scale, reach, shards=(), held_as=jnp.bfloat16):
    factor_of = levels(rng, shape, shards, -0.22, 0.18) if shards else 1.0
    drawn = jax.random.normal(rng, shape, jnp.float32) * scale * factor_of
    return jnp.minimum(jnp.maximum(drawn, -reach), reach).astype(held_as)


def setup_inputs(seed: int = 0) -> dict:
    arg_keys = jax.random.split(jax.random.key(seed), 7)
    residual = scatter_about(arg_keys[0], (RHS, NSUBS, NGRPS, 2 * FACE), 1.0, 6.0, ((1, 64), (2, 4)), jnp.float32)
    bounds = draw_bounds(jax.random.fold_in(arg_keys[6], 71), 0)
    local_inverse = draw_local_inverse(jax.random.fold_in(arg_keys[6], 71), 0)
    corner_basis = draw_corner_basis(jax.random.fold_in(arg_keys[6], 71), 0)
    corner_map = touch_ends(jax.random.randint(arg_keys[4], (NSUBS, NGRPS, CORNERS), 0, NCO), jax.random.fold_in(arg_keys[4], 1), 0, NCO - 1).astype(jnp.int32)
    coarse_inverse = draw_coarse_inverse(jax.random.fold_in(arg_keys[6], 71), 0)
    return dict(residual=residual, bounds=bounds, local_inverse=local_inverse, corner_basis=corner_basis, corner_map=corner_map, coarse_inverse=coarse_inverse)


def apply_operator(block, local_inverse, corners_wide, corner_table, coarse_inverse):
    width = 4 * FACE
    packed = block.astype(jnp.bfloat16)
    up_sub = packed[..., :FACE]
    up_grp = packed[..., FACE:]
    low_sub = jnp.roll(up_sub, 1, axis=1)
    low_grp = jnp.roll(up_grp, 1, axis=2)
    load_rows = jnp.concatenate([up_sub, -low_sub, up_grp, -low_grp], axis=-1)
    per_device = jnp.transpose(load_rows, (1, 2, 0, 3)).reshape(NSUBS * NGRPS, RHS, width)
    inverses = local_inverse.reshape(NSUBS * NGRPS, width, width)
    local_part = lax.map(lambda pair: jnp.dot(pair[0], pair[1], preferred_element_type=jnp.float32), (per_device, inverses))
    weights = jnp.einsum('drk,dck->drc', per_device.astype(jnp.float32), corners_wide, precision=lax.Precision.HIGHEST)
    coarse_load = jnp.einsum('drc,dcn->rn', weights, corner_table, precision=lax.Precision.HIGHEST)
    coarse_value = jnp.dot(coarse_load, coarse_inverse, precision=lax.Precision.HIGHEST)
    picked = jnp.einsum('rn,dcn->drc', coarse_value, corner_table, precision=lax.Precision.HIGHEST)
    displaced = local_part + jnp.einsum('drc,dck->drk', picked, corners_wide, precision=lax.Precision.HIGHEST)
    displaced = displaced.reshape(NSUBS, NGRPS, RHS, width)
    jump_sub = displaced[..., :FACE] - jnp.roll(displaced[..., FACE:2 * FACE], -1, axis=0)
    jump_grp = displaced[..., 2 * FACE:3 * FACE] - jnp.roll(displaced[..., 3 * FACE:], -1, axis=1)
    return jnp.transpose(jnp.concatenate([jump_sub, jump_grp], axis=-1), (2, 0, 1, 3))


def reference(residual, bounds, local_inverse, corner_basis, corner_map, coarse_inverse):
    centre = (bounds[0] + bounds[1]) / 2.0
    radius = (bounds[1] - bounds[0]) / 2.0
    corners_wide = corner_basis.reshape(NSUBS * NGRPS, CORNERS, 4 * FACE).astype(jnp.float32)
    corner_ids = corner_map.reshape(NSUBS * NGRPS, CORNERS)
    corner_table = (corner_ids[:, :, None] == jnp.arange(NCO, dtype=jnp.int32)[None, None, :]).astype(jnp.float32)
    previous = residual
    image = apply_operator(previous, local_inverse, corners_wide, corner_table, coarse_inverse)
    current = (image - centre * previous) / radius
    blocks = [previous, current]
    for level in range(1, 2 * S_STEP):
        image = apply_operator(current, local_inverse, corners_wide, corner_table, coarse_inverse)
        following = 2.0 * (image - centre * current) / radius - previous
        blocks.append(following)
        previous, current = current, following
    basis = jnp.stack(blocks)
    merged = basis.reshape(GRAM, -1)
    gram = jnp.dot(merged, merged.T, precision=lax.Precision.HIGHEST) / (2.0 * FACE * NSUBS)
    return basis, gram
```

```python
import jax
import jax.numpy as jnp
from jax import lax
from jax.sharding import Mesh
from jax.sharding import PartitionSpec as P

BLOCKS = 5
SUB = ("z", "y", "core")
PLANE = ("y", "x")
HIGH = lax.Precision.HIGHEST


def hdot(a, b):
    return jnp.dot(a, b, precision=HIGH, preferred_element_type=jnp.float32)


def bdot(a, b):
    return jnp.dot(a, b, preferred_element_type=jnp.float32)


def along(x, axis, by):
    count = lax.axis_size(axis)
    return lax.ppermute(x, axis, [(i, (i + by) % count) for i in range(count)])


def exchange(x, axis):
    return lax.all_to_all(x, axis, split_axis=0, concat_axis=0, tiled=True)


def body(residual, bounds, local_inverse, corner_basis, corner_map, coarse_inverse):
    rhs, half = residual.shape[0], residual.shape[3]
    face = half // 2
    width = 2 * half
    inverse = local_inverse.reshape(width, width)
    corners = corner_basis.reshape(-1, width)
    count = corners.shape[0]
    ncoarse = coarse_inverse.shape[1]
    nz, ny, nc, nx = (lax.axis_size(a) for a in ("z", "y", "core", "x"))
    planes = ny * nx
    core = lax.axis_index("core")
    first = core == 0
    centre = (bounds[0] + bounds[1]) / 2.0
    radius = (bounds[1] - bounds[0]) / 2.0
    alpha = 2.0 / radius

    ids = corner_map.reshape(-1)
    low = ids % nx
    mid = (ids // nx) % nc
    ids = mid * (ncoarse // nc) + (ids // (nx * nc)) * nx + low
    own_row = coarse_inverse.reshape(nz * ny, nc, nx)
    own_row = own_row.transpose(1, 0, 2).reshape(1, ncoarse)

    block = residual.reshape(rhs, half)
    high = block.astype(jnp.bfloat16)
    rest = (block - high.astype(jnp.float32)).astype(jnp.bfloat16)
    id_row = jnp.pad(ids.astype(jnp.bfloat16), (0, face - count))[None]
    seg = [slice(i * face, (i + 1) * face) for i in range(4)]

    def up_pack(col, cseg):
        return jnp.concatenate([high[:, col], rest[:, col], corners[:, cseg], id_row], axis=0)

    def low_pack(cseg):
        return jnp.concatenate([corners[:, cseg], id_row], axis=0)

    from_prev_sub = along(up_pack(seg[0], seg[0]), SUB, 1)
    from_prev_grp = along(up_pack(seg[1], seg[2]), "x", 1)
    from_next_sub = along(low_pack(seg[1]), SUB, -1)
    from_next_grp = along(low_pack(seg[3]), "x", -1)

    def unpack_ids(row):
        return row[:count].astype(jnp.float32).astype(jnp.int32)

    def one_hot(values):
        return (values[:, None] == jnp.arange(ncoarse, dtype=jnp.int32)[None, :]).astype(jnp.float32)

    k = 2 * rhs
    ids_all = jnp.concatenate(
        [
            ids,
            unpack_ids(from_next_sub[count]),
            unpack_ids(from_prev_sub[k + count]),
            unpack_ids(from_next_grp[count]),
            unpack_ids(from_prev_grp[k + count]),
        ]
    )
    spread_own = one_hot(ids)
    spread = one_hot(ids_all)
    zero = jnp.zeros((count, face), jnp.bfloat16)
    wide = jnp.concatenate(
        [
            corners,
            jnp.concatenate([-from_next_sub[:count], zero, zero, zero], axis=1),
            jnp.concatenate([zero, -from_prev_sub[k : k + count], zero, zero], axis=1),
            jnp.concatenate([zero, zero, -from_next_grp[:count], zero], axis=1),
            jnp.concatenate([zero, zero, zero, -from_prev_grp[k : k + count]], axis=1),
        ],
        axis=0,
    )
    wide32 = wide.astype(jnp.float32)

    def whole(packed):
        return packed[:rhs].astype(jnp.float32) + packed[rhs:k].astype(jnp.float32)

    load0 = jnp.concatenate(
        [block[:, :face], -whole(from_prev_sub), block[:, face:], -whole(from_prev_grp)], axis=1
    )

    def jumps(u):
        next_sub = along(u[:, seg[1]], SUB, -1)
        next_grp = along(u[:, seg[3]], "x", -1)
        prev_sub = along(u[:, seg[0]], SUB, 1)
        prev_grp = along(u[:, seg[2]], "x", 1)
        return jnp.concatenate(
            [
                u[:, seg[0]] - next_sub,
                u[:, seg[1]] - prev_sub,
                u[:, seg[2]] - next_grp,
                u[:, seg[3]] - prev_grp,
            ],
            axis=1,
        )

    def local(load):
        return bdot(load.astype(jnp.bfloat16), inverse)

    def coarse_terms(load):
        return hdot(bdot(load.astype(jnp.bfloat16), corners.T), spread_own)

    def image_terms(u):
        return hdot(hdot(u, wide32.T), spread)

    def lifted(z):
        return hdot(hdot(z, spread.T), wide32)

    def swapped(v):
        return along(v, "core", 1)

    def halves(own, other):
        return jnp.concatenate([jnp.where(first, own, other), jnp.where(first, other, own)], axis=0)

    u0 = local(load0)
    w0_part = coarse_terms(load0)
    m_part = hdot(spread.T, hdot(bdot(wide, corners.T), spread_own))
    m_half = ncoarse // nc
    m_chunk = m_half // planes
    m_keep = jnp.where(first, m_part[:m_half], m_part[m_half:])
    m_send = jnp.where(first, m_part[m_half:], m_part[:m_half])
    got = swapped(jnp.concatenate([w0_part, m_send], axis=0))
    w0_part = w0_part + got[:rhs]
    m_keep = m_keep + got[rhs:]
    jump0 = jumps(u0)
    pad = jnp.zeros((planes, 7, ncoarse), jnp.float32)
    got = exchange(
        jnp.concatenate(
            [
                jnp.broadcast_to(w0_part, (planes, rhs, ncoarse)),
                m_keep.reshape(planes, m_chunk, ncoarse),
                jnp.broadcast_to(own_row, (planes, 1, ncoarse)),
                pad,
            ],
            axis=1,
        ),
        PLANE,
    )
    sums = jnp.sum(got[:, : rhs + m_chunk], axis=0)
    rows = got[:, rhs + m_chunk]
    got = exchange(
        jnp.broadcast_to(
            jnp.concatenate([sums, rows], axis=0), (nz, rhs + m_chunk + planes, ncoarse)
        ),
        "z",
    )
    sums = jnp.sum(got[:, : rhs + m_chunk], axis=0)
    w0, m_rows = sums[:rhs], sums[rhs:]
    a_half = got[:, rhs + m_chunk :].reshape(nz * planes, ncoarse)
    coarse = halves(a_half, swapped(a_half))
    z0 = hdot(w0, coarse)

    load1 = (jump0 + lifted(z0) - centre * load0) / radius
    u1 = local(load1)
    w1_part = coarse_terms(load1)
    g1_part = image_terms(u1)
    part = jnp.where(first, w1_part, g1_part) + swapped(jnp.where(first, g1_part, w1_part))
    jump1 = jumps(u1)
    got = exchange(
        jnp.broadcast_to(
            jnp.concatenate([part, m_rows], axis=0), (planes, rhs + m_chunk, ncoarse)
        ),
        PLANE,
    )
    part = jnp.sum(got[:, :rhs], axis=0)
    m_own = got[:, rhs:].reshape(m_half, ncoarse)
    m_full = halves(m_own, swapped(m_own))
    part = jnp.sum(exchange(jnp.broadcast_to(part, (nz, rhs, ncoarse)), "z"), axis=0)
    both = halves(part, swapped(part))
    w1, g1 = both[:rhs], both[rhs:]
    z1 = hdot(w1, coarse)
    w2 = alpha * (g1 + hdot(z1, m_full) - centre * w1) - w0
    z2 = hdot(w2, coarse)

    lift12 = lifted(jnp.concatenate([z1, z2], axis=0))
    load2 = alpha * (jump1 + lift12[:rhs] - centre * load1) - load0
    jump2 = jumps(local(load2))
    load3 = alpha * (jump2 + lift12[rhs:] - centre * load2) - load1
    u3 = local(load3)
    next_sub = along(u3[:, seg[1]], SUB, -1)
    next_grp = along(u3[:, seg[3]], "x", -1)

    def upper(load):
        return jnp.concatenate([load[:, seg[0]], load[:, seg[2]]], axis=1)

    b1, b2, b3 = upper(load1), upper(load2), upper(load3)
    image3 = upper(u3) - jnp.concatenate([next_sub, next_grp], axis=1)
    known4 = alpha * (image3 - centre * b3) - b2

    w3_part = coarse_terms(load3)
    g3_part = image_terms(u3)
    stacked = jnp.concatenate([block, b1, b2, b3, known4], axis=0)
    terms = hdot(stacked, stacked.T)
    order = BLOCKS * rhs
    gram_part = jnp.concatenate(
        [terms[i * rhs : (i + 1) * rhs, i * rhs :] for i in range(BLOCKS)]
        + [jnp.zeros((rhs, ncoarse - rhs * BLOCKS * (BLOCKS + 1) // 2), jnp.float32)],
        axis=1,
    )
    mid_rows = rhs // 2
    to0 = jnp.concatenate([w3_part, gram_part[:mid_rows]], axis=0)
    to1 = jnp.concatenate([g3_part, gram_part[mid_rows:]], axis=0)
    part = jnp.where(first, to0, to1) + swapped(jnp.where(first, to1, to0))
    depth = rhs + mid_rows
    part = jnp.sum(exchange(jnp.broadcast_to(part, (planes, depth, ncoarse)), PLANE), axis=0)
    part = jnp.sum(exchange(jnp.broadcast_to(part, (nz, depth, ncoarse)), "z"), axis=0)
    both = halves(part, swapped(part))
    w3, g3 = both[:rhs], both[depth : depth + rhs]
    gram_sum = jnp.concatenate([both[rhs:depth], both[depth + rhs :]], axis=0)
    z3 = hdot(w3, coarse)
    b4 = known4 + alpha * upper(lifted(z3))

    wk = alpha * (g3 - centre * w3) - w2
    cross = alpha * hdot(jnp.concatenate([block_w for block_w in (w0, w1, w2, w3, wk)], axis=0), z3.T)
    quad = alpha * alpha * hdot(hdot(z3, m_full), z3.T)
    last = cross[4 * rhs :]
    last = last + last.T + quad
    extra = jnp.concatenate([cross[: 4 * rhs], last], axis=0)
    offset, pieces = 0, []
    for i in range(BLOCKS):
        length = (BLOCKS - i) * rhs
        pieces.append(jnp.pad(gram_sum[:, offset : offset + length], ((0, 0), (i * rhs, 0))))
        offset += length
    upper_gram = jnp.concatenate(pieces, axis=0)
    upper_gram = upper_gram + jnp.pad(extra, ((0, 0), (4 * rhs, 0)))
    level = jnp.arange(order) // rhs
    gram = jnp.where(level[:, None] <= level[None, :], upper_gram, upper_gram.T)
    scale = 1.0 / (half * nz * ny * nc)
    basis = jnp.stack([block, b1, b2, b3, b4])
    return basis.reshape(BLOCKS, rhs, 1, 1, half), gram * scale


def solution(mesh):
    split = Mesh(mesh.devices.reshape(8, 4, 2, mesh.shape["grp"]), ("z", "y", "core", "x"))
    in_specs = (
        P(None, SUB, "x", None),
        P(),
        P(SUB, "x", None, None),
        P(SUB, "x", None, None),
        P(SUB, "x", None),
        P(("z", "y", "core", "x"), None),
    )
    out_specs = (P(None, None, SUB, "x", None), P())
    return jax.shard_map(body, mesh=split, in_specs=in_specs, out_specs=out_specs, check_vma=False)
```

```python
import functools

import jax
import jax.numpy as jnp
from jax import lax
from jax.experimental import pallas as pl
from jax.experimental.pallas import tpu as pltpu
from jax.sharding import Mesh
from jax.sharding import PartitionSpec as P

BLOCKS = 5
RHS = 16
FACE = 256
WIDTH = 4 * FACE
NCO = 256
SLOT = 32
SLOTS = 5 * SLOT
SUB = ("z", "y", "core")
PLANE = ("y", "x")
HIGH = lax.Precision.HIGHEST
F32, BF16 = jnp.float32, jnp.bfloat16
SEG = [slice(i * FACE, (i + 1) * FACE) for i in range(4)]


NN = (((1,), (0,)), ((), ()))
NT = (((1,), (1,)), ((), ()))


def hdot(a, b, dims=NN):
    return lax.dot_general(a, b, dims, precision=HIGH, preferred_element_type=F32)


def bdot(a, b, dims=NN):
    return lax.dot_general(a, b, dims, preferred_element_type=F32)


def dot3(a, exact, dims=NN):
    rows = a.shape[0]
    top = a.astype(BF16)
    rest = a - top.astype(F32)
    mid = rest.astype(BF16)
    low = (rest - mid.astype(F32)).astype(BF16)
    got = bdot(jnp.concatenate([top, mid, low], axis=0), exact, dims)
    return got[:rows] + got[rows : 2 * rows] + got[2 * rows :]


def call(kernel, outs, args, spaces=None, scratch=()):
    vmem = pl.BlockSpec(memory_space=pltpu.VMEM)
    specs = [vmem if s is None else pl.BlockSpec(memory_space=s) for s in (spaces or [None] * len(args))]
    return pl.pallas_call(
        kernel,
        out_shape=[jax.ShapeDtypeStruct(s, d) for s, d in outs],
        in_specs=specs,
        out_specs=[vmem] * len(outs),
        scratch_shapes=list(scratch),
        name=kernel.__name__,
    )(*args)


K_SCRATCH = (pltpu.VMEM((WIDTH, WIDTH), BF16), pltpu.SemaphoreType.DMA(()))


def along(x, axis, by):
    count = lax.axis_size(axis)
    return lax.ppermute(x, axis, [(i, (i + by) % count) for i in range(count)])


def exchange(x, axis):
    return lax.all_to_all(x, axis, split_axis=0, concat_axis=0, tiled=True)


def swapped(v):
    return along(v, "core", 1)


def bounds_of(ref):
    low, high = ref[0], ref[1]
    centre = (low + high) * 0.5
    return centre, 1.0 / jnp.full((1, 128), (high - low) * 0.5, F32)[:, :1]


def pack_kernel(block, corners, ids, row, up_sub, up_grp, low_sub, low_grp, labels, own_row):
    count = corners.shape[0]
    given = ids[...]
    label = ((given // 4) % 2) * 128 + (given // 8) * 4 + given % 4
    labels[...] = jnp.full((1, 256), -1, jnp.int32)
    labels[:, :count] = label
    text = labels[...].astype(F32).astype(BF16)
    x = block[...]
    top = x.astype(BF16)
    rest = (x - top.astype(F32)).astype(BF16)
    for out, col, cseg in ((up_sub, SEG[0], SEG[0]), (up_grp, SEG[1], SEG[2])):
        out[:RHS] = top[:, col]
        out[RHS : 2 * RHS] = rest[:, col]
        out[2 * RHS : 2 * RHS + count] = corners[:, cseg]
        out[2 * RHS + count :] = jnp.broadcast_to(text, (8, FACE))
    for out, cseg in ((low_sub, SEG[1]), (low_grp, SEG[3])):
        out[:count] = corners[:, cseg]
        out[count:] = jnp.broadcast_to(text, (8, FACE))
    n = lax.broadcasted_iota(jnp.int32, (NCO, NCO), 0)
    m = lax.broadcasted_iota(jnp.int32, (NCO, NCO), 1)
    order = (((n // 4) % 2) * 128 + (n // 8) * 4 + n % 4 == m).astype(F32).astype(BF16)
    wide_row = jnp.broadcast_to(row[...], (RHS, NCO))
    moved = dot3(wide_row, order)[:8]
    first = lax.broadcasted_iota(jnp.int32, (8, NCO), 0) == 0
    own_row[...] = jnp.where(first, moved, 0.0)


def terms_of(load, u, wide, spread_t):
    both = dot3(dot3(jnp.concatenate([load * 0.5, u], axis=0), wide, NT), spread_t, NT)
    return both[:RHS], both[RHS:]


def lifted(z, wide, spread_t):
    return dot3(dot3(z, spread_t), wide)


def put_faces(u, outs):
    for out, s in zip(outs, SEG, strict=True):
        out[...] = u[:, s]


def split_by_core(first, second, keep, send):
    zero = lax.axis_index("core") == 0

    @pl.when(zero)
    def _():
        keep[...] = first
        send[...] = second

    @pl.when(jnp.logical_not(zero))
    def _():
        keep[...] = second
        send[...] = first


def start_kernel(
    block, from_prev_sub, from_prev_grp, from_next_sub, from_next_grp, corners, labels, inverse,
    load_out, wide_out, spread_out, f0, f1, f2, f3, keep, send, k_mem, k_sem,
):
    fetch = pltpu.make_async_copy(inverse, k_mem, k_sem)
    fetch.start()
    count = corners.shape[0]
    k = 2 * RHS

    def whole(ref):
        return ref[:RHS].astype(F32) + ref[RHS:k].astype(F32)

    load_out[:, SEG[0]] = block[:, :FACE]
    load_out[:, SEG[1]] = -whole(from_prev_sub)
    load_out[:, SEG[2]] = block[:, FACE:]
    load_out[:, SEG[3]] = -whole(from_prev_grp)
    wide_out[...] = jnp.zeros((SLOTS, WIDTH), BF16)
    wide_out[:count] = corners[...]
    wide_out[SLOT : SLOT + count, SEG[0]] = -from_next_sub[:count]
    wide_out[2 * SLOT : 2 * SLOT + count, SEG[1]] = -from_prev_sub[k : k + count]
    wide_out[3 * SLOT : 3 * SLOT + count, SEG[2]] = -from_next_grp[:count]
    wide_out[4 * SLOT : 4 * SLOT + count, SEG[3]] = -from_prev_grp[k : k + count]
    lane = lax.broadcasted_iota(jnp.int32, (8, 256), 1)
    ids = jnp.where(lane < SLOT, jnp.broadcast_to(labels[...], (8, 256)).astype(F32), -1.0)
    others = (
        from_next_sub[count:], from_prev_sub[k + count :], from_next_grp[count:], from_prev_grp[k + count :]
    )
    for i, other in enumerate(others):
        moved = pltpu.roll(other.astype(F32), SLOT * (i + 1), 1)
        mine = jnp.logical_and(lane >= SLOT * (i + 1), lane < SLOT * (i + 2))
        ids = jnp.where(mine, moved, ids)
    number = lax.broadcasted_iota(jnp.int32, (NCO, 256), 0).astype(F32)
    spread_out[...] = (number == ids[:1]).astype(F32).astype(BF16)
    wide = wide_out[...]
    spread_t = spread_out[:, :SLOTS]
    products = bdot(wide, wide, NT) * 0.5
    half = dot3(products, spread_t, NT)
    matrix = hdot(spread_t.astype(F32), half)
    load = load_out[...]
    w, _ = terms_of(load, load, wide, spread_t)
    split_by_core(
        jnp.concatenate([w[:8], matrix[:128]], axis=0), jnp.concatenate([w[8:], matrix[128:]], axis=0), keep, send
    )
    fetch.wait()
    put_faces(bdot(load.astype(BF16), k_mem[...]), (f0, f1, f2, f3))


def plane0_kernel(keep, got, own_row, out):
    total = keep[:8] + got[:8]
    for p in range(16):
        out[p, :8] = total
        out[p, 8:16] = keep[8 + 8 * p : 16 + 8 * p] + got[8 + 8 * p : 16 + 8 * p]
        out[p, 16:] = own_row[...]


def depth0_kernel(got, out):
    total = got[0, :16]
    for p in range(1, 16):
        total = total + got[p, :16]
    rows = jnp.concatenate([got[p, 16:17] for p in range(16)], axis=0)
    for q in range(8):
        out[q, :16] = total
        out[q, 16:] = rows


def after0_kernel(got, m_rows, own):
    total = got[0, :16]
    for q in range(1, 8):
        total = total + got[q, :16]
    own[:8] = total[:8]
    m_rows[...] = total[8:]
    for q in range(8):
        own[8 + 16 * q : 24 + 16 * q] = got[q, 16:]


def jumped(faces, nexts):
    return [
        faces[0][...] - nexts[0][...],
        faces[1][...] - nexts[1][...],
        faces[2][...] - nexts[2][...],
        faces[3][...] - nexts[3][...],
    ]


def ordered(zero, own, got):
    return jnp.where(zero, own, got), jnp.where(zero, got, own)


def block1_kernel(
    bounds, own, got, load0, n0, n1, n2, n3, f0, f1, f2, f3, spread, wide_in, inverse,
    coarse, w0, load1, o0, o1, o2, o3, keep, send, k_mem, k_sem,
):
    fetch = pltpu.make_async_copy(inverse, k_mem, k_sem)
    fetch.start()
    zero = lax.axis_index("core") == 0
    centre, inv = bounds_of(bounds)
    first, second = ordered(zero, own[...], got[...])
    coarse[:128] = first[8:]
    coarse[128:] = second[8:]
    w0[:8] = first[:8]
    w0[8:] = second[:8]
    wide, spread_t = wide_in[...], spread[:, :SLOTS]
    z0 = hdot(w0[...], coarse[...])
    lift = lifted(z0, wide, spread_t)
    for s, jump in zip(SEG, jumped((f0, f1, f2, f3), (n0, n1, n2, n3)), strict=True):
        load1[:, s] = (jump + lift[:, s] - centre * load0[:, s]) * inv
    load = load1[...]
    fetch.wait()
    u = bdot(load.astype(BF16), k_mem[...])
    put_faces(u, (o0, o1, o2, o3))
    w, g = terms_of(load, u, wide, spread_t)
    split_by_core(w, g, keep, send)


def plane1_kernel(keep, got, m_rows, out):
    total = keep[...] + got[...]
    for p in range(16):
        out[p, :16] = total
        out[p, 16:] = m_rows[...]


def depth1_kernel(got, out, m_own):
    total = got[0, :16]
    for p in range(1, 16):
        total = total + got[p, :16]
    for q in range(8):
        out[q] = total
    for p in range(16):
        m_own[8 * p : 8 * p + 8] = got[p, 16:]


def sum_kernel(got, out):
    total = got[0]
    for q in range(1, got.shape[0]):
        total = total + got[q]
    out[...] = total


def block2_kernel(
    bounds, own, got, m_own, m_got, coarse, w0, load0, load1, n0, n1, n2, n3, f0, f1, f2, f3, spread, wide_in, inverse,
    matrix, w1, w2, load2, known3, o0, o1, o2, o3, k_mem, k_sem,
):
    fetch = pltpu.make_async_copy(inverse, k_mem, k_sem)
    fetch.start()
    zero = lax.axis_index("core") == 0
    centre, inv = bounds_of(bounds)
    alpha = 2.0 * inv
    w, g = ordered(zero, own[...], got[...])
    first, second = ordered(zero, m_own[...], m_got[...])
    matrix[:128] = first
    matrix[128:] = second
    w1[...] = w
    z1 = hdot(w, coarse[...])
    after = alpha * (g + hdot(z1, matrix[...]) - centre * w) - w0[...]
    w2[...] = after
    z2 = hdot(after, coarse[...])
    lift = lifted(jnp.concatenate([z1, z2], axis=0), wide_in[...], spread[:, :SLOTS])
    for s, jump in zip(SEG, jumped((f0, f1, f2, f3), (n0, n1, n2, n3)), strict=True):
        load2[:, s] = alpha * (jump + lift[:RHS, s] - centre * load1[:, s]) - load0[:, s]
    known3[...] = alpha * (lift[RHS:] - centre * load2[...]) - load1[...]
    fetch.wait()
    put_faces(bdot(load2[...].astype(BF16), k_mem[...]), (o0, o1, o2, o3))


def block3_kernel(
    bounds, known3, n0, n1, n2, n3, f0, f1, f2, f3, spread, wide_in, inverse, load3, o0, o1, o2, o3, w3, g3, k_mem, k_sem,
):
    fetch = pltpu.make_async_copy(inverse, k_mem, k_sem)
    fetch.start()
    _, inv = bounds_of(bounds)
    alpha = 2.0 * inv
    for s, jump in zip(SEG, jumped((f0, f1, f2, f3), (n0, n1, n2, n3)), strict=True):
        load3[:, s] = known3[:, s] + alpha * jump
    fetch.wait()
    load = load3[...]
    u = bdot(load.astype(BF16), k_mem[...])
    put_faces(u, (o0, o1, o2, o3))
    w, g = terms_of(load, u, wide_in[...], spread[:, :SLOTS])
    w3[...] = w
    g3[...] = g


def gram_kernel(bounds, block, load1, load2, load3, f0, f2, n0, n2, w3, g3, basis, known4, keep, send, stack):
    centre, inv = bounds_of(bounds)
    alpha = 2.0 * inv
    left, right = slice(0, FACE), slice(FACE, 2 * FACE)
    basis[0] = block[...]
    for level, load in ((1, load1), (2, load2), (3, load3)):
        basis[level, :, left] = load[:, SEG[0]]
        basis[level, :, right] = load[:, SEG[2]]
    for half, s, f, n in ((left, SEG[0], f0, n0), (right, SEG[2], f2, n2)):
        known4[:, half] = alpha * (f[...] - n[...] - centre * load3[:, s]) - load2[:, s]
    basis[4] = known4[...]
    for level in range(BLOCKS):
        stack[level * RHS : (level + 1) * RHS] = basis[level]
    stack[BLOCKS * RHS :] = jnp.zeros((128 - BLOCKS * RHS, 2 * FACE), F32)
    terms = hdot(stack[: BLOCKS * RHS], stack[...], NT)
    t = [terms[i * RHS : (i + 1) * RHS] for i in range(BLOCKS)]
    lane = lax.broadcasted_iota(jnp.int32, (RHS, 128), 1)
    first = jnp.where(lane < 80, t[0], pltpu.roll(t[2], 48, 1))
    second = jnp.where(lane < 64, pltpu.roll(t[1], 112, 1), pltpu.roll(t[3], 16, 1))
    second = jnp.where(lane < 96, second, pltpu.roll(t[4], 32, 1))
    packed = jnp.concatenate([first, second], axis=1)
    split_by_core(
        jnp.concatenate([w3[...], packed[:8]], axis=0), jnp.concatenate([g3[...], packed[8:]], axis=0), keep, send
    )


def plane2_kernel(keep, got, out):
    total = keep[...] + got[...]
    for p in range(16):
        out[p] = total


def depth2_kernel(got, out):
    total = got[0]
    for p in range(1, 16):
        total = total + got[p]
    for q in range(8):
        out[q] = total


def final_kernel(bounds, own, got, coarse, matrix, w0, w1, w2, known4, spread, wide_in, block4, gram, square):
    zero = lax.axis_index("core") == 0
    centre, inv = bounds_of(bounds)
    alpha = 2.0 * inv
    first, second = ordered(zero, own[...], got[...])
    w3, g3 = first[:RHS], second[:RHS]
    packed = jnp.concatenate([first[RHS:], second[RHS:]], axis=0)
    z3 = hdot(w3, coarse[...])
    lift = lifted(z3, wide_in[...], spread[:, :SLOTS])
    block4[:, :FACE] = known4[:, :FACE] + alpha * lift[:, SEG[0]]
    block4[:, FACE:] = known4[:, FACE:] + alpha * lift[:, SEG[2]]
    wk = alpha * (g3 - centre * w3) - w2[...]
    z_row = jnp.concatenate([jnp.zeros((64, NCO), F32), z3, jnp.zeros((48, NCO), F32)], axis=0)
    rows = jnp.concatenate([w0[...], w1[...], w2[...], w3, wk, hdot(z3, matrix[...])], axis=0)
    cross = hdot(rows, z_row, NT)
    h0, h1 = packed[:, :128], packed[:, 128:]
    parts = [h0, pltpu.roll(h1, 16, 1), pltpu.roll(h0, 80, 1), pltpu.roll(h1, 112, 1), pltpu.roll(h1, 96, 1)]
    square[...] = jnp.zeros((128, 128), F32)
    for i in range(BLOCKS):
        square[i * RHS : (i + 1) * RHS] = parts[i] + alpha * cross[i * RHS : (i + 1) * RHS]
    last = slice(4 * RHS, 5 * RHS)
    square[last] = square[last] + alpha * alpha * cross[5 * RHS :]
    sided = jnp.concatenate(
        [jnp.zeros((64, 128), F32), alpha * cross[last], jnp.zeros((48, 128), F32)], axis=0
    )
    up = square[...]
    r = lax.broadcasted_iota(jnp.int32, (128, 128), 0) // RHS
    c = lax.broadcasted_iota(jnp.int32, (128, 128), 1) // RHS
    whole = jnp.where(r <= c, up, up.T) + jnp.where(jnp.logical_and(r == 4, c == 4), sided.T, 0.0)
    gram[...] = (whole * (1.0 / (2 * FACE * 64)))[: BLOCKS * RHS, : BLOCKS * RHS]


def body(residual, bounds, local_inverse, corner_basis, corner_map, coarse_inverse):
    block = residual.reshape(RHS, 2 * FACE)
    inverse = local_inverse.reshape(WIDTH, WIDTH)
    corners = corner_basis.reshape(-1, WIDTH)
    count = corners.shape[0]
    face = ((RHS, FACE), F32)
    smem, anyspace = pltpu.SMEM, pl.ANY

    up_sub, up_grp, low_sub, low_grp, labels, own_row = call(
        pack_kernel,
        [((64, FACE), BF16), ((64, FACE), BF16), ((32, FACE), BF16), ((32, FACE), BF16),
         ((1, 256), jnp.int32), ((8, NCO), F32)],
        [block, corners, corner_map.reshape(1, count), coarse_inverse],
    )
    from_prev_sub = along(up_sub, SUB, 1)
    from_prev_grp = along(up_grp, "x", 1)
    from_next_sub = along(low_sub, SUB, -1)
    from_next_grp = along(low_grp, "x", -1)

    def neighbours(faces):
        return [
            along(faces[1], SUB, -1),
            along(faces[0], SUB, 1),
            along(faces[3], "x", -1),
            along(faces[2], "x", 1),
        ]

    load0, wide, spread, *rest = call(
        start_kernel,
        [((RHS, WIDTH), F32), ((SLOTS, WIDTH), BF16), ((NCO, 256), BF16), face, face, face, face,
         ((136, NCO), F32), ((136, NCO), F32)],
        [block, from_prev_sub, from_prev_grp, from_next_sub, from_next_grp, corners, labels, inverse],
        [None] * 7 + [anyspace],
        K_SCRATCH,
    )
    u0, (keep, send) = rest[:4], rest[4:]
    (v,) = call(plane0_kernel, [((16, 24, NCO), F32)], [keep, swapped(send), own_row])
    near0 = neighbours(u0)
    (v,) = call(depth0_kernel, [((8, 32, NCO), F32)], [exchange(v, PLANE)])
    m_rows, own = call(after0_kernel, [((8, NCO), F32), ((136, NCO), F32)], [exchange(v, "z")])

    coarse, w0, load1, *rest = call(
        block1_kernel,
        [((NCO, NCO), F32), ((RHS, NCO), F32), ((RHS, WIDTH), F32), face, face, face, face, face, face],
        [bounds, own, swapped(own), load0, *near0, *u0, spread, wide, inverse],
        [smem] + [None] * 13 + [anyspace],
        K_SCRATCH,
    )
    u1, (keep, send) = rest[:4], rest[4:]
    (v,) = call(plane1_kernel, [((16, 24, NCO), F32)], [keep, swapped(send), m_rows])
    near1 = neighbours(u1)
    v, m_own = call(depth1_kernel, [((8, 16, NCO), F32), ((128, NCO), F32)], [exchange(v, PLANE)])
    m_got = swapped(m_own)
    (own,) = call(sum_kernel, [((RHS, NCO), F32)], [exchange(v, "z")])

    matrix, w1, w2, load2, known3, *u2 = call(
        block2_kernel,
        [((NCO, NCO), F32), ((RHS, NCO), F32), ((RHS, NCO), F32), ((RHS, WIDTH), F32), ((RHS, WIDTH), F32),
         face, face, face, face],
        [bounds, own, swapped(own), m_own, m_got, coarse, w0, load0, load1, *near1, *u1, spread, wide, inverse],
        [smem] + [None] * 18 + [anyspace],
        K_SCRATCH,
    )
    near2 = neighbours(u2)
    load3, f0, f1, f2, f3, w3, g3 = call(
        block3_kernel,
        [((RHS, WIDTH), F32), face, face, face, face, face, face],
        [bounds, known3, *near2, *u2, spread, wide, inverse],
        [smem] + [None] * 11 + [anyspace],
        K_SCRATCH,
    )
    n0, n2 = along(f1, SUB, -1), along(f3, "x", -1)
    basis, known4, keep, send = call(
        gram_kernel,
        [((BLOCKS, RHS, 2 * FACE), F32), ((RHS, 2 * FACE), F32), ((24, NCO), F32), ((24, NCO), F32)],
        [bounds, block, load1, load2, load3, f0, f2, n0, n2, w3, g3],
        [smem] + [None] * 10,
        [pltpu.VMEM((128, 2 * FACE), F32)],
    )
    (v,) = call(plane2_kernel, [((16, 24, NCO), F32)], [keep, swapped(send)])
    (v,) = call(depth2_kernel, [((8, 24, NCO), F32)], [exchange(v, PLANE)])
    (own,) = call(sum_kernel, [((24, NCO), F32)], [exchange(v, "z")])
    block4, gram = call(
        final_kernel,
        [((RHS, 2 * FACE), F32), ((BLOCKS * RHS, BLOCKS * RHS), F32)],
        [bounds, own, swapped(own), coarse, matrix, w0, w1, w2, known4, spread, wide],
        [smem] + [None] * 10,
        [pltpu.VMEM((128, 128), F32)],
    )
    basis = basis.at[4].set(block4)
    return basis.reshape(BLOCKS, RHS, 1, 1, 2 * FACE), gram


def solution(mesh):
    split = Mesh(mesh.devices.reshape(8, 4, 2, mesh.shape["grp"]), ("z", "y", "core", "x"))
    in_specs = (
        P(None, SUB, "x", None),
        P(),
        P(SUB, "x", None, None),
        P(SUB, "x", None, None),
        P(SUB, "x", None),
        P(("z", "y", "core", "x"), None),
    )
    out_specs = (P(None, None, SUB, "x", None), P())
    return jax.shard_map(body, mesh=split, in_specs=in_specs, out_specs=out_specs, check_vma=False)
```

```python
import functools

import jax
import jax.numpy as jnp
from jax import lax
from jax.experimental import pallas as pl
from jax.experimental.pallas import tpu as pltpu
from jax.sharding import Mesh
from jax.sharding import PartitionSpec as P

BLOCKS = 5
RHS = 16
FACE = 256
WIDTH = 4 * FACE
NCO = 256
SLOT = 32
SLOTS = 5 * SLOT
SUB = ("z", "y", "core")
PLANE = ("y", "x")
HIGH = lax.Precision.HIGHEST
F32, BF16 = jnp.float32, jnp.bfloat16
SEG = [slice(i * FACE, (i + 1) * FACE) for i in range(4)]


NN = (((1,), (0,)), ((), ()))
NT = (((1,), (1,)), ((), ()))


def hdot(a, b, dims=NN):
    return lax.dot_general(a, b, dims, precision=HIGH, preferred_element_type=F32)


def bdot(a, b, dims=NN):
    return lax.dot_general(a, b, dims, preferred_element_type=F32)


def dot3(a, exact, dims=NN):
    rows = a.shape[0]
    top = a.astype(BF16)
    rest = a - top.astype(F32)
    mid = rest.astype(BF16)
    low = (rest - mid.astype(F32)).astype(BF16)
    got = bdot(jnp.concatenate([top, mid, low], axis=0), exact, dims)
    return got[:rows] + got[rows : 2 * rows] + got[2 * rows :]


def call(kernel, outs, args, spaces=None, scratch=(), limit=12):
    vmem = pl.BlockSpec(memory_space=pltpu.VMEM)
    specs = [vmem if s is None else pl.BlockSpec(memory_space=s) for s in (spaces or [None] * len(args))]
    return pl.pallas_call(
        kernel,
        out_shape=[jax.ShapeDtypeStruct(s, d) for s, d in outs],
        in_specs=specs,
        out_specs=[vmem] * len(outs),
        scratch_shapes=list(scratch),
        compiler_params=pltpu.CompilerParams(vmem_limit_bytes=limit << 20),
        name=kernel.__name__,
    )(*args)


def along(x, axis, by):
    count = lax.axis_size(axis)
    return lax.ppermute(x, axis, [(i, (i + by) % count) for i in range(count)])


def exchange(x, axis):
    return lax.all_to_all(x, axis, split_axis=0, concat_axis=0, tiled=True)


def swapped(v):
    return along(v, "core", 1)


def bounds_of(ref):
    low, high = ref[0], ref[1]
    centre = (low + high) * 0.5
    return centre, 1.0 / jnp.full((1, 128), (high - low) * 0.5, F32)[:, :1]


def pack_kernel(block, corners, ids, row, up_sub, up_grp, low_sub, low_grp, labels, own_row):
    count = corners.shape[0]
    given = ids[...]
    label = ((given // 4) % 2) * 128 + (given // 8) * 4 + given % 4
    labels[...] = jnp.full((1, 256), -1, jnp.int32)
    labels[:, :count] = label
    text = labels[...].astype(F32).astype(BF16)
    x = block[...]
    top = x.astype(BF16)
    rest = (x - top.astype(F32)).astype(BF16)
    for out, col, cseg in ((up_sub, SEG[0], SEG[0]), (up_grp, SEG[1], SEG[2])):
        out[:RHS] = top[:, col]
        out[RHS : 2 * RHS] = rest[:, col]
        out[2 * RHS : 2 * RHS + count] = corners[:, cseg]
        out[2 * RHS + count :] = jnp.broadcast_to(text, (8, FACE))
    for out, cseg in ((low_sub, SEG[1]), (low_grp, SEG[3])):
        out[:count] = corners[:, cseg]
        out[count:] = jnp.broadcast_to(text, (8, FACE))
    n = lax.broadcasted_iota(jnp.int32, (NCO, NCO), 0)
    m = lax.broadcasted_iota(jnp.int32, (NCO, NCO), 1)
    order = (((n // 4) % 2) * 128 + (n // 8) * 4 + n % 4 == m).astype(F32).astype(BF16)
    wide_row = jnp.broadcast_to(row[...], (RHS, NCO))
    moved = dot3(wide_row, order)[:8]
    first = lax.broadcasted_iota(jnp.int32, (8, NCO), 0) == 0
    own_row[...] = jnp.where(first, moved, 0.0)


def terms_of(load, u, wide, spread_t):
    both = dot3(dot3(jnp.concatenate([load * 0.5, u], axis=0), wide, NT), spread_t, NT)
    return both[:RHS], both[RHS:]


def lifted(z, wide, spread_t):
    return dot3(dot3(z, spread_t), wide)


def put_faces(u, outs):
    for out, s in zip(outs, SEG, strict=True):
        out[...] = u[:, s]


def split_by_core(first, second, keep, send):
    zero = lax.axis_index("core") == 0

    @pl.when(zero)
    def _():
        keep[...] = first
        send[...] = second

    @pl.when(jnp.logical_not(zero))
    def _():
        keep[...] = second
        send[...] = first


def start_kernel(
    block, from_prev_sub, from_prev_grp, from_next_sub, from_next_grp, corners, labels, inverse,
    load_out, wide_out, spread_out, f0, f1, f2, f3, keep, send,
):
    count = corners.shape[0]
    k = 2 * RHS

    def whole(ref):
        return ref[:RHS].astype(F32) + ref[RHS:k].astype(F32)

    load_out[:, SEG[0]] = block[:, :FACE]
    load_out[:, SEG[1]] = -whole(from_prev_sub)
    load_out[:, SEG[2]] = block[:, FACE:]
    load_out[:, SEG[3]] = -whole(from_prev_grp)
    wide_out[...] = jnp.zeros((SLOTS, WIDTH), BF16)
    wide_out[:count] = corners[...]
    wide_out[SLOT : SLOT + count, SEG[0]] = -from_next_sub[:count]
    wide_out[2 * SLOT : 2 * SLOT + count, SEG[1]] = -from_prev_sub[k : k + count]
    wide_out[3 * SLOT : 3 * SLOT + count, SEG[2]] = -from_next_grp[:count]
    wide_out[4 * SLOT : 4 * SLOT + count, SEG[3]] = -from_prev_grp[k : k + count]
    lane = lax.broadcasted_iota(jnp.int32, (8, 256), 1)
    ids = jnp.where(lane < SLOT, jnp.broadcast_to(labels[...], (8, 256)).astype(F32), -1.0)
    others = (
        from_next_sub[count:], from_prev_sub[k + count :], from_next_grp[count:], from_prev_grp[k + count :]
    )
    for i, other in enumerate(others):
        moved = pltpu.roll(other.astype(F32), SLOT * (i + 1), 1)
        mine = jnp.logical_and(lane >= SLOT * (i + 1), lane < SLOT * (i + 2))
        ids = jnp.where(mine, moved, ids)
    number = lax.broadcasted_iota(jnp.int32, (NCO, 256), 0).astype(F32)
    spread_out[...] = (number == ids[:1]).astype(F32).astype(BF16)
    wide = wide_out[...]
    spread_t = spread_out[:, :SLOTS]
    products = bdot(wide, wide, NT) * 0.5
    half = dot3(products, spread_t, NT)
    matrix = hdot(spread_t.astype(F32), half)
    load = load_out[...]
    w, _ = terms_of(load, load, wide, spread_t)
    split_by_core(
        jnp.concatenate([w[:8], matrix[:128]], axis=0), jnp.concatenate([w[8:], matrix[128:]], axis=0), keep, send
    )
    put_faces(bdot(load.astype(BF16), inverse[...]), (f0, f1, f2, f3))


def plane0_kernel(keep, got, own_row, out):
    total = keep[:8] + got[:8]
    for p in range(16):
        out[p, :8] = total
        out[p, 8:16] = keep[8 + 8 * p : 16 + 8 * p] + got[8 + 8 * p : 16 + 8 * p]
        out[p, 16:] = own_row[...]


def depth0_kernel(got, out):
    total = got[0, :16]
    for p in range(1, 16):
        total = total + got[p, :16]
    rows = jnp.concatenate([got[p, 16:17] for p in range(16)], axis=0)
    for q in range(8):
        out[q, :16] = total
        out[q, 16:] = rows


def after0_kernel(got, m_rows, own):
    total = got[0, :16]
    for q in range(1, 8):
        total = total + got[q, :16]
    own[:8] = total[:8]
    m_rows[...] = total[8:]
    for q in range(8):
        own[8 + 16 * q : 24 + 16 * q] = got[q, 16:]


def jumped(faces, nexts):
    return [
        faces[0][...] - nexts[0][...],
        faces[1][...] - nexts[1][...],
        faces[2][...] - nexts[2][...],
        faces[3][...] - nexts[3][...],
    ]


def ordered(zero, own, got):
    return jnp.where(zero, own, got), jnp.where(zero, got, own)


def block1_kernel(
    bounds, own, got, load0, n0, n1, n2, n3, f0, f1, f2, f3, spread, wide_in, inverse,
    coarse, w0, load1, o0, o1, o2, o3, keep, send,
):
    zero = lax.axis_index("core") == 0
    centre, inv = bounds_of(bounds)
    first, second = ordered(zero, own[...], got[...])
    coarse[:128] = first[8:]
    coarse[128:] = second[8:]
    w0[:8] = first[:8]
    w0[8:] = second[:8]
    wide, spread_t = wide_in[...], spread[:, :SLOTS]
    z0 = hdot(w0[...], coarse[...])
    lift = lifted(z0, wide, spread_t)
    for s, jump in zip(SEG, jumped((f0, f1, f2, f3), (n0, n1, n2, n3)), strict=True):
        load1[:, s] = (jump + lift[:, s] - centre * load0[:, s]) * inv
    load = load1[...]
    u = bdot(load.astype(BF16), inverse[...])
    put_faces(u, (o0, o1, o2, o3))
    w, g = terms_of(load, u, wide, spread_t)
    split_by_core(w, g, keep, send)


def plane1_kernel(keep, got, m_rows, out):
    total = keep[...] + got[...]
    for p in range(16):
        out[p, :16] = total
        out[p, 16:] = m_rows[...]


def depth1_kernel(got, out, m_own):
    total = got[0, :16]
    for p in range(1, 16):
        total = total + got[p, :16]
    for q in range(8):
        out[q] = total
    for p in range(16):
        m_own[8 * p : 8 * p + 8] = got[p, 16:]


def sum_kernel(got, out):
    total = got[0]
    for q in range(1, got.shape[0]):
        total = total + got[q]
    out[...] = total


def block2_kernel(
    bounds, own, got, m_own, m_got, coarse, w0, load0, load1, n0, n1, n2, n3, f0, f1, f2, f3, spread, wide_in, inverse,
    matrix, w1, w2, load2, known3, o0, o1, o2, o3,
):
    zero = lax.axis_index("core") == 0
    centre, inv = bounds_of(bounds)
    alpha = 2.0 * inv
    w, g = ordered(zero, own[...], got[...])
    first, second = ordered(zero, m_own[...], m_got[...])
    matrix[:128] = first
    matrix[128:] = second
    w1[...] = w
    z1 = hdot(w, coarse[...])
    after = alpha * (g + hdot(z1, matrix[...]) - centre * w) - w0[...]
    w2[...] = after
    z2 = hdot(after, coarse[...])
    lift = lifted(jnp.concatenate([z1, z2], axis=0), wide_in[...], spread[:, :SLOTS])
    for s, jump in zip(SEG, jumped((f0, f1, f2, f3), (n0, n1, n2, n3)), strict=True):
        load2[:, s] = alpha * (jump + lift[:RHS, s] - centre * load1[:, s]) - load0[:, s]
    known3[...] = alpha * (lift[RHS:] - centre * load2[...]) - load1[...]
    put_faces(bdot(load2[...].astype(BF16), inverse[...]), (o0, o1, o2, o3))


def block3_kernel(
    bounds, known3, n0, n1, n2, n3, f0, f1, f2, f3, spread, wide_in, inverse, load3, o0, o1, o2, o3, w3, g3,
):
    _, inv = bounds_of(bounds)
    alpha = 2.0 * inv
    for s, jump in zip(SEG, jumped((f0, f1, f2, f3), (n0, n1, n2, n3)), strict=True):
        load3[:, s] = known3[:, s] + alpha * jump
    load = load3[...]
    u = bdot(load.astype(BF16), inverse[...])
    put_faces(u, (o0, o1, o2, o3))
    w, g = terms_of(load, u, wide_in[...], spread[:, :SLOTS])
    w3[...] = w
    g3[...] = g


def gram_kernel(bounds, block, load1, load2, load3, f0, f2, n0, n2, w3, g3, basis, known4, keep, send, stack):
    centre, inv = bounds_of(bounds)
    alpha = 2.0 * inv
    left, right = slice(0, FACE), slice(FACE, 2 * FACE)
    basis[0] = block[...]
    for level, load in ((1, load1), (2, load2), (3, load3)):
        basis[level, :, left] = load[:, SEG[0]]
        basis[level, :, right] = load[:, SEG[2]]
    for half, s, f, n in ((left, SEG[0], f0, n0), (right, SEG[2], f2, n2)):
        known4[:, half] = alpha * (f[...] - n[...] - centre * load3[:, s]) - load2[:, s]
    basis[4] = known4[...]
    for level in range(BLOCKS):
        stack[level * RHS : (level + 1) * RHS] = basis[level]
    stack[BLOCKS * RHS :] = jnp.zeros((128 - BLOCKS * RHS, 2 * FACE), F32)
    terms = hdot(stack[: BLOCKS * RHS], stack[...], NT)
    t = [terms[i * RHS : (i + 1) * RHS] for i in range(BLOCKS)]
    lane = lax.broadcasted_iota(jnp.int32, (RHS, 128), 1)
    first = jnp.where(lane < 80, t[0], pltpu.roll(t[2], 48, 1))
    second = jnp.where(lane < 64, pltpu.roll(t[1], 112, 1), pltpu.roll(t[3], 16, 1))
    second = jnp.where(lane < 96, second, pltpu.roll(t[4], 32, 1))
    packed = jnp.concatenate([first, second], axis=1)
    split_by_core(
        jnp.concatenate([w3[...], packed[:8]], axis=0), jnp.concatenate([g3[...], packed[8:]], axis=0), keep, send
    )


def plane2_kernel(keep, got, out):
    total = keep[...] + got[...]
    for p in range(16):
        out[p] = total


def depth2_kernel(got, out):
    total = got[0]
    for p in range(1, 16):
        total = total + got[p]
    for q in range(8):
        out[q] = total


def final_kernel(bounds, own, got, coarse, matrix, w0, w1, w2, known4, spread, wide_in, block4, gram, square):
    zero = lax.axis_index("core") == 0
    centre, inv = bounds_of(bounds)
    alpha = 2.0 * inv
    first, second = ordered(zero, own[...], got[...])
    w3, g3 = first[:RHS], second[:RHS]
    packed = jnp.concatenate([first[RHS:], second[RHS:]], axis=0)
    z3 = hdot(w3, coarse[...])
    lift = lifted(z3, wide_in[...], spread[:, :SLOTS])
    block4[:, :FACE] = known4[:, :FACE] + alpha * lift[:, SEG[0]]
    block4[:, FACE:] = known4[:, FACE:] + alpha * lift[:, SEG[2]]
    wk = alpha * (g3 - centre * w3) - w2[...]
    z_row = jnp.concatenate([jnp.zeros((64, NCO), F32), z3, jnp.zeros((48, NCO), F32)], axis=0)
    rows = jnp.concatenate([w0[...], w1[...], w2[...], w3, wk, hdot(z3, matrix[...])], axis=0)
    cross = hdot(rows, z_row, NT)
    h0, h1 = packed[:, :128], packed[:, 128:]
    parts = [h0, pltpu.roll(h1, 16, 1), pltpu.roll(h0, 80, 1), pltpu.roll(h1, 112, 1), pltpu.roll(h1, 96, 1)]
    square[...] = jnp.zeros((128, 128), F32)
    for i in range(BLOCKS):
        square[i * RHS : (i + 1) * RHS] = parts[i] + alpha * cross[i * RHS : (i + 1) * RHS]
    last = slice(4 * RHS, 5 * RHS)
    square[last] = square[last] + alpha * alpha * cross[5 * RHS :]
    sided = jnp.concatenate(
        [jnp.zeros((64, 128), F32), alpha * cross[last], jnp.zeros((48, 128), F32)], axis=0
    )
    up = square[...]
    r = lax.broadcasted_iota(jnp.int32, (128, 128), 0) // RHS
    c = lax.broadcasted_iota(jnp.int32, (128, 128), 1) // RHS
    whole = jnp.where(r <= c, up, up.T) + jnp.where(jnp.logical_and(r == 4, c == 4), sided.T, 0.0)
    gram[...] = (whole * (1.0 / (2 * FACE * 64)))[: BLOCKS * RHS, : BLOCKS * RHS]


def body(residual, bounds, local_inverse, corner_basis, corner_map, coarse_inverse):
    block = residual.reshape(RHS, 2 * FACE)
    inverse = local_inverse.reshape(WIDTH, WIDTH)
    corners = corner_basis.reshape(-1, WIDTH)
    count = corners.shape[0]
    face = ((RHS, FACE), F32)
    smem = pltpu.SMEM

    up_sub, up_grp, low_sub, low_grp, labels, own_row = call(
        pack_kernel,
        [((64, FACE), BF16), ((64, FACE), BF16), ((32, FACE), BF16), ((32, FACE), BF16),
         ((1, 256), jnp.int32), ((8, NCO), F32)],
        [block, corners, corner_map.reshape(1, count), coarse_inverse],
    )
    from_prev_sub = along(up_sub, SUB, 1)
    from_prev_grp = along(up_grp, "x", 1)
    from_next_sub = along(low_sub, SUB, -1)
    from_next_grp = along(low_grp, "x", -1)

    def neighbours(faces):
        return [
            along(faces[1], SUB, -1),
            along(faces[0], SUB, 1),
            along(faces[3], "x", -1),
            along(faces[2], "x", 1),
        ]

    load0, wide, spread, *rest = call(
        start_kernel,
        [((RHS, WIDTH), F32), ((SLOTS, WIDTH), BF16), ((NCO, 256), BF16), face, face, face, face,
         ((136, NCO), F32), ((136, NCO), F32)],
        [block, from_prev_sub, from_prev_grp, from_next_sub, from_next_grp, corners, labels, inverse],
    )
    u0, (keep, send) = rest[:4], rest[4:]
    (v,) = call(plane0_kernel, [((16, 24, NCO), F32)], [keep, swapped(send), own_row])
    near0 = neighbours(u0)
    (v,) = call(depth0_kernel, [((8, 32, NCO), F32)], [exchange(v, PLANE)])
    m_rows, own = call(after0_kernel, [((8, NCO), F32), ((136, NCO), F32)], [exchange(v, "z")])

    coarse, w0, load1, *rest = call(
        block1_kernel,
        [((NCO, NCO), F32), ((RHS, NCO), F32), ((RHS, WIDTH), F32), face, face, face, face, face, face],
        [bounds, own, swapped(own), load0, *near0, *u0, spread, wide, inverse],
        [smem] + [None] * 14,
    )
    u1, (keep, send) = rest[:4], rest[4:]
    (v,) = call(plane1_kernel, [((16, 24, NCO), F32)], [keep, swapped(send), m_rows])
    near1 = neighbours(u1)
    v, m_own = call(depth1_kernel, [((8, 16, NCO), F32), ((128, NCO), F32)], [exchange(v, PLANE)])
    m_got = swapped(m_own)
    (own,) = call(sum_kernel, [((RHS, NCO), F32)], [exchange(v, "z")])

    matrix, w1, w2, load2, known3, *u2 = call(
        block2_kernel,
        [((NCO, NCO), F32), ((RHS, NCO), F32), ((RHS, NCO), F32), ((RHS, WIDTH), F32), ((RHS, WIDTH), F32),
         face, face, face, face],
        [bounds, own, swapped(own), m_own, m_got, coarse, w0, load0, load1, *near1, *u1, spread, wide, inverse],
        [smem] + [None] * 19,
    )
    near2 = neighbours(u2)
    load3, f0, f1, f2, f3, w3, g3 = call(
        block3_kernel,
        [((RHS, WIDTH), F32), face, face, face, face, face, face],
        [bounds, known3, *near2, *u2, spread, wide, inverse],
        [smem] + [None] * 12,
    )
    n0, n2 = along(f1, SUB, -1), along(f3, "x", -1)
    basis, known4, keep, send = call(
        gram_kernel,
        [((BLOCKS, RHS, 2 * FACE), F32), ((RHS, 2 * FACE), F32), ((24, NCO), F32), ((24, NCO), F32)],
        [bounds, block, load1, load2, load3, f0, f2, n0, n2, w3, g3],
        [smem] + [None] * 10,
        [pltpu.VMEM((128, 2 * FACE), F32)],
    )
    (v,) = call(plane2_kernel, [((16, 24, NCO), F32)], [keep, swapped(send)])
    (v,) = call(depth2_kernel, [((8, 24, NCO), F32)], [exchange(v, PLANE)])
    (own,) = call(sum_kernel, [((24, NCO), F32)], [exchange(v, "z")])
    block4, gram = call(
        final_kernel,
        [((RHS, 2 * FACE), F32), ((BLOCKS * RHS, BLOCKS * RHS), F32)],
        [bounds, own, swapped(own), coarse, matrix, w0, w1, w2, known4, spread, wide],
        [smem] + [None] * 10,
        [pltpu.VMEM((128, 128), F32)],
    )
    basis = basis.at[4].set(block4)
    return basis.reshape(BLOCKS, RHS, 1, 1, 2 * FACE), gram


def solution(mesh):
    split = Mesh(mesh.devices.reshape(8, 4, 2, mesh.shape["grp"]), ("z", "y", "core", "x"))
    in_specs = (
        P(None, SUB, "x", None),
        P(),
        P(SUB, "x", None, None),
        P(SUB, "x", None, None),
        P(SUB, "x", None),
        P(("z", "y", "core", "x"), None),
    )
    out_specs = (P(None, None, SUB, "x", None), P())
    return jax.shard_map(body, mesh=split, in_specs=in_specs, out_specs=out_specs, check_vma=False)
```

```python
import functools

import jax
import jax.numpy as jnp
from jax import lax
from jax.experimental import pallas as pl
from jax.experimental.pallas import tpu as pltpu
from jax.sharding import Mesh
from jax.sharding import PartitionSpec as P

BLOCKS = 5
RHS = 16
FACE = 256
WIDTH = 4 * FACE
NCO = 256
SLOT = 32
SLOTS = 5 * SLOT
SUB = ("z", "y", "core")
PLANE = ("y", "x")
HIGH = lax.Precision.HIGHEST
F32, BF16 = jnp.float32, jnp.bfloat16
SEG = [slice(i * FACE, (i + 1) * FACE) for i in range(4)]


NN = (((1,), (0,)), ((), ()))
NT = (((1,), (1,)), ((), ()))


def hdot(a, b, dims=NN):
    return lax.dot_general(a, b, dims, precision=HIGH, preferred_element_type=F32)


def bdot(a, b, dims=NN):
    return lax.dot_general(a, b, dims, preferred_element_type=F32)


def dot3(a, exact, dims=NN):
    rows = a.shape[0]
    top = a.astype(BF16)
    rest = a - top.astype(F32)
    mid = rest.astype(BF16)
    low = (rest - mid.astype(F32)).astype(BF16)
    got = bdot(jnp.concatenate([top, mid, low], axis=0), exact, dims)
    return got[:rows] + got[rows : 2 * rows] + got[2 * rows :]


def call(kernel, outs, args, spaces=None, scratch=(), limit=12):
    vmem = pl.BlockSpec(memory_space=pltpu.VMEM)
    specs = [vmem if s is None else pl.BlockSpec(memory_space=s) for s in (spaces or [None] * len(args))]
    return pl.pallas_call(
        kernel,
        out_shape=[jax.ShapeDtypeStruct(s, d) for s, d in outs],
        in_specs=specs,
        out_specs=[vmem] * len(outs),
        scratch_shapes=list(scratch),
        compiler_params=pltpu.CompilerParams(vmem_limit_bytes=limit << 20),
        name=kernel.__name__,
    )(*args)


def along(x, axis, by):
    count = lax.axis_size(axis)
    return lax.ppermute(x, axis, [(i, (i + by) % count) for i in range(count)])


def exchange(x, axis):
    return lax.all_to_all(x, axis, split_axis=0, concat_axis=0, tiled=True)


def swapped(v):
    return along(v, "core", 1)


def bounds_of(ref):
    low, high = ref[0], ref[1]
    centre = (low + high) * 0.5
    return centre, 1.0 / jnp.full((1, 128), (high - low) * 0.5, F32)[:, :1]


def label_of(n):
    return ((n // 4) % 2) * 128 + ((n // 8) % 4 * 4 + n % 4) * 8 + n // 32


def pack_kernel(
    block_hbm, corners_hbm, ids_hbm, row_hbm,
    up_sub, up_grp, low_sub, low_grp, labels, own_row, block, corners, wide_block, given, row, sems,
):
    copies = [
        pltpu.make_async_copy(src, dst, sems.at[i])
        for i, (src, dst) in enumerate(
            ((block_hbm, wide_block), (corners_hbm, corners), (ids_hbm, given), (row_hbm, row))
        )
    ]
    for copy in copies:
        copy.start()
    n = lax.broadcasted_iota(jnp.int32, (NCO, NCO), 0)
    m = lax.broadcasted_iota(jnp.int32, (NCO, NCO), 1)
    order = (label_of(n) == m).astype(F32).astype(BF16)
    first = lax.broadcasted_iota(jnp.int32, (8, NCO), 0) == 0
    for copy in copies:
        copy.wait()
    count = corners.shape[0]
    labels[...] = jnp.full((1, 256), -1, jnp.int32)
    labels[:, :count] = label_of(given[...])
    text = labels[...].astype(F32).astype(BF16)
    x = wide_block[...].reshape(RHS, 2 * FACE)
    block[...] = x
    top = x.astype(BF16)
    rest = (x - top.astype(F32)).astype(BF16)
    for out, col, cseg in ((up_sub, SEG[0], SEG[0]), (up_grp, SEG[1], SEG[2])):
        out[:RHS] = top[:, col]
        out[RHS : 2 * RHS] = rest[:, col]
        out[2 * RHS : 2 * RHS + count] = corners[:, cseg]
        out[2 * RHS + count :] = jnp.broadcast_to(text, (8, FACE))
    for out, cseg in ((low_sub, SEG[1]), (low_grp, SEG[3])):
        out[:count] = corners[:, cseg]
        out[count:] = jnp.broadcast_to(text, (8, FACE))
    moved = dot3(jnp.broadcast_to(row[...], (RHS, NCO)), order)[:8]
    own_row[...] = jnp.where(first, moved, 0.0)


def terms_of(load, u, wide, spread_t):
    both = dot3(dot3(jnp.concatenate([load * 0.5, u], axis=0), wide, NT), spread_t, NT)
    return both[:RHS], both[RHS:]


def lifted(z, wide, spread_t):
    return dot3(dot3(z, spread_t), wide)


def put_faces(u, outs):
    for out, s in zip(outs, SEG, strict=True):
        out[...] = u[:, s]


def on_core(zero_branch, other_branch):
    zero = lax.axis_index("core") == 0
    pl.when(zero)(zero_branch)
    pl.when(jnp.logical_not(zero))(other_branch)


def split_by_core(first, second, keep, send):
    def zero():
        keep[...] = first
        send[...] = second

    def one():
        keep[...] = second
        send[...] = first

    on_core(zero, one)


def high_low(x):
    top = x.astype(BF16).astype(F32)
    return top, x - top


def start_kernel(
    block, from_prev_sub, from_prev_grp, from_next_sub, from_next_grp, corners, labels, inverse,
    load_out, wide_out, spread_out, f0, f1, f2, f3,
):
    count = corners.shape[0]
    k = 2 * RHS

    def whole(ref):
        return ref[:RHS].astype(F32) + ref[RHS:k].astype(F32)

    load_out[:, SEG[0]] = block[:, :FACE]
    load_out[:, SEG[1]] = -whole(from_prev_sub)
    load_out[:, SEG[2]] = block[:, FACE:]
    load_out[:, SEG[3]] = -whole(from_prev_grp)
    put_faces(bdot(load_out[...].astype(BF16), inverse[...]), (f0, f1, f2, f3))
    wide_out[...] = jnp.zeros((SLOTS, WIDTH), BF16)
    wide_out[:count] = corners[...]
    wide_out[SLOT : SLOT + count, SEG[0]] = -from_next_sub[:count]
    wide_out[2 * SLOT : 2 * SLOT + count, SEG[1]] = -from_prev_sub[k : k + count]
    wide_out[3 * SLOT : 3 * SLOT + count, SEG[2]] = -from_next_grp[:count]
    wide_out[4 * SLOT : 4 * SLOT + count, SEG[3]] = -from_prev_grp[k : k + count]
    lane = lax.broadcasted_iota(jnp.int32, (8, 256), 1)
    ids = jnp.where(lane < SLOT, jnp.broadcast_to(labels[...], (8, 256)).astype(F32), -1.0)
    others = (
        from_next_sub[count:], from_prev_sub[k + count :], from_next_grp[count:], from_prev_grp[k + count :]
    )
    for i, other in enumerate(others):
        moved = pltpu.roll(other.astype(F32), SLOT * (i + 1), 1)
        mine = jnp.logical_and(lane >= SLOT * (i + 1), lane < SLOT * (i + 2))
        ids = jnp.where(mine, moved, ids)
    number = lax.broadcasted_iota(jnp.int32, (NCO, 256), 0).astype(F32)
    spread_out[...] = (number == ids[:1]).astype(F32).astype(BF16)


def moment_kernel(load0, f0, f1, f2, f3, wide_in, spread, inverse, m0, m1, w0, g1):
    wide, spread_t = wide_in[...], spread[:, :SLOTS]
    spread_wide = spread_t.astype(F32)
    m0[...] = hdot(spread_wide, dot3(bdot(wide, wide, NT) * 0.5, spread_t, NT))
    pairs = dot3(bdot(wide, inverse[...]), wide, NT)
    m1[...] = hdot(spread_wide, dot3(pairs, spread_t, NT))
    u = jnp.concatenate([f[...] for f in (f0, f1, f2, f3)], axis=1)
    w, g = terms_of(load0[...], u, wide, spread_t)
    w0[...] = w
    g1[...] = g


def jumped(faces, nexts):
    return [f[...] - n[...] for f, n in zip(faces, nexts, strict=True)]


def join_kernel(n0, n1, n2, n3, f0, f1, f2, f3, wide_in, spread, inverse, m0, m1, w0, g1, keep, send):
    jump = jnp.concatenate(jumped((f0, f1, f2, f3), (n0, n1, n2, n3)), axis=1)
    top, rest = high_low(jump)
    u = bdot(jnp.concatenate([top.astype(BF16), rest.astype(BF16)], axis=0), inverse[...])
    u = u[:RHS] + u[RHS:]
    g2 = dot3(dot3(u, wide_in[...], NT), spread[:, :SLOTS], NT)

    def put(first, second):
        first[:NCO] = m0[...]
        first[NCO : NCO + RHS] = w0[...]
        first[NCO + RHS :] = g1[:8]
        second[:NCO] = m1[...]
        second[NCO : NCO + 8] = g1[8:]
        second[NCO + 8 :] = g2

    on_core(lambda: put(keep, send), lambda: put(send, keep))


def plane0_kernel(keep, got, out):
    for p in range(16):
        rows = slice(16 * p, 16 * p + 16)
        pieces = [keep[rows] + got[rows]]
        if p < 12:
            rows = slice(NCO + 2 * p, NCO + 2 * p + 2)
            pieces += [*high_low(keep[rows] + got[rows]), jnp.zeros((4, NCO), F32)]
        else:
            pieces += [jnp.zeros((8, NCO), F32)]
        out[p] = jnp.concatenate(pieces, axis=0).astype(BF16)


def summed(got):
    total = got[0].astype(F32)
    for p in range(1, got.shape[0]):
        total = total + got[p].astype(F32)
    return total


def depth0_kernel(got, own_row, out):
    total = summed(got)
    g = total[16:18] + total[18:20]
    rows = [total[:16], *high_low(g), *high_low(own_row[:1]), jnp.zeros((2, NCO), F32)]
    value = jnp.concatenate(rows, axis=0).astype(BF16)
    for q in range(8):
        out[q] = value


def spread0_kernel(got, out):
    every = [got[q].astype(F32) for q in range(8)]
    total = functools.reduce(jnp.add, every)
    g = total[16:18] + total[18:20]
    rows = [total[:16], *high_low(g), jnp.zeros((4, NCO), F32)]
    rows += [r[20:21] for r in every] + [r[21:22] for r in every]
    value = jnp.concatenate(rows, axis=0).astype(BF16)
    for p in range(16):
        out[p] = value


def collect0_kernel(got, out):
    g = []
    for p in range(16):
        out[16 * p : 16 * p + 16] = got[p, :16]
        g.append(got[p, 16:24].astype(F32))
        out[320 + 8 * p : 328 + 8 * p] = got[p, 24:32]
        out[448 + 8 * p : 456 + 8 * p] = got[p, 32:40]
    out[256:320] = jnp.concatenate([r[:2] for r in g] + [r[2:4] for r in g], axis=0).astype(BF16)


def bounds_terms(ref):
    centre, inv = bounds_of(ref)
    return centre, inv, 2.0 * inv


def block1_kernel(
    bounds, own, got, load0, n0, n1, n2, n3, f0, f1, f2, f3, spread, wide_in, inverse,
    coarse, m0, m1, w0, g1, g2, z0, load1, o0, o1, o2, o3,
):
    centre, inv, _ = bounds_terms(bounds)

    def put(first, second):
        for half, part in ((slice(0, 128), first), (slice(128, 256), second)):
            coarse[half] = part[320:448].astype(F32) + part[448:576].astype(F32)
        m0[...] = first[:NCO]
        m1[...] = second[:NCO]
        left = first[256:288].astype(F32) + first[288:320].astype(F32)
        right = second[256:288].astype(F32) + second[288:320].astype(F32)
        w0[...] = left[:16]
        g1[:8] = left[16:24]
        g1[8:] = right[:8]
        g2[...] = right[8:24]

    on_core(lambda: put(own, got), lambda: put(got, own))
    z = hdot(w0[...], coarse[...])
    z0[...] = z
    lift = lifted(z, wide_in[...], spread[:, :SLOTS])
    for s, jump in zip(SEG, jumped((f0, f1, f2, f3), (n0, n1, n2, n3)), strict=True):
        load1[:, s] = (jump + lift[:, s] - centre * load0[:, s]) * inv
    put_faces(bdot(load1[...].astype(BF16), inverse[...]), (o0, o1, o2, o3))


def solve_kernel(bounds, z0, w0, g1, g2, m0, m1, coarse, spread, wide_in, w1, w2, lift1, lift2):
    centre, inv, alpha = bounds_terms(bounds)
    z, w = z0[...], w0[...]
    after = (g1[...] + dot3(z, m0[...]) - centre * w) * inv
    w1[...] = after
    z1 = hdot(after, coarse[...])
    image = (g2[...] + dot3(z, m1[...]) - centre * g1[...]) * inv
    last = alpha * (image + dot3(z1, m0[...]) - centre * after) - w
    w2[...] = last
    z2 = hdot(last, coarse[...])
    lift = lifted(jnp.concatenate([z1, z2], axis=0), wide_in[...], spread[:, :SLOTS])
    lift1[...] = lift[:RHS]
    lift2[...] = lift[RHS:]


def next_kernel(
    bounds, lift, n0, n1, n2, n3, f0, f1, f2, f3, before, now, inverse, load, o0, o1, o2, o3,
):
    centre, _, alpha = bounds_terms(bounds)
    for s, jump in zip(SEG, jumped((f0, f1, f2, f3), (n0, n1, n2, n3)), strict=True):
        load[:, s] = alpha * (jump + lift[:, s] - centre * now[:, s]) - before[:, s]
    put_faces(bdot(load[...].astype(BF16), inverse[...]), (o0, o1, o2, o3))


def terms_kernel(load3, f0, f1, f2, f3, spread, wide_in, w3, g3):
    u = jnp.concatenate([f[...] for f in (f0, f1, f2, f3)], axis=1)
    w, g = terms_of(load3[...], u, wide_in[...], spread[:, :SLOTS])
    w3[...] = w
    g3[...] = g


def gram_kernel(bounds, block, load1, load2, load3, f0, f2, n0, n2, w3, g3, known4, keep, send, stack):
    centre, _, alpha = bounds_terms(bounds)
    left, right = slice(0, FACE), slice(FACE, 2 * FACE)
    stack[:RHS] = block[...]
    for level, load in ((1, load1), (2, load2), (3, load3)):
        stack[level * RHS : (level + 1) * RHS, left] = load[:, SEG[0]]
        stack[level * RHS : (level + 1) * RHS, right] = load[:, SEG[2]]
    for half, s, f, n in ((left, SEG[0], f0, n0), (right, SEG[2], f2, n2)):
        known4[:, half] = alpha * (f[...] - n[...] - centre * load3[:, s]) - load2[:, s]
    stack[4 * RHS : 5 * RHS] = known4[...]
    stack[BLOCKS * RHS :] = jnp.zeros((128 - BLOCKS * RHS, 2 * FACE), F32)
    terms = hdot(stack[: BLOCKS * RHS], stack[...], NT)
    t = [terms[i * RHS : (i + 1) * RHS] for i in range(BLOCKS)]
    lane = lax.broadcasted_iota(jnp.int32, (RHS, 128), 1)
    first = jnp.where(lane < 80, t[0], pltpu.roll(t[2], 48, 1))
    second = jnp.where(lane < 64, pltpu.roll(t[1], 112, 1), pltpu.roll(t[3], 16, 1))
    second = jnp.where(lane < 96, second, pltpu.roll(t[4], 32, 1))
    packed = jnp.concatenate([first, second], axis=1)
    split_by_core(
        jnp.concatenate([w3[...], jnp.zeros((RHS, NCO), F32)], axis=0),
        jnp.concatenate([g3[...], packed], axis=0),
        keep,
        send,
    )


def coded(total):
    zero = lax.axis_index("core") == 0
    return jnp.where(zero, jnp.concatenate(high_low(total[:RHS]), axis=0), total).astype(BF16)


def decoded(total):
    zero = lax.axis_index("core") == 0
    whole = jnp.concatenate([total[:RHS] + total[RHS:], jnp.zeros((RHS, NCO), F32)], axis=0)
    return jnp.where(zero, whole, total)


def plane1_kernel(keep, got, out):
    value = coded(keep[...] + got[...])
    for p in range(16):
        out[p] = value


def depth1_kernel(got, out):
    value = coded(decoded(summed(got)))
    for q in range(8):
        out[q] = value


def sum_kernel(got, out):
    out[...] = decoded(summed(got))


def final_kernel(
    bounds, own, got, coarse, matrix, w0, w1, w2, known4, block, load1, load2, load3, spread, wide_in,
    basis, gram, square,
):
    centre, _, alpha = bounds_terms(bounds)
    basis[0] = block[...]
    for level, load in ((1, load1), (2, load2), (3, load3)):
        basis[level, :, :FACE] = load[:, SEG[0]]
        basis[level, :, FACE:] = load[:, SEG[2]]
    zero = lax.axis_index("core") == 0
    w3 = jnp.where(zero, own[:RHS], got[:RHS])
    second = jnp.where(zero, got[...], own[...])
    g3, packed = second[:RHS], second[RHS:]
    z3 = hdot(w3, coarse[...])
    lift = lifted(z3, wide_in[...], spread[:, :SLOTS])
    basis[4, :, :FACE] = known4[:, :FACE] + alpha * lift[:, SEG[0]]
    basis[4, :, FACE:] = known4[:, FACE:] + alpha * lift[:, SEG[2]]
    wk = alpha * (g3 - centre * w3) - w2[...]
    z_row = jnp.concatenate([jnp.zeros((64, NCO), F32), z3, jnp.zeros((48, NCO), F32)], axis=0)
    rows = jnp.concatenate([w0[...], w1[...], w2[...], w3, wk, dot3(z3, matrix[...])], axis=0)
    cross = hdot(rows, z_row, NT)
    h0, h1 = packed[:, :128], packed[:, 128:]
    parts = [h0, pltpu.roll(h1, 16, 1), pltpu.roll(h0, 80, 1), pltpu.roll(h1, 112, 1), pltpu.roll(h1, 96, 1)]
    square[...] = jnp.zeros((128, 128), F32)
    for i in range(BLOCKS):
        square[i * RHS : (i + 1) * RHS] = parts[i] + alpha * cross[i * RHS : (i + 1) * RHS]
    last = slice(4 * RHS, 5 * RHS)
    square[last] = square[last] + alpha * alpha * cross[5 * RHS :]
    sided = jnp.concatenate([jnp.zeros((64, 128), F32), alpha * cross[last], jnp.zeros((48, 128), F32)], axis=0)
    up = square[...]
    r = lax.broadcasted_iota(jnp.int32, (128, 128), 0) // RHS
    c = lax.broadcasted_iota(jnp.int32, (128, 128), 1) // RHS
    whole = jnp.where(r <= c, up, up.T) + jnp.where(jnp.logical_and(r == 4, c == 4), sided.T, 0.0)
    gram[...] = (whole * (1.0 / (2 * FACE * 64)))[: BLOCKS * RHS, : BLOCKS * RHS]


def body(residual, bounds, local_inverse, corner_basis, corner_map, coarse_inverse):
    inverse = local_inverse.reshape(WIDTH, WIDTH)
    corners = corner_basis.reshape(-1, WIDTH)
    count = corners.shape[0]
    face = ((RHS, FACE), F32)
    load = ((RHS, WIDTH), F32)
    small = ((RHS, NCO), F32)
    smem, hbm = pltpu.SMEM, pl.ANY

    up_sub, up_grp, low_sub, low_grp, labels, own_row, block, corners = call(
        pack_kernel,
        [((64, FACE), BF16), ((64, FACE), BF16), ((32, FACE), BF16), ((32, FACE), BF16),
         ((1, 256), jnp.int32), ((8, NCO), F32), ((RHS, 2 * FACE), F32), ((count, WIDTH), BF16)],
        [residual, corners, corner_map.reshape(1, count), coarse_inverse],
        [hbm] * 4,
        [pltpu.VMEM((RHS, 1, 1, 2 * FACE), F32), pltpu.VMEM((1, count), jnp.int32), pltpu.VMEM((1, NCO), F32),
         pltpu.SemaphoreType.DMA((4,))],
    )
    from_prev_sub = along(up_sub, SUB, 1)
    from_prev_grp = along(up_grp, "x", 1)
    from_next_sub = along(low_sub, SUB, -1)
    from_next_grp = along(low_grp, "x", -1)

    def neighbours(faces):
        return [
            along(faces[1], SUB, -1),
            along(faces[0], SUB, 1),
            along(faces[3], "x", -1),
            along(faces[2], "x", 1),
        ]

    load0, wide, spread, *u0 = call(
        start_kernel,
        [load, ((SLOTS, WIDTH), BF16), ((NCO, 256), BF16), face, face, face, face],
        [block, from_prev_sub, from_prev_grp, from_next_sub, from_next_grp, corners, labels, inverse],
    )
    near0 = neighbours(u0)
    m0, m1, w0, g1 = call(
        moment_kernel,
        [((NCO, NCO), F32), ((NCO, NCO), F32), small, small],
        [load0, *u0, wide, spread, inverse],
    )
    keep, send = call(
        join_kernel,
        [((280, NCO), F32), ((280, NCO), F32)],
        [*near0, *u0, wide, spread, inverse, m0, m1, w0, g1],
    )
    (v,) = call(plane0_kernel, [((16, 24, NCO), BF16)], [keep, swapped(send)])
    (v,) = call(depth0_kernel, [((8, 24, NCO), BF16)], [exchange(v, PLANE), own_row])
    (v,) = call(spread0_kernel, [((16, 40, NCO), BF16)], [exchange(v, "z")])
    (own,) = call(collect0_kernel, [((576, NCO), BF16)], [exchange(v, PLANE)])

    coarse, m0, m1, w0, g1, g2, z0, load1, *u1 = call(
        block1_kernel,
        [((NCO, NCO), F32), ((NCO, NCO), BF16), ((NCO, NCO), BF16), small, small, small, small, load,
         face, face, face, face],
        [bounds, own, swapped(own), load0, *near0, *u0, spread, wide, inverse],
        [smem] + [None] * 14,
    )
    near1 = neighbours(u1)
    w1, w2, lift1, lift2 = call(
        solve_kernel,
        [small, small, load, load],
        [bounds, z0, w0, g1, g2, m0, m1, coarse, spread, wide],
        [smem] + [None] * 9,
    )
    load2, *u2 = call(
        next_kernel,
        [load, face, face, face, face],
        [bounds, lift1, *near1, *u1, load0, load1, inverse],
        [smem] + [None] * 12,
    )
    near2 = neighbours(u2)
    load3, *u3 = call(
        next_kernel,
        [load, face, face, face, face],
        [bounds, lift2, *near2, *u2, load1, load2, inverse],
        [smem] + [None] * 12,
    )
    n0, n2 = along(u3[1], SUB, -1), along(u3[3], "x", -1)
    w3, g3 = call(terms_kernel, [small, small], [load3, *u3, spread, wide])
    known4, keep, send = call(
        gram_kernel,
        [((RHS, 2 * FACE), F32), ((32, NCO), F32), ((32, NCO), F32)],
        [bounds, block, load1, load2, load3, u3[0], u3[2], n0, n2, w3, g3],
        [smem] + [None] * 10,
        [pltpu.VMEM((128, 2 * FACE), F32)],
    )
    (v,) = call(plane1_kernel, [((16, 32, NCO), BF16)], [keep, swapped(send)])
    (v,) = call(depth1_kernel, [((8, 32, NCO), BF16)], [exchange(v, PLANE)])
    (own,) = call(sum_kernel, [((32, NCO), F32)], [exchange(v, "z")])
    basis, gram = call(
        final_kernel,
        [((BLOCKS, RHS, 2 * FACE), F32), ((BLOCKS * RHS, BLOCKS * RHS), F32)],
        [bounds, own, swapped(own), coarse, m0, w0, w1, w2, known4, block, load1, load2, load3, spread, wide],
        [smem] + [None] * 14,
        [pltpu.VMEM((128, 128), F32)],
    )
    return basis.reshape(BLOCKS, RHS, 1, 1, 2 * FACE), gram


def solution(mesh):
    split = Mesh(mesh.devices.reshape(8, 4, 2, mesh.shape["grp"]), ("z", "y", "core", "x"))
    in_specs = (
        P(None, SUB, "x", None),
        P(),
        P(SUB, "x", None, None),
        P(SUB, "x", None, None),
        P(SUB, "x", None),
        P(("z", "y", "core", "x"), None),
    )
    out_specs = (P(None, None, SUB, "x", None), P())
    return jax.shard_map(body, mesh=split, in_specs=in_specs, out_specs=out_specs, check_vma=False)
```

```python
import functools

import jax
import jax.numpy as jnp
from jax import lax
from jax.experimental import pallas as pl
from jax.experimental.pallas import tpu as pltpu
from jax.sharding import Mesh
from jax.sharding import PartitionSpec as P

BLOCKS = 5
RHS = 16
FACE = 256
WIDTH = 4 * FACE
NCO = 256
SLOT = 32
SLOTS = 5 * SLOT
SUB = ("z", "y", "core")
PLANE = ("y", "x")
HIGH = lax.Precision.HIGHEST
F32, BF16 = jnp.float32, jnp.bfloat16
SEG = [slice(i * FACE, (i + 1) * FACE) for i in range(4)]


NN = (((1,), (0,)), ((), ()))
NT = (((1,), (1,)), ((), ()))


def hdot(a, b, dims=NN):
    return lax.dot_general(a, b, dims, precision=HIGH, preferred_element_type=F32)


def bdot(a, b, dims=NN):
    return lax.dot_general(a, b, dims, preferred_element_type=F32)


def dot3(a, exact, dims=NN):
    rows = a.shape[0]
    top = a.astype(BF16)
    rest = a - top.astype(F32)
    mid = rest.astype(BF16)
    low = (rest - mid.astype(F32)).astype(BF16)
    got = bdot(jnp.concatenate([top, mid, low], axis=0), exact, dims)
    return got[:rows] + got[rows : 2 * rows] + got[2 * rows :]


def call(kernel, outs, args, spaces=None, scratch=(), limit=12, out_space=None):
    vmem = pl.BlockSpec(memory_space=pltpu.VMEM)
    out_spec = pl.BlockSpec(memory_space=out_space) if out_space is not None else vmem
    specs = [vmem if s is None else pl.BlockSpec(memory_space=s) for s in (spaces or [None] * len(args))]
    return pl.pallas_call(
        kernel,
        out_shape=[jax.ShapeDtypeStruct(s, d) for s, d in outs],
        in_specs=specs,
        out_specs=[out_spec] * len(outs),
        scratch_shapes=list(scratch),
        compiler_params=pltpu.CompilerParams(vmem_limit_bytes=limit << 20),
        name=kernel.__name__,
    )(*args)


def along(x, axis, by):
    count = lax.axis_size(axis)
    return lax.ppermute(x, axis, [(i, (i + by) % count) for i in range(count)])


def exchange(x, axis):
    return lax.all_to_all(x, axis, split_axis=0, concat_axis=0, tiled=True)


def swapped(v):
    return along(v, "core", 1)


def in_pairs(v, axis, first):
    count = lax.axis_size(axis)
    pairs = []
    for i in range(first, first + count, 2):
        a, b = i % count, (i + 1) % count
        pairs += [(a, b), (b, a)]
    return lax.ppermute(v, axis, pairs)


def neighbours(sends):
    inter = in_pairs(sends[1], SUB, 1)
    odd = in_pairs(sends[3], "x", 1)
    even = in_pairs(sends[2], "x", 0)
    intra = swapped(sends[0])
    return [intra, inter, even, odd]


def bounds_of(ref):
    low, high = ref[0], ref[1]
    centre = (low + high) * 0.5
    return centre, 1.0 / jnp.full((1, 128), (high - low) * 0.5, F32)[:, :1]


def label_of(n):
    return ((n // 4) % 2) * 128 + ((n // 8) % 4 * 4 + n % 4) * 8 + n // 32


def pack_kernel(
    block_hbm, corners_hbm, ids_hbm, row_hbm,
    intra, inter, even, odd, labels, own_row, block, corners, wide_block, given, row, packs, sems,
):
    copies = [
        pltpu.make_async_copy(src, dst, sems.at[i])
        for i, (src, dst) in enumerate(
            ((block_hbm, wide_block), (corners_hbm, corners), (ids_hbm, given), (row_hbm, row))
        )
    ]
    for copy in copies:
        copy.start()
    n = lax.broadcasted_iota(jnp.int32, (NCO, NCO), 0)
    m = lax.broadcasted_iota(jnp.int32, (NCO, NCO), 1)
    order = (label_of(n) == m).astype(F32).astype(BF16)
    first = lax.broadcasted_iota(jnp.int32, (8, NCO), 0) == 0
    for copy in copies:
        copy.wait()
    count = corners.shape[0]
    labels[...] = jnp.full((1, 256), -1, jnp.int32)
    labels[:, :count] = label_of(given[...])
    text = labels[...].astype(F32).astype(BF16)
    x = wide_block[...].reshape(RHS, 2 * FACE)
    block[...] = x
    top = x.astype(BF16)
    rest = (x - top.astype(F32)).astype(BF16)
    for i, s in enumerate(SEG):
        if i % 2 == 0:
            packs[i, :RHS] = top[:, SEG[i // 2]]
            packs[i, RHS : 2 * RHS] = rest[:, SEG[i // 2]]
        else:
            packs[i, : 2 * RHS] = jnp.zeros((2 * RHS, FACE), BF16)
        packs[i, 2 * RHS : 2 * RHS + count] = corners[:, s]
        packs[i, 2 * RHS + count :] = jnp.broadcast_to(text, (8, FACE))
    put_sends([packs[i] for i in range(4)], (intra, inter, even, odd))
    moved = dot3(jnp.broadcast_to(row[...], (RHS, NCO)), order)[:8]
    own_row[...] = jnp.where(first, moved, 0.0)


def terms_of(load, u, wide, spread_t):
    both = dot3(dot3(jnp.concatenate([load * 0.5, u], axis=0), wide, NT), spread_t, NT)
    return both[:RHS], both[RHS:]


def lifted(z, wide, spread_t):
    return dot3(dot3(z, spread_t), wide)


def either(axis, even_branch, odd_branch):
    even = lax.axis_index(axis) % 2 == 0
    pl.when(even)(even_branch)
    pl.when(jnp.logical_not(even))(odd_branch)


def on_core(zero_branch, other_branch):
    either("core", zero_branch, other_branch)


def put_pair(axis, up, low, first, second):
    def even():
        first[...] = up
        second[...] = low

    def odd():
        first[...] = low
        second[...] = up

    either(axis, even, odd)


def put_sends(faces, outs):
    put_pair("core", faces[0], faces[1], outs[0], outs[1])
    put_pair("x", faces[2], faces[3], outs[2], outs[3])


def put_image(u, out, sends):
    out[...] = u
    put_sends([u[:, s] for s in SEG], sends)


def arrived(refs):
    values = [r[...] for r in refs]
    if values[0].dtype != F32:
        values = [v.astype(F32) for v in values]
    zero, even = lax.axis_index("core") == 0, lax.axis_index("x") % 2 == 0
    return [
        jnp.where(zero, values[0], values[1]),
        jnp.where(zero, values[1], values[0]),
        jnp.where(even, values[2], values[3]),
        jnp.where(even, values[3], values[2]),
    ]


def split_by_core(first, second, keep, send):
    def zero():
        keep[...] = first
        send[...] = second

    def one():
        keep[...] = second
        send[...] = first

    on_core(zero, one)


def high_low(x):
    top = x.astype(BF16).astype(F32)
    return top, x - top


def start_kernel(
    block, intra, inter, even, odd, corners, labels, inverse, load_out, wide_out, spread_out, image, s0, s1, s2, s3,
):
    count = corners.shape[0]
    k = 2 * RHS
    next_sub, prev_sub, next_grp, prev_grp = arrived((intra, inter, even, odd))
    load_out[:, SEG[0]] = block[:, :FACE]
    load_out[:, SEG[1]] = -(prev_sub[:RHS] + prev_sub[RHS:k])
    load_out[:, SEG[2]] = block[:, FACE:]
    load_out[:, SEG[3]] = -(prev_grp[:RHS] + prev_grp[RHS:k])
    put_image(bdot(load_out[...].astype(BF16), inverse[...]), image, (s0, s1, s2, s3))
    wide_out[...] = jnp.zeros((SLOTS, WIDTH), BF16)
    wide_out[:count] = corners[...]
    others = (next_sub, prev_sub, next_grp, prev_grp)
    for i, other in enumerate(others):
        wide_out[SLOT * (i + 1) : SLOT * (i + 1) + count, SEG[i]] = (-other[k : k + count]).astype(BF16)
    lane = lax.broadcasted_iota(jnp.int32, (8, 256), 1)
    ids = jnp.where(lane < SLOT, jnp.broadcast_to(labels[...], (8, 256)).astype(F32), -1.0)
    for i, other in enumerate(others):
        moved = pltpu.roll(other[k + count :], SLOT * (i + 1), 1)
        mine = jnp.logical_and(lane >= SLOT * (i + 1), lane < SLOT * (i + 2))
        ids = jnp.where(mine, moved, ids)
    number = lax.broadcasted_iota(jnp.int32, (NCO, 256), 0).astype(F32)
    spread_out[...] = (number == ids[:1]).astype(F32).astype(BF16)


def moment_kernel(load0, image, wide_in, spread, inverse, m0, m1, w0, g1):
    wide, spread_t = wide_in[...], spread[:, :SLOTS]
    spread_wide = spread_t.astype(F32)
    m0[...] = hdot(spread_wide, dot3(bdot(wide, wide, NT) * 0.5, spread_t, NT))
    pairs = dot3(bdot(wide, inverse[...]), wide, NT)
    m1[...] = hdot(spread_wide, dot3(pairs, spread_t, NT))
    w, g = terms_of(load0[...], image[...], wide, spread_t)
    w0[...] = w
    g1[...] = g


def jumped(image, near):
    return [image[:, s] - n for s, n in zip(SEG, arrived(near), strict=True)]


def join_kernel(n0, n1, n2, n3, image, wide_in, spread, inverse, m0, m1, w0, g1, keep, send):
    jump = jnp.concatenate(jumped(image, (n0, n1, n2, n3)), axis=1)
    top, rest = high_low(jump)
    u = bdot(jnp.concatenate([top.astype(BF16), rest.astype(BF16)], axis=0), inverse[...])
    u = u[:RHS] + u[RHS:]
    g2 = dot3(dot3(u, wide_in[...], NT), spread[:, :SLOTS], NT)

    def put(first, second):
        first[:NCO] = m0[...]
        first[NCO : NCO + RHS] = w0[...]
        first[NCO + RHS :] = g1[:8]
        second[:NCO] = m1[...]
        second[NCO : NCO + 8] = g1[8:]
        second[NCO + 8 :] = g2

    on_core(lambda: put(keep, send), lambda: put(send, keep))


def plane0_kernel(keep, got, out):
    for p in range(16):
        rows = slice(16 * p, 16 * p + 16)
        pieces = [keep[rows] + got[rows]]
        if p < 12:
            rows = slice(NCO + 2 * p, NCO + 2 * p + 2)
            pieces += [*high_low(keep[rows] + got[rows]), jnp.zeros((4, NCO), F32)]
        else:
            pieces += [jnp.zeros((8, NCO), F32)]
        out[p] = jnp.concatenate(pieces, axis=0).astype(BF16)


def summed(got):
    total = got[0].astype(F32)
    for p in range(1, got.shape[0]):
        total = total + got[p].astype(F32)
    return total


def depth0_kernel(got, own_row, out):
    total = summed(got)
    g = total[16:18] + total[18:20]
    rows = [total[:16], *high_low(g), *high_low(own_row[:1]), jnp.zeros((2, NCO), F32)]
    value = jnp.concatenate(rows, axis=0).astype(BF16)
    for q in range(8):
        out[q] = value


def spread0_kernel(got, out):
    every = [got[q].astype(F32) for q in range(8)]
    total = functools.reduce(jnp.add, every)
    g = total[16:18] + total[18:20]
    rows = [total[:16], *high_low(g), jnp.zeros((4, NCO), F32)]
    rows += [r[20:21] for r in every] + [r[21:22] for r in every]
    value = jnp.concatenate(rows, axis=0).astype(BF16)
    for p in range(16):
        out[p] = value


def collect0_kernel(got, out):
    g = []
    for p in range(16):
        out[16 * p : 16 * p + 16] = got[p, :16]
        g.append(got[p, 16:24].astype(F32))
        out[320 + 8 * p : 328 + 8 * p] = got[p, 24:32]
        out[448 + 8 * p : 456 + 8 * p] = got[p, 32:40]
    out[256:320] = jnp.concatenate([r[:2] for r in g] + [r[2:4] for r in g], axis=0).astype(BF16)


def bounds_terms(ref):
    centre, inv = bounds_of(ref)
    return centre, inv, 2.0 * inv


def block1_kernel(
    bounds, own, got, load0, n0, n1, n2, n3, image, spread, wide_in, inverse,
    coarse, m0, m1, w0, g1, g2, z0, load1, image1, s0, s1, s2, s3,
):
    centre, inv, _ = bounds_terms(bounds)

    def put(first, second):
        for half, part in ((slice(0, 128), first), (slice(128, 256), second)):
            coarse[half] = part[320:448].astype(F32) + part[448:576].astype(F32)
        m0[...] = first[:NCO]
        m1[...] = second[:NCO]
        left = first[256:288].astype(F32) + first[288:320].astype(F32)
        right = second[256:288].astype(F32) + second[288:320].astype(F32)
        w0[...] = left[:16]
        g1[:8] = left[16:24]
        g1[8:] = right[:8]
        g2[...] = right[8:24]

    on_core(lambda: put(own, got), lambda: put(got, own))
    z = hdot(w0[...], coarse[...])
    z0[...] = z
    lift = lifted(z, wide_in[...], spread[:, :SLOTS])
    for s, jump in zip(SEG, jumped(image, (n0, n1, n2, n3)), strict=True):
        load1[:, s] = (jump + lift[:, s] - centre * load0[:, s]) * inv
    put_image(bdot(load1[...].astype(BF16), inverse[...]), image1, (s0, s1, s2, s3))


def solve_kernel(bounds, z0, w0, g1, g2, m0, m1, coarse, spread, wide_in, w1, w2, lift1, lift2):
    centre, inv, alpha = bounds_terms(bounds)
    z, w = z0[...], w0[...]
    after = (g1[...] + dot3(z, m0[...]) - centre * w) * inv
    w1[...] = after
    z1 = hdot(after, coarse[...])
    image = (g2[...] + dot3(z, m1[...]) - centre * g1[...]) * inv
    last = alpha * (image + dot3(z1, m0[...]) - centre * after) - w
    w2[...] = last
    z2 = hdot(last, coarse[...])
    lift = lifted(jnp.concatenate([z1, z2], axis=0), wide_in[...], spread[:, :SLOTS])
    lift1[...] = lift[:RHS]
    lift2[...] = lift[RHS:]


def next_kernel(
    bounds, lift, n0, n1, n2, n3, image, before, now, inverse, load, image_out, s0, s1, s2, s3,
):
    centre, _, alpha = bounds_terms(bounds)
    for s, jump in zip(SEG, jumped(image, (n0, n1, n2, n3)), strict=True):
        load[:, s] = alpha * (jump + lift[:, s] - centre * now[:, s]) - before[:, s]
    put_image(bdot(load[...].astype(BF16), inverse[...]), image_out, (s0, s1, s2, s3))


def last_kernel(
    bounds, lift, n0, n1, n2, n3, image, before, now, inverse, load, image_out, low_sub, low_grp,
):
    centre, _, alpha = bounds_terms(bounds)
    for s, jump in zip(SEG, jumped(image, (n0, n1, n2, n3)), strict=True):
        load[:, s] = alpha * (jump + lift[:, s] - centre * now[:, s]) - before[:, s]
    u = bdot(load[...].astype(BF16), inverse[...])
    image_out[...] = u
    low_sub[...] = u[:, SEG[1]]
    low_grp[...] = u[:, SEG[3]]


def terms_kernel(bounds, block, load1, load2, load3, image, spread, wide_in, w3, g3, stack, early, partial4):
    centre, _, alpha = bounds_terms(bounds)
    w, g = terms_of(load3[...], image[...], wide_in[...], spread[:, :SLOTS])
    w3[...] = w
    g3[...] = g
    left, right = slice(0, FACE), slice(FACE, 2 * FACE)
    stack[:RHS] = block[...]
    for level, load in ((1, load1), (2, load2), (3, load3)):
        stack[level * RHS : (level + 1) * RHS, left] = load[:, SEG[0]]
        stack[level * RHS : (level + 1) * RHS, right] = load[:, SEG[2]]
    for half, s in ((left, SEG[0]), (right, SEG[2])):
        partial4[:, half] = alpha * (image[:, s] - centre * load3[:, s]) - load2[:, s]
    early[...] = hdot(stack[...], stack[...], NT)


def gram_kernel(bounds, stack, early, partial4, n0, n2, w3, g3, known4, keep, send):
    _, _, alpha = bounds_terms(bounds)
    known4[:, :FACE] = partial4[:, :FACE] - alpha * n0[...]
    known4[:, FACE:] = partial4[:, FACE:] - alpha * n2[...]
    q = known4[...]
    q_all = jnp.concatenate([stack[...], q, jnp.zeros((48, 2 * FACE), F32)], axis=0)
    late = hdot(q, q_all, NT)
    late = jnp.concatenate([late[:, :64].T, late[:, 64:80]], axis=0)
    terms = jnp.concatenate(
        [
            jnp.concatenate([early[...], jnp.zeros((RHS, 64), F32)], axis=0),
            late,
            jnp.zeros((BLOCKS * RHS, 48), F32),
        ],
        axis=1,
    )
    t = [terms[i * RHS : (i + 1) * RHS] for i in range(BLOCKS)]
    lane = lax.broadcasted_iota(jnp.int32, (RHS, 128), 1)
    first = jnp.where(lane < 80, t[0], pltpu.roll(t[2], 48, 1))
    second = jnp.where(lane < 64, pltpu.roll(t[1], 112, 1), pltpu.roll(t[3], 16, 1))
    second = jnp.where(lane < 96, second, pltpu.roll(t[4], 32, 1))
    packed = jnp.concatenate([first, second], axis=1)
    split_by_core(
        jnp.concatenate([w3[...], jnp.zeros((RHS, NCO), F32)], axis=0),
        jnp.concatenate([g3[...], packed], axis=0),
        keep,
        send,
    )


def coded(total):
    zero = lax.axis_index("core") == 0
    return jnp.where(zero, jnp.concatenate(high_low(total[:RHS]), axis=0), total).astype(BF16)


def decoded(total):
    zero = lax.axis_index("core") == 0
    whole = jnp.concatenate([total[:RHS] + total[RHS:], jnp.zeros((RHS, NCO), F32)], axis=0)
    return jnp.where(zero, whole, total)


def plane1_kernel(keep, got, out):
    value = coded(keep[...] + got[...])
    for p in range(16):
        out[p] = value


def depth1_kernel(got, out):
    value = coded(decoded(summed(got)))
    for q in range(8):
        out[q] = value


def sum_kernel(got, out):
    out[...] = decoded(summed(got))


def final_kernel(
    bounds, own, got, coarse, matrix, w0, w1, w2, known4, block, load1, load2, load3, spread, wide_in,
    basis_hbm, gram_hbm, basis, gram, square, sems,
):
    centre, _, alpha = bounds_terms(bounds)
    basis[0] = block[...].reshape(RHS, 1, 1, 2 * FACE)
    for level, load in ((1, load1), (2, load2), (3, load3)):
        value = jnp.concatenate([load[:, SEG[0]], load[:, SEG[2]]], axis=1)
        basis[level] = value.reshape(RHS, 1, 1, 2 * FACE)
    early = pltpu.make_async_copy(basis.at[:4], basis_hbm.at[:4], sems.at[0])
    early.start()
    zero = lax.axis_index("core") == 0
    w3 = jnp.where(zero, own[:RHS], got[:RHS])
    second = jnp.where(zero, got[...], own[...])
    g3, packed = second[:RHS], second[RHS:]
    z3 = hdot(w3, coarse[...])
    lift = lifted(z3, wide_in[...], spread[:, :SLOTS])
    value = known4[...] + alpha * jnp.concatenate([lift[:, SEG[0]], lift[:, SEG[2]]], axis=1)
    basis[4] = value.reshape(RHS, 1, 1, 2 * FACE)
    late = pltpu.make_async_copy(basis.at[4], basis_hbm.at[4], sems.at[1])
    late.start()
    wk = alpha * (g3 - centre * w3) - w2[...]
    z_row = jnp.concatenate([jnp.zeros((64, NCO), F32), z3, jnp.zeros((48, NCO), F32)], axis=0)
    rows = jnp.concatenate([w0[...], w1[...], w2[...], w3, wk, dot3(z3, matrix[...])], axis=0)
    cross = hdot(rows, z_row, NT)
    h0, h1 = packed[:, :128], packed[:, 128:]
    parts = [h0, pltpu.roll(h1, 16, 1), pltpu.roll(h0, 80, 1), pltpu.roll(h1, 112, 1), pltpu.roll(h1, 96, 1)]
    square[...] = jnp.zeros((128, 128), F32)
    for i in range(BLOCKS):
        square[i * RHS : (i + 1) * RHS] = parts[i] + alpha * cross[i * RHS : (i + 1) * RHS]
    last = slice(4 * RHS, 5 * RHS)
    square[last] = square[last] + alpha * alpha * cross[5 * RHS :]
    sided = jnp.concatenate([jnp.zeros((64, 128), F32), alpha * cross[last], jnp.zeros((48, 128), F32)], axis=0)
    up = square[...]
    r = lax.broadcasted_iota(jnp.int32, (128, 128), 0) // RHS
    c = lax.broadcasted_iota(jnp.int32, (128, 128), 1) // RHS
    whole = jnp.where(r <= c, up, up.T) + jnp.where(jnp.logical_and(r == 4, c == 4), sided.T, 0.0)
    gram[...] = (whole * (1.0 / (2 * FACE * 64)))[: BLOCKS * RHS, : BLOCKS * RHS]
    result = pltpu.make_async_copy(gram, gram_hbm, sems.at[2])
    result.start()
    early.wait()
    late.wait()
    result.wait()


def fetch_kernel(inverse_hbm, out, sem):
    copy = pltpu.make_async_copy(inverse_hbm, out, sem)
    copy.start()
    copy.wait()


def body(residual, bounds, local_inverse, corner_basis, corner_map, coarse_inverse):
    corners = corner_basis.reshape(-1, WIDTH)
    count = corners.shape[0]
    face = ((RHS, FACE), F32)
    load = ((RHS, WIDTH), F32)
    small = ((RHS, NCO), F32)
    smem, hbm = pltpu.SMEM, pltpu.HBM

    *packs, labels, own_row, block, corners = call(
        pack_kernel,
        [((64, FACE), BF16)] * 4
        + [((1, 256), jnp.int32), ((8, NCO), F32), ((RHS, 2 * FACE), F32), ((count, WIDTH), BF16)],
        [residual, corners, corner_map.reshape(1, count), coarse_inverse],
        [hbm] * 4,
        [pltpu.VMEM((RHS, 1, 1, 2 * FACE), F32), pltpu.VMEM((1, count), jnp.int32), pltpu.VMEM((1, NCO), F32),
         pltpu.VMEM((4, 64, FACE), BF16), pltpu.SemaphoreType.DMA((4,))],
    )
    near = neighbours(packs)
    (inverse,) = call(
        fetch_kernel,
        [((WIDTH, WIDTH), BF16)],
        [local_inverse.reshape(WIDTH, WIDTH)],
        [hbm],
        [pltpu.SemaphoreType.DMA(())],
    )
    load0, wide, spread, image0, *sends = call(
        start_kernel,
        [load, ((SLOTS, WIDTH), BF16), ((NCO, 256), BF16), load, face, face, face, face],
        [block, *near, corners, labels, inverse],
    )
    near0 = neighbours(sends)
    m0, m1, w0, g1 = call(
        moment_kernel,
        [((NCO, NCO), F32), ((NCO, NCO), F32), small, small],
        [load0, image0, wide, spread, inverse],
    )
    keep, send = call(
        join_kernel,
        [((280, NCO), F32), ((280, NCO), F32)],
        [*near0, image0, wide, spread, inverse, m0, m1, w0, g1],
    )
    (v,) = call(plane0_kernel, [((16, 24, NCO), BF16)], [keep, swapped(send)])
    (v,) = call(depth0_kernel, [((8, 24, NCO), BF16)], [exchange(v, PLANE), own_row])
    (v,) = call(spread0_kernel, [((16, 40, NCO), BF16)], [exchange(v, "z")])
    (own,) = call(collect0_kernel, [((576, NCO), BF16)], [exchange(v, PLANE)])

    coarse, m0, m1, w0, g1, g2, z0, load1, image1, *sends = call(
        block1_kernel,
        [((NCO, NCO), F32), ((NCO, NCO), BF16), ((NCO, NCO), BF16), small, small, small, small, load, load,
         face, face, face, face],
        [bounds, own, swapped(own), load0, *near0, image0, spread, wide, inverse],
        [smem] + [None] * 11,
    )
    near1 = neighbours(sends)
    w1, w2, lift1, lift2 = call(
        solve_kernel,
        [small, small, load, load],
        [bounds, z0, w0, g1, g2, m0, m1, coarse, spread, wide],
        [smem] + [None] * 9,
    )
    load2, image2, *sends = call(
        next_kernel,
        [load, load, face, face, face, face],
        [bounds, lift1, *near1, image1, load0, load1, inverse],
        [smem] + [None] * 9,
    )
    near2 = neighbours(sends)
    load3, image3, low_sub, low_grp = call(
        last_kernel,
        [load, load, face, face],
        [bounds, lift2, *near2, image2, load1, load2, inverse],
        [smem] + [None] * 9,
    )
    n0, n2 = along(low_sub, SUB, -1), along(low_grp, "x", -1)
    w3, g3, stack, early, partial4 = call(
        terms_kernel,
        [small, small, ((4 * RHS, 2 * FACE), F32), ((4 * RHS, 4 * RHS), F32), ((RHS, 2 * FACE), F32)],
        [bounds, block, load1, load2, load3, image3, spread, wide],
        [smem] + [None] * 7,
    )
    known4, keep, send = call(
        gram_kernel,
        [((RHS, 2 * FACE), F32), ((32, NCO), F32), ((32, NCO), F32)],
        [bounds, stack, early, partial4, n0, n2, w3, g3],
        [smem] + [None] * 7,
    )
    (v,) = call(plane1_kernel, [((16, 32, NCO), BF16)], [keep, swapped(send)])
    (v,) = call(depth1_kernel, [((8, 32, NCO), BF16)], [exchange(v, PLANE)])
    (own,) = call(sum_kernel, [((32, NCO), F32)], [exchange(v, "z")])
    basis, gram = call(
        final_kernel,
        [((BLOCKS, RHS, 1, 1, 2 * FACE), F32), ((BLOCKS * RHS, BLOCKS * RHS), F32)],
        [bounds, own, swapped(own), coarse, m0, w0, w1, w2, known4, block, load1, load2, load3, spread, wide],
        [smem] + [None] * 14,
        [pltpu.VMEM((BLOCKS, RHS, 1, 1, 2 * FACE), F32), pltpu.VMEM((BLOCKS * RHS, BLOCKS * RHS), F32),
         pltpu.VMEM((128, 128), F32), pltpu.SemaphoreType.DMA((3,))],
        out_space=hbm,
    )
    return basis, gram


def solution(mesh):
    split = Mesh(mesh.devices.reshape(8, 4, 2, mesh.shape["grp"]), ("z", "y", "core", "x"))
    in_specs = (
        P(None, SUB, "x", None),
        P(),
        P(SUB, "x", None, None),
        P(SUB, "x", None, None),
        P(SUB, "x", None),
        P(("z", "y", "core", "x"), None),
    )
    out_specs = (P(None, None, SUB, "x", None), P())
    return jax.shard_map(body, mesh=split, in_specs=in_specs, out_specs=out_specs, check_vma=False)
```

```python
import functools

import jax
import jax.numpy as jnp
from jax import lax
from jax.experimental import pallas as pl
from jax.experimental.pallas import tpu as pltpu
from jax.sharding import Mesh
from jax.sharding import PartitionSpec as P

BLOCKS = 5
RHS = 16
FACE = 256
WIDTH = 4 * FACE
NCO = 256
SLOT = 32
SLOTS = 5 * SLOT
SUB = ("z", "y", "core")
PLANE = ("y", "x")
HIGH = lax.Precision.HIGHEST
F32, BF16 = jnp.float32, jnp.bfloat16
SEG = [slice(i * FACE, (i + 1) * FACE) for i in range(4)]


NN = (((1,), (0,)), ((), ()))
NT = (((1,), (1,)), ((), ()))


def hdot(a, b, dims=NN):
    return lax.dot_general(a, b, dims, precision=HIGH, preferred_element_type=F32)


def bdot(a, b, dims=NN):
    return lax.dot_general(a, b, dims, preferred_element_type=F32)


def dot3(a, exact, dims=NN):
    rows = a.shape[0]
    top = a.astype(BF16)
    rest = a - top.astype(F32)
    mid = rest.astype(BF16)
    low = (rest - mid.astype(F32)).astype(BF16)
    got = bdot(jnp.concatenate([top, mid, low], axis=0), exact, dims)
    return got[:rows] + got[rows : 2 * rows] + got[2 * rows :]


def call(kernel, outs, args, spaces=None, scratch=(), limit=12, out_space=None, aliases=None):
    vmem = pl.BlockSpec(memory_space=pltpu.VMEM)
    out_spec = pl.BlockSpec(memory_space=out_space) if out_space is not None else vmem
    specs = [vmem if s is None else pl.BlockSpec(memory_space=s) for s in (spaces or [None] * len(args))]
    return pl.pallas_call(
        kernel,
        out_shape=[jax.ShapeDtypeStruct(s, d) for s, d in outs],
        in_specs=specs,
        out_specs=[out_spec] * len(outs),
        scratch_shapes=list(scratch),
        input_output_aliases=aliases or {},
        compiler_params=pltpu.CompilerParams(vmem_limit_bytes=limit << 20),
        name=kernel.__name__,
    )(*args)


def along(x, axis, by):
    count = lax.axis_size(axis)
    return lax.ppermute(x, axis, [(i, (i + by) % count) for i in range(count)])


def exchange(x, axis):
    return lax.all_to_all(x, axis, split_axis=0, concat_axis=0, tiled=True)


def swapped(v):
    return along(v, "core", 1)


def in_pairs(v, axis, first):
    count = lax.axis_size(axis)
    pairs = []
    for i in range(first, first + count, 2):
        a, b = i % count, (i + 1) % count
        pairs += [(a, b), (b, a)]
    return lax.ppermute(v, axis, pairs)


def neighbours(sends):
    return [
        in_pairs(sends[0], SUB, 1),
        in_pairs(sends[1], "x", 1),
        in_pairs(sends[2], "x", 0),
        swapped(sends[3]),
    ]


def label_of(n):
    return ((n // 4) % 2) * 128 + ((n // 8) % 4 * 4 + n % 4) * 8 + n // 32


def pack_kernel(
    block_hbm, corners_hbm, ids_hbm,
    s0, s1, s2, s3, labels, block, corners, wide_block, given, packs, sems,
):
    copies = [
        pltpu.make_async_copy(src, dst, sems.at[i])
        for i, (src, dst) in enumerate(
            ((block_hbm, wide_block), (corners_hbm, corners), (ids_hbm, given))
        )
    ]
    for copy in copies:
        copy.start()
    for copy in copies:
        copy.wait()
    count = corners.shape[0]
    labels[...] = jnp.full((1, 256), -1, jnp.int32)
    labels[:, :count] = label_of(given[...])
    text = labels[...].astype(F32).astype(BF16)
    x = wide_block[...].reshape(RHS, 2 * FACE)
    block[...] = x
    top = x.astype(BF16)
    rest = (x - top.astype(F32)).astype(BF16)
    for i, s in enumerate(SEG):
        if i % 2 == 0:
            packs[i, :RHS] = top[:, SEG[i // 2]]
            packs[i, RHS : 2 * RHS] = rest[:, SEG[i // 2]]
        else:
            packs[i, : 2 * RHS] = jnp.zeros((2 * RHS, FACE), BF16)
        packs[i, 2 * RHS : 2 * RHS + count] = corners[:, s]
        packs[i, 2 * RHS + count :] = jnp.broadcast_to(text, (8, FACE))
    put_sends([packs[i] for i in range(4)], (s0, s1, s2, s3))


def terms_of(load, u, wide, spread_t):
    both = dot3(dot3(jnp.concatenate([load * 0.5, u], axis=0), wide, NT), spread_t, NT)
    return both[:RHS], both[RHS:]


def lifted(z, wide, spread_t):
    return dot3(dot3(z, spread_t), wide)


def either(axis, even_branch, odd_branch):
    even = lax.axis_index(axis) % 2 == 0
    pl.when(even)(even_branch)
    pl.when(jnp.logical_not(even))(odd_branch)


def on_core(zero_branch, other_branch):
    either("core", zero_branch, other_branch)


def put_pair(axis, up, low, first, second):
    def even():
        first[...] = up
        second[...] = low

    def odd():
        first[...] = low
        second[...] = up

    either(axis, even, odd)


def put_sends(faces, outs):
    put_pair("core", faces[0], faces[1], outs[3], outs[0])
    put_pair("x", faces[2], faces[3], outs[2], outs[1])


def put_image(u, out, sends):
    out[...] = u
    put_sends([u[:, s] for s in SEG], sends)


def arrived(refs):
    values = [r[...] for r in refs]
    if values[0].dtype != F32:
        values = [v.astype(F32) for v in values]
    zero, even = lax.axis_index("core") == 0, lax.axis_index("x") % 2 == 0
    return [
        jnp.where(zero, values[3], values[0]),
        jnp.where(zero, values[0], values[3]),
        jnp.where(even, values[2], values[1]),
        jnp.where(even, values[1], values[2]),
    ]


def split_by_core(first, second, keep, send):
    def zero():
        keep[...] = first
        send[...] = second

    def one():
        keep[...] = second
        send[...] = first

    on_core(zero, one)


def high_low(x):
    top = x.astype(BF16).astype(F32)
    return top, x - top


def start_kernel(
    block, r0, r1, r2, r3, corners, labels, inverse, load_out, wide_out, spread_out, image, s0, s1, s2, s3,
):
    count = corners.shape[0]
    k = 2 * RHS
    next_sub, prev_sub, next_grp, prev_grp = arrived((r0, r1, r2, r3))
    load_out[:, SEG[0]] = block[:, :FACE]
    load_out[:, SEG[1]] = -(prev_sub[:RHS] + prev_sub[RHS:k])
    load_out[:, SEG[2]] = block[:, FACE:]
    load_out[:, SEG[3]] = -(prev_grp[:RHS] + prev_grp[RHS:k])
    put_image(bdot(load_out[...].astype(BF16), inverse[...]), image, (s0, s1, s2, s3))
    wide_out[...] = jnp.zeros((SLOTS, WIDTH), BF16)
    wide_out[:count] = corners[...]
    others = (next_sub, prev_sub, next_grp, prev_grp)
    for i, other in enumerate(others):
        wide_out[SLOT * (i + 1) : SLOT * (i + 1) + count, SEG[i]] = (-other[k : k + count]).astype(BF16)
    lane = lax.broadcasted_iota(jnp.int32, (8, 256), 1)
    ids = jnp.where(lane < SLOT, jnp.broadcast_to(labels[...], (8, 256)).astype(F32), -1.0)
    for i, other in enumerate(others):
        moved = pltpu.roll(other[k + count :], SLOT * (i + 1), 1)
        mine = jnp.logical_and(lane >= SLOT * (i + 1), lane < SLOT * (i + 2))
        ids = jnp.where(mine, moved, ids)
    number = lax.broadcasted_iota(jnp.int32, (NCO, 256), 0).astype(F32)
    spread_out[...] = (number == ids[:1]).astype(F32).astype(BF16)


def moment_kernel(bounds, row, load0, image, wide_in, spread, inverse, coef, own_row, m0, m1, w0, g1):
    low, high = bounds[0], bounds[1]
    centre = jnp.full((1, WIDTH), (low + high) * 0.5, F32)
    inv = 1.0 / jnp.full((1, WIDTH), (high - low) * 0.5, F32)
    coef[...] = jnp.concatenate([centre, inv, 2.0 * inv, jnp.zeros((5, WIDTH), F32)], axis=0)
    n = lax.broadcasted_iota(jnp.int32, (NCO, NCO), 0)
    m = lax.broadcasted_iota(jnp.int32, (NCO, NCO), 1)
    order = (label_of(n) == m).astype(F32).astype(BF16)
    own_row[...] = dot3(jnp.broadcast_to(row[...], (RHS, NCO)), order)[:8]
    wide, spread_t = wide_in[...], spread[:, :SLOTS]
    spread_wide = spread_t.astype(F32)
    m0[...] = hdot(spread_wide, dot3(bdot(wide, wide, NT) * 0.5, spread_t, NT))
    pairs = dot3(bdot(wide, inverse[...]), wide, NT)
    m1[...] = hdot(spread_wide, dot3(pairs, spread_t, NT))
    w, g = terms_of(load0[...], image[...], wide, spread_t)
    w0[...] = w
    g1[...] = g


def jumped(image, near):
    return [image[:, s] - n for s, n in zip(SEG, arrived(near), strict=True)]


def join_kernel(coef, load0, n0, n1, n2, n3, image, wide_in, spread, inverse, m0, m1, w0, g1, base1, keep, send):
    centre, inv, _ = terms_in(coef, WIDTH)
    jump = jnp.concatenate(jumped(image, (n0, n1, n2, n3)), axis=1)
    base1[...] = (jump - centre * load0[...]) * inv
    top, rest = high_low(jump)
    u = bdot(jnp.concatenate([top.astype(BF16), rest.astype(BF16)], axis=0), inverse[...])
    u = u[:RHS] + u[RHS:]
    g2 = dot3(dot3(u, wide_in[...], NT), spread[:, :SLOTS], NT)

    def put(first, second):
        first[:NCO] = m0[...]
        first[NCO : NCO + RHS] = w0[...]
        first[NCO + RHS :] = g1[:8]
        second[:NCO] = m1[...]
        second[NCO : NCO + 8] = g1[8:]
        second[NCO + 8 :] = g2

    on_core(lambda: put(keep, send), lambda: put(send, keep))


def plane0_kernel(keep, got, out):
    for p in range(16):
        rows = slice(16 * p, 16 * p + 16)
        pieces = [keep[rows] + got[rows]]
        if p < 12:
            rows = slice(NCO + 2 * p, NCO + 2 * p + 2)
            pieces += [*high_low(keep[rows] + got[rows]), jnp.zeros((4, NCO), F32)]
        else:
            pieces += [jnp.zeros((8, NCO), F32)]
        out[p] = jnp.concatenate(pieces, axis=0).astype(BF16)


def summed(got):
    total = got[0].astype(F32)
    for p in range(1, got.shape[0]):
        total = total + got[p].astype(F32)
    return total


def depth0_kernel(got, own_row, out):
    total = summed(got)
    g = total[16:18] + total[18:20]
    rows = [total[:16], *high_low(g), *high_low(own_row[:1]), jnp.zeros((2, NCO), F32)]
    value = jnp.concatenate(rows, axis=0).astype(BF16)
    for q in range(8):
        out[q] = value


def spread0_kernel(got, out):
    every = [got[q].astype(F32) for q in range(8)]
    total = functools.reduce(jnp.add, every)
    g = total[16:18] + total[18:20]
    rows = [total[:16], *high_low(g), jnp.zeros((4, NCO), F32)]
    rows += [r[20:21] for r in every] + [r[21:22] for r in every]
    value = jnp.concatenate(rows, axis=0).astype(BF16)
    for p in range(16):
        out[p] = value


def collect0_kernel(got, out):
    g = []
    for p in range(16):
        out[16 * p : 16 * p + 16] = got[p, :16]
        g.append(got[p, 16:24].astype(F32))
        out[320 + 8 * p : 328 + 8 * p] = got[p, 24:32]
        out[448 + 8 * p : 456 + 8 * p] = got[p, 32:40]
    out[256:320] = jnp.concatenate([r[:2] for r in g] + [r[2:4] for r in g], axis=0).astype(BF16)


def terms_in(coef, width):
    return coef[0:1, :width], coef[1:2, :width], coef[2:3, :width]


def block1_kernel(
    own, got, base1, coef, spread, wide_in, inverse, coarse, w0, z0, load1, image1, s0, s1, s2, s3,
):
    _, inv, _ = terms_in(coef, WIDTH)

    def put(first, second):
        for half, part in ((slice(0, 128), first), (slice(128, 256), second)):
            coarse[half] = part[320:448].astype(F32) + part[448:576].astype(F32)
        w0[...] = first[256:272].astype(F32) + first[288:304].astype(F32)

    on_core(lambda: put(own, got), lambda: put(got, own))
    z = hdot(w0[...], coarse[...])
    z0[...] = z
    load1[...] = base1[...] + inv * lifted(z, wide_in[...], spread[:, :SLOTS])
    put_image(bdot(load1[...].astype(BF16), inverse[...]), image1, (s0, s1, s2, s3))


def solve_kernel(coef, own, got, z0, w0, coarse, spread, wide_in, w1, w2, lift1, lift2, m0, m1, g1, g2):
    centre, inv, alpha = terms_in(coef, NCO)

    def put(first, second):
        m0[...] = first[:NCO]
        m1[...] = second[:NCO]
        left = first[272:288].astype(F32) + first[304:320].astype(F32)
        right = second[256:288].astype(F32) + second[288:320].astype(F32)
        g1[:8] = left[:8]
        g1[8:] = right[:8]
        g2[...] = right[8:24]

    on_core(lambda: put(own, got), lambda: put(got, own))
    z, w = z0[...], w0[...]
    after = (g1[...] + dot3(z, m0[...]) - centre * w) * inv
    w1[...] = after
    z1 = hdot(after, coarse[...])
    image = (g2[...] + dot3(z, m1[...]) - centre * g1[...]) * inv
    last = alpha * (image + dot3(z1, m0[...]) - centre * after) - w
    w2[...] = last
    z2 = hdot(last, coarse[...])
    lift = lifted(jnp.concatenate([z1, z2], axis=0), wide_in[...], spread[:, :SLOTS])
    lift1[...] = lift[:RHS]
    lift2[...] = lift[RHS:]


def next_kernel(
    coef, lift, n0, n1, n2, n3, image, before, now, inverse, load, image_out, s0, s1, s2, s3,
):
    centre, _, alpha = terms_in(coef, FACE)
    for s, jump in zip(SEG, jumped(image, (n0, n1, n2, n3)), strict=True):
        load[:, s] = alpha * (jump + lift[:, s] - centre * now[:, s]) - before[:, s]
    put_image(bdot(load[...].astype(BF16), inverse[...]), image_out, (s0, s1, s2, s3))


def last_kernel(
    coef, lift, n0, n1, n2, n3, image, before, now, inverse, load, image_out, low_sub, low_grp,
):
    centre, _, alpha = terms_in(coef, FACE)
    for s, jump in zip(SEG, jumped(image, (n0, n1, n2, n3)), strict=True):
        load[:, s] = alpha * (jump + lift[:, s] - centre * now[:, s]) - before[:, s]
    u = bdot(load[...].astype(BF16), inverse[...])
    image_out[...] = u
    low_sub[...] = u[:, SEG[1]]
    low_grp[...] = u[:, SEG[3]]


def terms_kernel(coef, block, load1, load2, load3, image, spread, wide_in, w3, g3, stack, early, partial4):
    centre, _, alpha = terms_in(coef, FACE)
    w, g = terms_of(load3[...], image[...], wide_in[...], spread[:, :SLOTS])
    w3[...] = w
    g3[...] = g
    left, right = slice(0, FACE), slice(FACE, 2 * FACE)
    stack[:RHS] = block[...]
    for level, load in ((1, load1), (2, load2), (3, load3)):
        stack[level * RHS : (level + 1) * RHS, left] = load[:, SEG[0]]
        stack[level * RHS : (level + 1) * RHS, right] = load[:, SEG[2]]
    for half, s in ((left, SEG[0]), (right, SEG[2])):
        partial4[:, half] = alpha * (image[:, s] - centre * load3[:, s]) - load2[:, s]
    known = jnp.concatenate([stack[...], jnp.zeros((64, 2 * FACE), F32)], axis=0)
    early[...] = jnp.concatenate([hdot(stack[...], known, NT), jnp.zeros((RHS, 128), F32)], axis=0)


def gram_kernel(coef, stack, early, partial4, n0, n2, w3, g3, known4, keep, send):
    _, _, alpha = terms_in(coef, FACE)
    known4[:, :FACE] = partial4[:, :FACE] - alpha * n0[...]
    known4[:, FACE:] = partial4[:, FACE:] - alpha * n2[...]
    q = known4[...]
    column = jnp.concatenate([jnp.zeros((64, 2 * FACE), F32), q, jnp.zeros((48, 2 * FACE), F32)], axis=0)
    terms = early[...] + hdot(jnp.concatenate([stack[...], q], axis=0), column, NT)
    t = [terms[i * RHS : (i + 1) * RHS] for i in range(BLOCKS)]
    lane = lax.broadcasted_iota(jnp.int32, (RHS, 128), 1)
    first = jnp.where(lane < 80, t[0], pltpu.roll(t[2], 48, 1))
    second = jnp.where(lane < 64, pltpu.roll(t[1], 112, 1), pltpu.roll(t[3], 16, 1))
    second = jnp.where(lane < 96, second, pltpu.roll(t[4], 32, 1))
    packed = jnp.concatenate([first, second], axis=1)
    split_by_core(
        jnp.concatenate([w3[...], jnp.zeros((RHS, NCO), F32)], axis=0),
        jnp.concatenate([g3[...], packed], axis=0),
        keep,
        send,
    )


def coded(total):
    zero = lax.axis_index("core") == 0
    return jnp.where(zero, jnp.concatenate(high_low(total[:RHS]), axis=0), total).astype(BF16)


def decoded(total):
    zero = lax.axis_index("core") == 0
    whole = jnp.concatenate([total[:RHS] + total[RHS:], jnp.zeros((RHS, NCO), F32)], axis=0)
    return jnp.where(zero, whole, total)


def plane1_kernel(keep, got, out):
    value = coded(keep[...] + got[...])
    for p in range(16):
        out[p] = value


def depth1_kernel(got, out):
    value = coded(decoded(summed(got)))
    for q in range(8):
        out[q] = value


def sum_kernel(got, out):
    out[...] = decoded(summed(got))


def store_kernel(stack, basis_hbm, basis, sem):
    for level in range(BLOCKS - 1):
        basis[level] = stack[level * RHS : (level + 1) * RHS].reshape(RHS, 1, 1, 2 * FACE)
    copy = pltpu.make_async_copy(basis, basis_hbm.at[: BLOCKS - 1], sem)
    copy.start()
    copy.wait()


def final_kernel(
    coef, own, got, coarse, matrix, w0, w1, w2, known4, spread, wide_in, stored,
    basis_hbm, gram_hbm, block4, gram, square, sems,
):
    centre, _, alpha = terms_in(coef, NCO)
    zero = lax.axis_index("core") == 0
    w3 = jnp.where(zero, own[:RHS], got[:RHS])
    second = jnp.where(zero, got[...], own[...])
    g3, packed = second[:RHS], second[RHS:]
    z3 = hdot(w3, coarse[...])
    lift = lifted(z3, wide_in[...], spread[:, :SLOTS])
    value = jnp.concatenate(
        [known4[:, :FACE] + alpha * lift[:, SEG[0]], known4[:, FACE:] + alpha * lift[:, SEG[2]]], axis=1
    )
    block4[...] = value.reshape(RHS, 1, 1, 2 * FACE)
    late = pltpu.make_async_copy(block4, basis_hbm.at[BLOCKS - 1], sems.at[0])
    late.start()
    wk = alpha * (g3 - centre * w3) - w2[...]
    z_row = jnp.concatenate([jnp.zeros((64, NCO), F32), z3, jnp.zeros((48, NCO), F32)], axis=0)
    rows = jnp.concatenate([w0[...], w1[...], w2[...], w3, wk, dot3(z3, matrix[...])], axis=0)
    cross = hdot(rows, z_row, NT)
    alpha = alpha[:, :128]
    h0, h1 = packed[:, :128], packed[:, 128:]
    parts = [h0, pltpu.roll(h1, 16, 1), pltpu.roll(h0, 80, 1), pltpu.roll(h1, 112, 1), pltpu.roll(h1, 96, 1)]
    square[...] = jnp.zeros((128, 128), F32)
    for i in range(BLOCKS):
        square[i * RHS : (i + 1) * RHS] = parts[i] + alpha * cross[i * RHS : (i + 1) * RHS]
    last = slice(4 * RHS, 5 * RHS)
    square[last] = square[last] + alpha * alpha * cross[5 * RHS :]
    sided = jnp.concatenate([jnp.zeros((64, 128), F32), alpha * cross[last], jnp.zeros((48, 128), F32)], axis=0)
    up = square[...]
    r = lax.broadcasted_iota(jnp.int32, (128, 128), 0) // RHS
    c = lax.broadcasted_iota(jnp.int32, (128, 128), 1) // RHS
    whole = jnp.where(r <= c, up, up.T) + jnp.where(jnp.logical_and(r == 4, c == 4), sided.T, 0.0)
    gram[...] = (whole * (1.0 / (2 * FACE * 64)))[: BLOCKS * RHS, : BLOCKS * RHS]
    result = pltpu.make_async_copy(gram, gram_hbm, sems.at[1])
    result.start()
    late.wait()
    result.wait()


def body(residual, bounds, local_inverse, corner_basis, corner_map, coarse_inverse):
    inverse = local_inverse.reshape(WIDTH, WIDTH)
    corners = corner_basis.reshape(-1, WIDTH)
    count = corners.shape[0]
    face = ((RHS, FACE), F32)
    load = ((RHS, WIDTH), F32)
    small = ((RHS, NCO), F32)
    half = ((RHS, 2 * FACE), F32)
    square = ((NCO, NCO), F32)
    blocks = ((BLOCKS, RHS, 1, 1, 2 * FACE), F32)
    smem, hbm = pltpu.SMEM, pltpu.HBM

    *packs, labels, block, corners = call(
        pack_kernel,
        [((64, FACE), BF16)] * 4 + [((1, 256), jnp.int32), half, ((count, WIDTH), BF16)],
        [residual, corners, corner_map.reshape(1, count)],
        [hbm] * 3,
        [pltpu.VMEM((RHS, 1, 1, 2 * FACE), F32), pltpu.VMEM((1, count), jnp.int32), pltpu.VMEM((4, 64, FACE), BF16),
         pltpu.SemaphoreType.DMA((3,))],
    )
    near = neighbours(packs)
    load0, wide, spread, image0, *sends = call(
        start_kernel,
        [load, ((SLOTS, WIDTH), BF16), ((NCO, 256), BF16), load, face, face, face, face],
        [block, *near, corners, labels, inverse],
    )
    near0 = neighbours(sends)
    coef, own_row, m0, m1, w0, g1 = call(
        moment_kernel,
        [((8, WIDTH), F32), ((8, NCO), F32), square, square, small, small],
        [bounds, coarse_inverse, load0, image0, wide, spread, inverse],
        [smem] + [None] * 6,
    )
    base1, keep, send = call(
        join_kernel,
        [load, ((280, NCO), F32), ((280, NCO), F32)],
        [coef, load0, *near0, image0, wide, spread, inverse, m0, m1, w0, g1],
    )
    (v,) = call(plane0_kernel, [((16, 24, NCO), BF16)], [keep, swapped(send)])
    (v,) = call(depth0_kernel, [((8, 24, NCO), BF16)], [exchange(v, PLANE), own_row])
    (v,) = call(spread0_kernel, [((16, 40, NCO), BF16)], [exchange(v, "z")])
    (own,) = call(collect0_kernel, [((576, NCO), BF16)], [exchange(v, PLANE)])

    got = swapped(own)
    coarse, w0, z0, load1, image1, *sends = call(
        block1_kernel,
        [square, small, small, load, load, face, face, face, face],
        [own, got, base1, coef, spread, wide, inverse],
    )
    near1 = neighbours(sends)
    w1, w2, lift1, lift2, m0 = call(
        solve_kernel,
        [small, small, load, load, ((NCO, NCO), BF16)],
        [coef, own, got, z0, w0, coarse, spread, wide],
        scratch=[pltpu.VMEM((NCO, NCO), BF16), pltpu.VMEM((RHS, NCO), F32), pltpu.VMEM((RHS, NCO), F32)],
    )
    load2, image2, *sends = call(
        next_kernel,
        [load, load, face, face, face, face],
        [coef, lift1, *near1, image1, load0, load1, inverse],
    )
    near2 = neighbours(sends)
    load3, image3, low_sub, low_grp = call(
        last_kernel,
        [load, load, face, face],
        [coef, lift2, *near2, image2, load1, load2, inverse],
    )
    n0, n2 = along(low_sub, SUB, -1), along(low_grp, "x", -1)
    w3, g3, stack, early, partial4 = call(
        terms_kernel,
        [small, small, ((4 * RHS, 2 * FACE), F32), ((BLOCKS * RHS, 128), F32), half],
        [coef, block, load1, load2, load3, image3, spread, wide],
    )
    known4, keep, send = call(
        gram_kernel,
        [half, ((32, NCO), F32), ((32, NCO), F32)],
        [coef, stack, early, partial4, n0, n2, w3, g3],
    )
    (stored,) = call(
        store_kernel,
        [blocks],
        [stack],
        scratch=[pltpu.VMEM((BLOCKS - 1, RHS, 1, 1, 2 * FACE), F32), pltpu.SemaphoreType.DMA(())],
        out_space=hbm,
    )
    (v,) = call(plane1_kernel, [((16, 32, NCO), BF16)], [keep, swapped(send)])
    (v,) = call(depth1_kernel, [((8, 32, NCO), BF16)], [exchange(v, PLANE)])
    (own,) = call(sum_kernel, [((32, NCO), F32)], [exchange(v, "z")])
    basis, gram = call(
        final_kernel,
        [blocks, ((BLOCKS * RHS, BLOCKS * RHS), F32)],
        [coef, own, swapped(own), coarse, m0, w0, w1, w2, known4, spread, wide, stored],
        [None] * 11 + [hbm],
        [pltpu.VMEM((RHS, 1, 1, 2 * FACE), F32), pltpu.VMEM((BLOCKS * RHS, BLOCKS * RHS), F32),
         pltpu.VMEM((128, 128), F32), pltpu.SemaphoreType.DMA((2,))],
        out_space=hbm,
        aliases={11: 0},
    )
    return basis, gram


def solution(mesh):
    split = Mesh(mesh.devices.reshape(8, 4, 2, mesh.shape["grp"]), ("z", "y", "core", "x"))
    in_specs = (
        P(None, SUB, "x", None),
        P(),
        P(SUB, "x", None, None),
        P(SUB, "x", None, None),
        P(SUB, "x", None),
        P(("z", "y", "core", "x"), None),
    )
    out_specs = (P(None, None, SUB, "x", None), P())
    return jax.shard_map(body, mesh=split, in_specs=in_specs, out_specs=out_specs, check_vma=False)
```

```python
import functools

import jax
import jax.numpy as jnp
from jax import lax
from jax.experimental import pallas as pl
from jax.experimental.pallas import tpu as pltpu
from jax.sharding import Mesh
from jax.sharding import PartitionSpec as P


BLOCKS = 5
RHS = 16
FACE = 256
WIDTH = 4 * FACE
NCO = 256
SLOT = 32
SLOTS = 5 * SLOT
SUB = ("z", "y", "core")
PLANE = ("y", "x")
HIGH = lax.Precision.HIGHEST
F32, BF16 = jnp.float32, jnp.bfloat16
SEG = [slice(i * FACE, (i + 1) * FACE) for i in range(4)]


NN = (((1,), (0,)), ((), ()))
NT = (((1,), (1,)), ((), ()))


def hdot(a, b, dims=NN):
    return lax.dot_general(a, b, dims, precision=HIGH, preferred_element_type=F32)


def bdot(a, b, dims=NN):
    return lax.dot_general(a, b, dims, preferred_element_type=F32)


def dot2(a, exact, dims=NN):
    rows = a.shape[0]
    top = a.astype(BF16)
    low = (a - top.astype(F32)).astype(BF16)
    got = bdot(jnp.concatenate([top, low], axis=0), exact, dims)
    return got[:rows] + got[rows:]


def call(kernel, outs, args, spaces=None, scratch=(), limit=12, out_space=None, aliases=None):
    vmem = pl.BlockSpec(memory_space=pltpu.VMEM)
    out_spec = pl.BlockSpec(memory_space=out_space) if out_space is not None else vmem
    specs = [vmem if s is None else pl.BlockSpec(memory_space=s) for s in (spaces or [None] * len(args))]
    if spaces:
        args = [
            pltpu.with_memory_space_constraint(a, pltpu.HBM) if s is pltpu.HBM else a for a, s in zip(args, spaces)
        ]
    run = pl.pallas_call(
        kernel,
        out_shape=[jax.ShapeDtypeStruct(s, d) for s, d in outs],
        in_specs=specs,
        out_specs=[out_spec] * len(outs),
        scratch_shapes=list(scratch),
        input_output_aliases=aliases or {},
        compiler_params=pltpu.CompilerParams(vmem_limit_bytes=limit << 20),
    )
    return run(*args)


def along(x, axis, by):
    count = lax.axis_size(axis)
    return lax.ppermute(x, axis, [(i, (i + by) % count) for i in range(count)])


def exchange(x, axis):
    return lax.all_to_all(x, axis, split_axis=0, concat_axis=0, tiled=True)


def swapped(v):
    return along(v, "core", 1)


def in_pairs(v, axis, first):
    count = lax.axis_size(axis)
    pairs = []
    for i in range(first, first + count, 2):
        a, b = i % count, (i + 1) % count
        pairs += [(a, b), (b, a)]
    return lax.ppermute(v, axis, pairs)


def neighbours(sends):
    return [in_pairs(sends[0], SUB, 1), in_pairs(sends[1], "x", 1), in_pairs(sends[2], "x", 0), swapped(sends[3])]


def label_of(n):
    return ((n // 4) % 2) * 128 + ((n // 8) % 4 * 4 + n % 4) * 8 + n // 32


def pack_kernel(
    block_hbm, corners_hbm, ids_hbm,
    s0, s1, s2, s3, labels, block, corners, wide_block, given, packs, sems,
):
    copies = [
        pltpu.make_async_copy(src, dst, sems.at[i])
        for i, (src, dst) in enumerate(
            ((block_hbm, wide_block), (corners_hbm, corners), (ids_hbm, given))
        )
    ]
    for copy in copies:
        copy.start()
    for copy in copies:
        copy.wait()
    count = corners.shape[0]
    labels[...] = jnp.full((1, 256), -1, jnp.int32)
    labels[:, :count] = label_of(given[...])
    text = labels[...].astype(F32).astype(BF16)
    x = wide_block[...].reshape(RHS, 2 * FACE)
    block[...] = x
    top = x.astype(BF16)
    rest = (x - top.astype(F32)).astype(BF16)
    for i, s in enumerate(SEG):
        if i % 2 == 0:
            packs[i, :RHS] = top[:, SEG[i // 2]]
            packs[i, RHS : 2 * RHS] = rest[:, SEG[i // 2]]
        else:
            packs[i, : 2 * RHS] = jnp.zeros((2 * RHS, FACE), BF16)
        packs[i, 2 * RHS : 2 * RHS + count] = corners[:, s]
        packs[i, 2 * RHS + count :] = jnp.broadcast_to(text, (8, FACE))
    put_sends([packs[i] for i in range(4)], (s0, s1, s2, s3))


def terms_of(load, u, wide, spread_t):
    both = dot2(dot2(jnp.concatenate([load * 0.5, u], axis=0), wide, NT), spread_t, NT)
    return both[:RHS], both[RHS:]


def lifted(z, wide, spread_t):
    return dot2(dot2(z, spread_t), wide)


def either(axis, even_branch, odd_branch):
    even = lax.axis_index(axis) % 2 == 0
    pl.when(even)(even_branch)
    pl.when(jnp.logical_not(even))(odd_branch)


def on_core(zero_branch, other_branch):
    either("core", zero_branch, other_branch)


def put_pair(axis, up, low, first, second):
    def even():
        first[...] = up
        second[...] = low

    def odd():
        first[...] = low
        second[...] = up

    either(axis, even, odd)


def put_sends(faces, outs):
    put_pair("core", faces[0], faces[1], outs[3], outs[0])
    put_pair("x", faces[2], faces[3], outs[2], outs[1])


def put_image(u, out, sends):
    out[...] = u
    put_sends([u[:, s] for s in SEG], sends)


def arrived(refs):
    values = [r[...] for r in refs]
    if values[0].dtype != F32:
        values = [v.astype(F32) for v in values]
    zero, even = lax.axis_index("core") == 0, lax.axis_index("x") % 2 == 0
    return [
        jnp.where(zero, values[3], values[0]),
        jnp.where(zero, values[0], values[3]),
        jnp.where(even, values[2], values[1]),
        jnp.where(even, values[1], values[2]),
    ]


def split_by_core(first, second, keep, send):
    def zero():
        keep[...] = first
        send[...] = second

    def one():
        keep[...] = second
        send[...] = first

    on_core(zero, one)


def high_low(x):
    top = x.astype(BF16).astype(F32)
    return top, x - top


def start_kernel(
    block, r0, r1, r2, r3, corners, labels, inverse, load_out, wide_out, spread_out, image, s0, s1, s2, s3,
):
    count = corners.shape[0]
    k = 2 * RHS
    next_sub, prev_sub, next_grp, prev_grp = arrived((r0, r1, r2, r3))
    load_out[:, SEG[0]] = block[:, :FACE]
    load_out[:, SEG[1]] = -(prev_sub[:RHS] + prev_sub[RHS:k])
    load_out[:, SEG[2]] = block[:, FACE:]
    load_out[:, SEG[3]] = -(prev_grp[:RHS] + prev_grp[RHS:k])
    put_image(bdot(load_out[...].astype(BF16), inverse[...]), image, (s0, s1, s2, s3))
    wide_out[...] = jnp.zeros((SLOTS, WIDTH), BF16)
    wide_out[:count] = corners[...]
    others = (next_sub, prev_sub, next_grp, prev_grp)
    for i, other in enumerate(others):
        wide_out[SLOT * (i + 1) : SLOT * (i + 1) + count, SEG[i]] = (-other[k : k + count]).astype(BF16)
    lane = lax.broadcasted_iota(jnp.int32, (8, 256), 1)
    ids = jnp.where(lane < SLOT, jnp.broadcast_to(labels[...], (8, 256)).astype(F32), -1.0)
    for i, other in enumerate(others):
        moved = pltpu.roll(other[k + count :], SLOT * (i + 1), 1)
        mine = jnp.logical_and(lane >= SLOT * (i + 1), lane < SLOT * (i + 2))
        ids = jnp.where(mine, moved, ids)
    number = lax.broadcasted_iota(jnp.int32, (NCO, 256), 0).astype(F32)
    spread_out[...] = (number == ids[:1]).astype(F32).astype(BF16)


def row_kernel(bounds, row_hbm, coef, own_row, row, sem):
    copy = pltpu.make_async_copy(row_hbm, row, sem)
    copy.start()
    low, high = bounds[0], bounds[1]
    centre = jnp.full((1, WIDTH), (low + high) * 0.5, F32)
    inv = 1.0 / jnp.full((1, WIDTH), (high - low) * 0.5, F32)
    coef[...] = jnp.concatenate([centre, inv, 2.0 * inv, jnp.zeros((5, WIDTH), F32)], axis=0)
    n = lax.broadcasted_iota(jnp.int32, (NCO, NCO), 0)
    m = lax.broadcasted_iota(jnp.int32, (NCO, NCO), 1)
    order = (label_of(n) == m).astype(F32).astype(BF16)
    copy.wait()
    own_row[...] = dot2(jnp.broadcast_to(row[...], (RHS, NCO)), order)[:8]


def fetch_kernel(inverse_hbm, out, sem):
    copy = pltpu.make_async_copy(inverse_hbm, out, sem)
    copy.start()
    copy.wait()


def moment_kernel(load0, image, wide_in, spread, inverse, keep, send):
    wide, spread_t = wide_in[...], spread[:, :SLOTS]
    pairs0 = bdot(wide, wide, NT) * 0.5
    pairs1 = dot2(bdot(wide, inverse[...]), wide, NT)
    half = dot2(jnp.concatenate([pairs0, pairs1], axis=0), spread_t, NT)
    half = jnp.concatenate([half[:SLOTS], half[SLOTS:]], axis=1)
    top = half.astype(BF16)
    low = (half - top.astype(F32)).astype(BF16)
    both = bdot(spread_t, jnp.concatenate([top, low], axis=1))
    both = both[:, : 2 * NCO] + both[:, 2 * NCO :]
    w, g = terms_of(load0[...], image[...], wide, spread_t)

    def put(first, second):
        first[:NCO] = both[:, :NCO]
        first[NCO:] = w
        second[:NCO] = both[:, NCO:]
        second[NCO:] = g

    on_core(lambda: put(keep, send), lambda: put(send, keep))


def jumped(image, near):
    return [image[:, s] - n for s, n in zip(SEG, arrived(near), strict=True)]


def join_kernel(coef, load0, n0, n1, n2, n3, image, wide_in, spread, inverse, base1, g2):
    centre, inv, _ = terms_in(coef, WIDTH)
    jump = jnp.concatenate(jumped(image, (n0, n1, n2, n3)), axis=1)
    base1[...] = (jump - centre * load0[...]) * inv
    u = dot2(jump, inverse[...])
    g2[...] = dot2(dot2(u, wide_in[...], NT), spread[:, :SLOTS], NT)


def plane0_kernel(keep, got, g2, out):
    pieces = [high_low(keep[NCO:] + got[NCO:]), high_low(g2[...])]
    zero = jnp.zeros((4, NCO), F32)
    for p in range(16):
        rows = slice(16 * p, 16 * p + 16)
        small = [piece[part][p : p + 1] for part in range(2) for piece in pieces]
        out[p] = jnp.concatenate([keep[rows] + got[rows], *small, zero], axis=0).astype(BF16)


def summed(got):
    total = got[0].astype(F32)
    for p in range(1, got.shape[0]):
        total = total + got[p].astype(F32)
    return total


def depth0_kernel(got, own_row, out):
    total = summed(got)
    g = total[16:18] + total[18:20]
    rows = [total[:16], *high_low(g), *high_low(own_row[:1]), jnp.zeros((2, NCO), F32)]
    value = jnp.concatenate(rows, axis=0).astype(BF16)
    for q in range(8):
        out[q] = value


def spread0_kernel(got, out):
    every = [got[q].astype(F32) for q in range(8)]
    total = functools.reduce(jnp.add, every)
    g = total[16:18] + total[18:20]
    rows = [total[:16], *high_low(g), jnp.zeros((4, NCO), F32)]
    rows += [r[20:21] for r in every] + [r[21:22] for r in every]
    value = jnp.concatenate(rows, axis=0).astype(BF16)
    for p in range(16):
        out[p] = value


def collect0_kernel(got, out):
    g = []
    for p in range(16):
        out[16 * p : 16 * p + 16] = got[p, :16]
        g.append(got[p, 16:24].astype(F32))
        out[320 + 8 * p : 328 + 8 * p] = got[p, 24:32]
        out[448 + 8 * p : 456 + 8 * p] = got[p, 32:40]
    out[256:320] = jnp.concatenate([r[i : i + 1] for i in range(4) for r in g], axis=0).astype(BF16)


def terms_in(coef, width):
    return coef[0:1, :width], coef[1:2, :width], coef[2:3, :width]


def block1_kernel(
    own, got, base1, coef, spread, wide_in, inverse, coarse, w0, z0, load1, image1, s0, s1, s2, s3,
):
    _, inv, _ = terms_in(coef, WIDTH)

    def put(first, second):
        for half, part in ((slice(0, 128), first), (slice(128, 256), second)):
            coarse[half] = part[320:448].astype(F32) + part[448:576].astype(F32)
        w0[...] = first[256:272].astype(F32) + first[288:304].astype(F32)

    on_core(lambda: put(own, got), lambda: put(got, own))
    z = hdot(w0[...], coarse[...])
    z0[...] = z
    load1[...] = base1[...] + inv * lifted(z, wide_in[...], spread[:, :SLOTS])
    put_image(bdot(load1[...].astype(BF16), inverse[...]), image1, (s0, s1, s2, s3))


def solve_kernel(coef, own, got, z0, w0, coarse, spread, wide_in, w1, w2, lift1, lift2, m0, m1, g1, g2):
    centre, inv, alpha = terms_in(coef, NCO)

    def put(first, second):
        m0[...] = first[:NCO]
        m1[...] = second[:NCO]
        g1[...] = second[256:272].astype(F32) + second[288:304].astype(F32)
        parts = [part[i : i + RHS].astype(F32) for part in (first, second) for i in (272, 304)]
        g2[...] = functools.reduce(jnp.add, parts)

    on_core(lambda: put(own, got), lambda: put(got, own))
    z, w = z0[...], w0[...]
    after = (g1[...] + dot2(z, m0[...]) - centre * w) * inv
    w1[...] = after
    z1 = hdot(after, coarse[...])
    image = (g2[...] + dot2(z, m1[...]) - centre * g1[...]) * inv
    last = alpha * (image + dot2(z1, m0[...]) - centre * after) - w
    w2[...] = last
    z2 = hdot(last, coarse[...])
    lift = lifted(jnp.concatenate([z1, z2], axis=0), wide_in[...], spread[:, :SLOTS])
    lift1[...] = lift[:RHS]
    lift2[...] = lift[RHS:]


def next_kernel(
    coef, lift, n0, n1, n2, n3, image, before, now, inverse, load, image_out, s0, s1, s2, s3,
):
    centre, _, alpha = terms_in(coef, FACE)
    for s, jump in zip(SEG, jumped(image, (n0, n1, n2, n3)), strict=True):
        load[:, s] = alpha * (jump + lift[:, s] - centre * now[:, s]) - before[:, s]
    put_image(bdot(load[...].astype(BF16), inverse[...]), image_out, (s0, s1, s2, s3))


def last_kernel(
    coef, lift, n0, n1, n2, n3, image, before, now, inverse, load, image_out, low_sub, low_grp,
):
    centre, _, alpha = terms_in(coef, FACE)
    for s, jump in zip(SEG, jumped(image, (n0, n1, n2, n3)), strict=True):
        load[:, s] = alpha * (jump + lift[:, s] - centre * now[:, s]) - before[:, s]
    u = bdot(load[...].astype(BF16), inverse[...])
    image_out[...] = u
    low_sub[...] = u[:, SEG[1]]
    low_grp[...] = u[:, SEG[3]]


def terms_kernel(coef, block, load1, load2, load3, image, spread, wide_in, stack, partial4, keep, send):
    centre, _, alpha = terms_in(coef, FACE)
    w, g = terms_of(load3[...], image[...], wide_in[...], spread[:, :SLOTS])
    left, right = slice(0, FACE), slice(FACE, 2 * FACE)
    stack[:RHS] = block[...]
    for level, load in ((1, load1), (2, load2), (3, load3)):
        stack[level * RHS : (level + 1) * RHS, left] = load[:, SEG[0]]
        stack[level * RHS : (level + 1) * RHS, right] = load[:, SEG[2]]
    for half, s in ((left, SEG[0]), (right, SEG[2])):
        partial4[:, half] = alpha * (image[:, s] - centre * load3[:, s]) - load2[:, s]
    known = jnp.concatenate([stack[...], jnp.zeros((64, 2 * FACE), F32)], axis=0)
    terms = hdot(stack[...], known, NT)
    t = [terms[i * RHS : (i + 1) * RHS] for i in range(BLOCKS - 1)]
    lane = lax.broadcasted_iota(jnp.int32, (RHS, 128), 1)
    first = jnp.where(lane < 64, t[0], pltpu.roll(t[1], 48, 1))
    second = jnp.where(lane < 32, pltpu.roll(t[2], 96, 1), pltpu.roll(t[3], 112, 1))
    split_by_core(
        jnp.concatenate([w, jnp.zeros((RHS, NCO), F32)], axis=0),
        jnp.concatenate([g, jnp.concatenate([first, second], axis=1)], axis=0),
        keep,
        send,
    )


def coded(total):
    zero = lax.axis_index("core") == 0
    return jnp.where(zero, jnp.concatenate(high_low(total[:RHS]), axis=0), total)


def decoded(total):
    zero = lax.axis_index("core") == 0
    whole = jnp.concatenate([total[:RHS] + total[RHS:], jnp.zeros((RHS, NCO), F32)], axis=0)
    return jnp.where(zero, whole, total)


def gram_kernel(coef, stack, partial4, n0, n2, keep, got, known4, out):
    _, _, alpha = terms_in(coef, FACE)
    known4[:, :FACE] = partial4[:, :FACE] - alpha * n0[...]
    known4[:, FACE:] = partial4[:, FACE:] - alpha * n2[...]
    q = known4[...]
    row = hdot(q, jnp.concatenate([stack[...], q, jnp.zeros((48, 2 * FACE), F32)], axis=0), NT)
    row = jnp.concatenate([row[:8], row[8:]], axis=1)
    value = jnp.concatenate([coded(keep[...] + got[...]), row], axis=0).astype(BF16)
    for p in range(16):
        out[p] = value


def depth1_kernel(got, out):
    total = summed(got)
    value = jnp.concatenate([coded(decoded(total[: 2 * RHS])), total[2 * RHS :]], axis=0).astype(BF16)
    for q in range(8):
        out[q] = value


def sum_kernel(got, out):
    total = summed(got)
    out[: 2 * RHS] = decoded(total[: 2 * RHS])
    out[2 * RHS :] = total[2 * RHS :]


def store_kernel(stack, basis_hbm, basis, sem):
    for level in range(BLOCKS - 1):
        basis[level] = stack[level * RHS : (level + 1) * RHS].reshape(RHS, 1, 1, 2 * FACE)
    copy = pltpu.make_async_copy(basis, basis_hbm.at[: BLOCKS - 1], sem)
    copy.start()
    copy.wait()


def final_kernel(
    coef, own, got, coarse, matrix, w0, w1, w2, known4, spread, wide_in, stored,
    basis_hbm, gram_hbm, block4, gram, square, sems,
):
    centre, _, alpha = terms_in(coef, NCO)
    zero = lax.axis_index("core") == 0
    w3 = jnp.where(zero, own[:RHS], got[:RHS])
    second = jnp.where(zero, got[: 2 * RHS], own[: 2 * RHS])
    g3, packed = second[:RHS], second[RHS:]
    row = own[2 * RHS :] + got[2 * RHS :]
    row = jnp.concatenate([row[:, :128], row[:, 128:]], axis=0)
    z3 = hdot(w3, coarse[...])
    lift = lifted(z3, wide_in[...], spread[:, :SLOTS])
    value = jnp.concatenate(
        [known4[:, :FACE] + alpha * lift[:, SEG[0]], known4[:, FACE:] + alpha * lift[:, SEG[2]]], axis=1
    )
    block4[...] = value.reshape(RHS, 1, 1, 2 * FACE)
    late = pltpu.make_async_copy(block4, basis_hbm.at[BLOCKS - 1], sems.at[0])
    late.start()
    wk = alpha * (g3 - centre * w3) - w2[...]
    z_row = jnp.concatenate([jnp.zeros((64, NCO), F32), z3, jnp.zeros((48, NCO), F32)], axis=0)
    rows = jnp.concatenate([w0[...], w1[...], w2[...], w3, wk, dot2(z3, matrix[...])], axis=0)
    cross = hdot(rows, z_row, NT)
    alpha = alpha[:, :128]
    h0, h1 = packed[:, :128], packed[:, 128:]
    parts = [h0, pltpu.roll(h0, 80, 1), pltpu.roll(h1, 32, 1), pltpu.roll(h1, 16, 1)]
    lane = lax.broadcasted_iota(jnp.int32, (RHS, 128), 1)
    for i in range(BLOCKS - 1):
        rows = slice(i * RHS, (i + 1) * RHS)
        square[rows] = jnp.where(lane < 64, parts[i], 0.0) + alpha * cross[rows]
    last = slice(4 * RHS, 5 * RHS)
    own4 = alpha * cross[last]
    square[last] = alpha * alpha * cross[5 * RHS :]
    square[5 * RHS :] = jnp.zeros((48, 128), F32)
    column = jnp.concatenate([jnp.zeros((64, 128), F32), row, jnp.zeros((48, 128), F32)], axis=0)
    sided = jnp.concatenate([jnp.zeros((64, 128), F32), own4, jnp.zeros((48, 128), F32)], axis=0)
    up = square[...]
    r = lax.broadcasted_iota(jnp.int32, (128, 128), 0) // RHS
    c = lax.broadcasted_iota(jnp.int32, (128, 128), 1) // RHS
    whole = jnp.where(r <= c, up, up.T) + column + sided + sided.T
    whole = whole + jnp.where(jnp.logical_and(r < 4, c == 4), column.T, 0.0)
    gram[...] = (whole * (1.0 / (2 * FACE * 64)))[: BLOCKS * RHS, : BLOCKS * RHS]
    result = pltpu.make_async_copy(gram, gram_hbm, sems.at[1])
    result.start()
    late.wait()
    result.wait()


def body(residual, bounds, local_inverse, corner_basis, corner_map, coarse_inverse):
    inverse = local_inverse.reshape(WIDTH, WIDTH)
    corners = corner_basis.reshape(-1, WIDTH)
    count = corners.shape[0]
    face = ((RHS, FACE), F32)
    load = ((RHS, WIDTH), F32)
    small = ((RHS, NCO), F32)
    half = ((RHS, 2 * FACE), F32)
    square = ((NCO, NCO), F32)
    blocks = ((BLOCKS, RHS, 1, 1, 2 * FACE), F32)
    smem, hbm = pltpu.SMEM, pltpu.HBM

    *packs, labels, block, corners = call(
        pack_kernel,
        [((64, FACE), BF16)] * 4 + [((1, 256), jnp.int32), half, ((count, WIDTH), BF16)],
        [residual, corners, corner_map.reshape(1, count)],
        [hbm] * 3,
        [pltpu.VMEM((RHS, 1, 1, 2 * FACE), F32), pltpu.VMEM((1, count), jnp.int32), pltpu.VMEM((4, 64, FACE), BF16),
         pltpu.SemaphoreType.DMA((3,))],
    )
    near = neighbours(packs)
    (inverse,) = call(fetch_kernel, [((WIDTH, WIDTH), BF16)], [inverse], [hbm], [pltpu.SemaphoreType.DMA(())])
    coef, own_row = call(
        row_kernel,
        [((8, WIDTH), F32), ((8, NCO), F32)],
        [bounds, coarse_inverse],
        [smem, hbm],
        [pltpu.VMEM((1, NCO), F32), pltpu.SemaphoreType.DMA(())],
    )
    load0, wide, spread, image0, *sends = call(
        start_kernel,
        [load, ((SLOTS, WIDTH), BF16), ((NCO, 256), BF16), load, face, face, face, face],
        [block, *near, corners, labels, inverse],
    )
    near0 = neighbours(sends)
    keep, send = call(
        moment_kernel,
        [((272, NCO), F32), ((272, NCO), F32)],
        [load0, image0, wide, spread, inverse],
    )
    got = swapped(send)
    base1, g2 = call(join_kernel, [load, small], [coef, load0, *near0, image0, wide, spread, inverse])
    (v,) = call(plane0_kernel, [((16, 24, NCO), BF16)], [keep, got, g2])
    (v,) = call(depth0_kernel, [((8, 24, NCO), BF16)], [exchange(v, PLANE), own_row])
    (v,) = call(spread0_kernel, [((16, 40, NCO), BF16)], [exchange(v, "z")])
    (own,) = call(collect0_kernel, [((576, NCO), BF16)], [exchange(v, PLANE)])

    got = swapped(own)
    coarse, w0, z0, load1, image1, *sends = call(
        block1_kernel,
        [square, small, small, load, load, face, face, face, face],
        [own, got, base1, coef, spread, wide, inverse],
    )
    near1 = neighbours(sends)
    w1, w2, lift1, lift2, m0 = call(
        solve_kernel,
        [small, small, load, load, ((NCO, NCO), BF16)],
        [coef, own, got, z0, w0, coarse, spread, wide],
        scratch=[pltpu.VMEM((NCO, NCO), BF16), pltpu.VMEM((RHS, NCO), F32), pltpu.VMEM((RHS, NCO), F32)],
    )
    load2, image2, *sends = call(
        next_kernel,
        [load, load, face, face, face, face],
        [coef, lift1, *near1, image1, load0, load1, inverse],
    )
    near2 = neighbours(sends)
    load3, image3, low_sub, low_grp = call(
        last_kernel,
        [load, load, face, face],
        [coef, lift2, *near2, image2, load1, load2, inverse],
    )
    n0 = along(low_sub, SUB, -1)
    n2 = along(low_grp, "x", -1)
    stack, partial4, keep, send = call(
        terms_kernel,
        [((4 * RHS, 2 * FACE), F32), half, ((32, NCO), F32), ((32, NCO), F32)],
        [coef, block, load1, load2, load3, image3, spread, wide],
    )
    got = swapped(send)
    known4, v = call(
        gram_kernel,
        [half, ((16, 40, NCO), BF16)],
        [coef, stack, partial4, n0, n2, keep, got],
    )
    (stored,) = call(
        store_kernel,
        [blocks],
        [stack],
        scratch=[pltpu.VMEM((BLOCKS - 1, RHS, 1, 1, 2 * FACE), F32), pltpu.SemaphoreType.DMA(())],
        out_space=hbm,
    )
    (v,) = call(depth1_kernel, [((8, 40, NCO), BF16)], [exchange(v, PLANE)])
    (own,) = call(sum_kernel, [((40, NCO), F32)], [exchange(v, "z")])
    basis, gram = call(
        final_kernel,
        [blocks, ((BLOCKS * RHS, BLOCKS * RHS), F32)],
        [coef, own, swapped(own), coarse, m0, w0, w1, w2, known4, spread, wide, stored],
        [None] * 11 + [hbm],
        [pltpu.VMEM((RHS, 1, 1, 2 * FACE), F32), pltpu.VMEM((BLOCKS * RHS, BLOCKS * RHS), F32),
         pltpu.VMEM((128, 128), F32), pltpu.SemaphoreType.DMA((2,))],
        out_space=hbm,
        aliases={11: 0},
    )
    return basis, gram


def solution(mesh):
    split = Mesh(mesh.devices.reshape(8, 4, 2, mesh.shape["grp"]), ("z", "y", "core", "x"))
    in_specs = (
        P(None, SUB, "x", None),
        P(),
        P(SUB, "x", None, None),
        P(SUB, "x", None, None),
        P(SUB, "x", None),
        P(("z", "y", "core", "x"), None),
    )
    out_specs = (P(None, None, SUB, "x", None), P())
    return jax.shard_map(body, mesh=split, in_specs=in_specs, out_specs=out_specs, check_vma=False)
```

```python
import functools

import jax
import jax.numpy as jnp
from jax import lax
from jax.experimental import pallas as pl
from jax.experimental.pallas import tpu as pltpu
from jax.sharding import Mesh
from jax.sharding import PartitionSpec as P


BLOCKS = 5
RHS = 16
FACE = 256
WIDTH = 4 * FACE
NCO = 256
SLOT = 32
SLOTS = 5 * SLOT
SUB = ("z", "y", "core")
PLANE = ("y", "x")
HIGH = lax.Precision.HIGHEST
F32, BF16 = jnp.float32, jnp.bfloat16
SEG = [slice(i * FACE, (i + 1) * FACE) for i in range(4)]


NN = (((1,), (0,)), ((), ()))
NT = (((1,), (1,)), ((), ()))


def hdot(a, b, dims=NN):
    return lax.dot_general(a, b, dims, precision=HIGH, preferred_element_type=F32)


def bdot(a, b, dims=NN):
    return lax.dot_general(a, b, dims, preferred_element_type=F32)


def dot2(a, exact, dims=NN):
    rows = a.shape[0]
    top = a.astype(BF16)
    low = (a - top.astype(F32)).astype(BF16)
    got = bdot(jnp.concatenate([top, low], axis=0), exact, dims)
    return got[:rows] + got[rows:]


def call(kernel, outs, args, spaces=None, scratch=(), limit=12, out_space=None, aliases=None):
    vmem = pl.BlockSpec(memory_space=pltpu.VMEM)
    out_spec = pl.BlockSpec(memory_space=out_space) if out_space is not None else vmem
    specs = [vmem if s is None else pl.BlockSpec(memory_space=s) for s in (spaces or [None] * len(args))]
    if spaces:
        args = [
            pltpu.with_memory_space_constraint(a, pltpu.HBM) if s is pltpu.HBM else a for a, s in zip(args, spaces)
        ]
    run = pl.pallas_call(
        kernel,
        out_shape=[jax.ShapeDtypeStruct(s, d) for s, d in outs],
        in_specs=specs,
        out_specs=[out_spec] * len(outs),
        scratch_shapes=list(scratch),
        input_output_aliases=aliases or {},
        compiler_params=pltpu.CompilerParams(vmem_limit_bytes=limit << 20),
    )
    return run(*args)


def along(x, axis, by):
    count = lax.axis_size(axis)
    return lax.ppermute(x, axis, [(i, (i + by) % count) for i in range(count)])


def exchange(x, axis):
    return lax.all_to_all(x, axis, split_axis=0, concat_axis=0, tiled=True)


def swapped(v):
    return along(v, "core", 1)


def in_pairs(v, axis, first):
    count = lax.axis_size(axis)
    pairs = []
    for i in range(first, first + count, 2):
        a, b = i % count, (i + 1) % count
        pairs += [(a, b), (b, a)]
    return lax.ppermute(v, axis, pairs)


def neighbours(sends):
    return [in_pairs(sends[0], SUB, 1), in_pairs(sends[1], "x", 1), in_pairs(sends[2], "x", 0), swapped(sends[3])]


def label_of(n):
    return ((n // 4) % 2) * 128 + ((n // 8) % 4 * 4 + n % 4) * 8 + n // 32


def pack_kernel(
    block_hbm, corners_hbm, ids_hbm,
    s0, s1, s2, s3, labels, block, corners, wide_block, given, packs, sems,
):
    copies = [
        pltpu.make_async_copy(src, dst, sems.at[i])
        for i, (src, dst) in enumerate(
            ((block_hbm, wide_block), (corners_hbm, corners), (ids_hbm, given))
        )
    ]
    for copy in copies:
        copy.start()
    for copy in copies:
        copy.wait()
    count = corners.shape[0]
    labels[...] = jnp.full((1, 256), -1, jnp.int32)
    labels[:, :count] = label_of(given[...])
    text = labels[...].astype(F32).astype(BF16)
    x = wide_block[...].reshape(RHS, 2 * FACE)
    block[...] = x
    top = x.astype(BF16)
    rest = (x - top.astype(F32)).astype(BF16)
    for i, s in enumerate(SEG):
        if i % 2 == 0:
            packs[i, :RHS] = top[:, SEG[i // 2]]
            packs[i, RHS : 2 * RHS] = rest[:, SEG[i // 2]]
        else:
            packs[i, : 2 * RHS] = jnp.zeros((2 * RHS, FACE), BF16)
        packs[i, 2 * RHS : 2 * RHS + count] = corners[:, s]
        packs[i, 2 * RHS + count :] = jnp.broadcast_to(text, (8, FACE))
    put_sends([packs[i] for i in range(4)], (s0, s1, s2, s3))


def terms_of(load, u, wide, spread_t):
    both = dot2(dot2(jnp.concatenate([load * 0.5, u], axis=0), wide, NT), spread_t, NT)
    return both[:RHS], both[RHS:]


def lifted(z, wide, spread_t):
    return dot2(dot2(z, spread_t), wide)


def either(axis, even_branch, odd_branch):
    even = lax.axis_index(axis) % 2 == 0
    pl.when(even)(even_branch)
    pl.when(jnp.logical_not(even))(odd_branch)


def on_core(zero_branch, other_branch):
    either("core", zero_branch, other_branch)


def put_pair(axis, up, low, first, second):
    def even():
        first[...] = up
        second[...] = low

    def odd():
        first[...] = low
        second[...] = up

    either(axis, even, odd)


def put_sends(faces, outs):
    put_pair("core", faces[0], faces[1], outs[3], outs[0])
    put_pair("x", faces[2], faces[3], outs[2], outs[1])


def put_image(u, out, sends):
    out[...] = u
    put_sends([u[:, s] for s in SEG], sends)


def arrived(refs):
    values = [r[...] for r in refs]
    if values[0].dtype != F32:
        values = [v.astype(F32) for v in values]
    zero, even = lax.axis_index("core") == 0, lax.axis_index("x") % 2 == 0
    return [
        jnp.where(zero, values[3], values[0]),
        jnp.where(zero, values[0], values[3]),
        jnp.where(even, values[2], values[1]),
        jnp.where(even, values[1], values[2]),
    ]


def split_by_core(first, second, keep, send):
    def zero():
        keep[...] = first
        send[...] = second

    def one():
        keep[...] = second
        send[...] = first

    on_core(zero, one)


def high_low(x):
    top = x.astype(BF16).astype(F32)
    return top, x - top


def start_kernel(
    block, r0, r1, r2, r3, corners, labels, inverse, load_out, wide_out, spread_out, image, s0, s1, s2, s3,
):
    count = corners.shape[0]
    k = 2 * RHS
    next_sub, prev_sub, next_grp, prev_grp = arrived((r0, r1, r2, r3))
    load_out[:, SEG[0]] = block[:, :FACE]
    load_out[:, SEG[1]] = -(prev_sub[:RHS] + prev_sub[RHS:k])
    load_out[:, SEG[2]] = block[:, FACE:]
    load_out[:, SEG[3]] = -(prev_grp[:RHS] + prev_grp[RHS:k])
    put_image(bdot(load_out[...].astype(BF16), inverse[...]), image, (s0, s1, s2, s3))
    wide_out[...] = jnp.zeros((SLOTS, WIDTH), BF16)
    wide_out[:count] = corners[...]
    others = (next_sub, prev_sub, next_grp, prev_grp)
    for i, other in enumerate(others):
        wide_out[SLOT * (i + 1) : SLOT * (i + 1) + count, SEG[i]] = (-other[k : k + count]).astype(BF16)
    lane = lax.broadcasted_iota(jnp.int32, (8, 256), 1)
    ids = jnp.where(lane < SLOT, jnp.broadcast_to(labels[...], (8, 256)).astype(F32), -1.0)
    for i, other in enumerate(others):
        moved = pltpu.roll(other[k + count :], SLOT * (i + 1), 1)
        mine = jnp.logical_and(lane >= SLOT * (i + 1), lane < SLOT * (i + 2))
        ids = jnp.where(mine, moved, ids)
    number = lax.broadcasted_iota(jnp.int32, (NCO, 256), 0).astype(F32)
    spread_out[...] = (number == ids[:1]).astype(F32).astype(BF16)


def fetch_kernel(bounds, inverse_hbm, row_hbm, out, coef, own_row, row, sems):
    fetch = pltpu.make_async_copy(inverse_hbm, out, sems.at[0])
    fetch.start()
    copy = pltpu.make_async_copy(row_hbm, row, sems.at[1])
    copy.start()
    low, high = bounds[0], bounds[1]
    centre = jnp.full((1, WIDTH), (low + high) * 0.5, F32)
    inv = 1.0 / jnp.full((1, WIDTH), (high - low) * 0.5, F32)
    coef[...] = jnp.concatenate([centre, inv, 2.0 * inv, jnp.zeros((5, WIDTH), F32)], axis=0)
    n = lax.broadcasted_iota(jnp.int32, (NCO, NCO), 0)
    m = lax.broadcasted_iota(jnp.int32, (NCO, NCO), 1)
    order = (label_of(n) == m).astype(F32).astype(BF16)
    copy.wait()
    own_row[...] = dot2(jnp.broadcast_to(row[...], (RHS, NCO)), order)[:8]
    fetch.wait()


def moment_kernel(load0, image, wide_in, spread, inverse, keep, send):
    wide, spread_t = wide_in[...], spread[:, :SLOTS]
    pairs0 = bdot(wide, wide, NT) * 0.5
    pairs1 = dot2(bdot(wide, inverse[...]), wide, NT)
    half = dot2(jnp.concatenate([pairs0, pairs1], axis=0), spread_t, NT)
    half = jnp.concatenate([half[:SLOTS], half[SLOTS:]], axis=1)
    top = half.astype(BF16)
    low = (half - top.astype(F32)).astype(BF16)
    both = bdot(spread_t, jnp.concatenate([top, low], axis=1))
    both = both[:, : 2 * NCO] + both[:, 2 * NCO :]
    w, g = terms_of(load0[...], image[...], wide, spread_t)

    def put(first, second):
        first[:NCO] = both[:, :NCO]
        first[NCO:] = w
        second[:NCO] = both[:, NCO:]
        second[NCO:] = g

    on_core(lambda: put(keep, send), lambda: put(send, keep))


def jumped(image, near):
    return [image[:, s] - n for s, n in zip(SEG, arrived(near), strict=True)]


def join_kernel(coef, load0, n0, n1, n2, n3, image, wide_in, spread, inverse, base1, g2):
    centre, inv, _ = terms_in(coef, WIDTH)
    jump = jnp.concatenate(jumped(image, (n0, n1, n2, n3)), axis=1)
    base1[...] = (jump - centre * load0[...]) * inv
    u = dot2(jump, inverse[...])
    g2[...] = dot2(dot2(u, wide_in[...], NT), spread[:, :SLOTS], NT)


def plane0_kernel(keep, got, g2, out):
    pieces = [high_low(keep[NCO:] + got[NCO:]), high_low(g2[...])]
    zero = jnp.zeros((4, NCO), F32)
    for p in range(16):
        rows = slice(16 * p, 16 * p + 16)
        small = [piece[part][p : p + 1] for part in range(2) for piece in pieces]
        out[p] = jnp.concatenate([keep[rows] + got[rows], *small, zero], axis=0).astype(BF16)


def summed(got):
    total = got[0].astype(F32)
    for p in range(1, got.shape[0]):
        total = total + got[p].astype(F32)
    return total


def depth0_kernel(got, own_row, out):
    total = summed(got)
    g = total[16:18] + total[18:20]
    rows = [total[:16], *high_low(g), *high_low(own_row[:1]), jnp.zeros((2, NCO), F32)]
    value = jnp.concatenate(rows, axis=0).astype(BF16)
    for q in range(8):
        out[q] = value


def spread0_kernel(got, out):
    every = [got[q].astype(F32) for q in range(8)]
    total = functools.reduce(jnp.add, every)
    g = total[16:18] + total[18:20]
    rows = [total[:16], *high_low(g), jnp.zeros((4, NCO), F32)]
    rows += [r[20:21] for r in every] + [r[21:22] for r in every]
    value = jnp.concatenate(rows, axis=0).astype(BF16)
    for p in range(16):
        out[p] = value


def collect0_kernel(got, out):
    g = []
    for p in range(16):
        out[16 * p : 16 * p + 16] = got[p, :16]
        g.append(got[p, 16:24].astype(F32))
        out[320 + 8 * p : 328 + 8 * p] = got[p, 24:32]
        out[448 + 8 * p : 456 + 8 * p] = got[p, 32:40]
    out[256:320] = jnp.concatenate([r[i : i + 1] for i in range(4) for r in g], axis=0).astype(BF16)


def terms_in(coef, width):
    return coef[0:1, :width], coef[1:2, :width], coef[2:3, :width]


def block1_kernel(
    own, got, base1, coef, spread, wide_in, inverse, coarse, w0, z0, load1, image1, s0, s1, s2, s3,
):
    _, inv, _ = terms_in(coef, WIDTH)

    def put(first, second):
        for half, part in ((slice(0, 128), first), (slice(128, 256), second)):
            coarse[half] = part[320:448].astype(F32) + part[448:576].astype(F32)
        w0[...] = first[256:272].astype(F32) + first[288:304].astype(F32)

    on_core(lambda: put(own, got), lambda: put(got, own))
    z = hdot(w0[...], coarse[...])
    z0[...] = z
    load1[...] = base1[...] + inv * lifted(z, wide_in[...], spread[:, :SLOTS])
    put_image(bdot(load1[...].astype(BF16), inverse[...]), image1, (s0, s1, s2, s3))


def solve_kernel(coef, own, got, z0, w0, coarse, spread, wide_in, w1, w2, lift1, lift2, m0, m1, g1, g2):
    centre, inv, alpha = terms_in(coef, NCO)

    def put(first, second):
        m0[...] = first[:NCO]
        m1[...] = second[:NCO]
        g1[...] = second[256:272].astype(F32) + second[288:304].astype(F32)
        parts = [part[i : i + RHS].astype(F32) for part in (first, second) for i in (272, 304)]
        g2[...] = functools.reduce(jnp.add, parts)

    on_core(lambda: put(own, got), lambda: put(got, own))
    z, w = z0[...], w0[...]
    after = (g1[...] + dot2(z, m0[...]) - centre * w) * inv
    w1[...] = after
    z1 = hdot(after, coarse[...])
    image = (g2[...] + dot2(z, m1[...]) - centre * g1[...]) * inv
    last = alpha * (image + dot2(z1, m0[...]) - centre * after) - w
    w2[...] = last
    z2 = hdot(last, coarse[...])
    lift = lifted(jnp.concatenate([z1, z2], axis=0), wide_in[...], spread[:, :SLOTS])
    lift1[...] = lift[:RHS]
    lift2[...] = lift[RHS:]


def next_kernel(
    coef, lift, n0, n1, n2, n3, image, before, now, inverse, load, image_out, s0, s1, s2, s3,
):
    centre, _, alpha = terms_in(coef, FACE)
    for s, jump in zip(SEG, jumped(image, (n0, n1, n2, n3)), strict=True):
        load[:, s] = alpha * (jump + lift[:, s] - centre * now[:, s]) - before[:, s]
    put_image(bdot(load[...].astype(BF16), inverse[...]), image_out, (s0, s1, s2, s3))


def last_kernel(
    coef, lift, n0, n1, n2, n3, image, before, now, inverse, load, image_out, low_sub, low_grp,
):
    centre, _, alpha = terms_in(coef, FACE)
    for s, jump in zip(SEG, jumped(image, (n0, n1, n2, n3)), strict=True):
        load[:, s] = alpha * (jump + lift[:, s] - centre * now[:, s]) - before[:, s]
    u = bdot(load[...].astype(BF16), inverse[...])
    image_out[...] = u
    low_sub[...] = u[:, SEG[1]]
    low_grp[...] = u[:, SEG[3]]


def terms_kernel(coef, block, load1, load2, load3, image, spread, wide_in, stack, partial4, keep, send):
    centre, _, alpha = terms_in(coef, FACE)
    w, g = terms_of(load3[...], image[...], wide_in[...], spread[:, :SLOTS])
    left, right = slice(0, FACE), slice(FACE, 2 * FACE)
    stack[:RHS] = block[...]
    for level, load in ((1, load1), (2, load2), (3, load3)):
        stack[level * RHS : (level + 1) * RHS, left] = load[:, SEG[0]]
        stack[level * RHS : (level + 1) * RHS, right] = load[:, SEG[2]]
    for half, s in ((left, SEG[0]), (right, SEG[2])):
        partial4[:, half] = alpha * (image[:, s] - centre * load3[:, s]) - load2[:, s]
    known = jnp.concatenate([stack[...], jnp.zeros((64, 2 * FACE), F32)], axis=0)
    terms = hdot(stack[...], known, NT)
    t = [terms[i * RHS : (i + 1) * RHS] for i in range(BLOCKS - 1)]
    lane = lax.broadcasted_iota(jnp.int32, (RHS, 128), 1)
    first = jnp.where(lane < 64, t[0], pltpu.roll(t[1], 48, 1))
    second = jnp.where(lane < 32, pltpu.roll(t[2], 96, 1), pltpu.roll(t[3], 112, 1))
    split_by_core(
        jnp.concatenate([w, jnp.zeros((RHS, NCO), F32)], axis=0),
        jnp.concatenate([g, jnp.concatenate([first, second], axis=1)], axis=0),
        keep,
        send,
    )


def coded(total):
    zero = lax.axis_index("core") == 0
    return jnp.where(zero, jnp.concatenate(high_low(total[:RHS]), axis=0), total)


def decoded(total):
    zero = lax.axis_index("core") == 0
    whole = jnp.concatenate([total[:RHS] + total[RHS:], jnp.zeros((RHS, NCO), F32)], axis=0)
    return jnp.where(zero, whole, total)


def gram_kernel(coef, stack, partial4, n0, n2, keep, got, known4, out):
    _, _, alpha = terms_in(coef, FACE)
    known4[:, :FACE] = partial4[:, :FACE] - alpha * n0[...]
    known4[:, FACE:] = partial4[:, FACE:] - alpha * n2[...]
    q = known4[...]
    row = hdot(q, jnp.concatenate([stack[...], q, jnp.zeros((48, 2 * FACE), F32)], axis=0), NT)
    row = jnp.concatenate([row[:8], row[8:]], axis=1)
    value = jnp.concatenate([coded(keep[...] + got[...]), row], axis=0).astype(BF16)
    for p in range(16):
        out[p] = value


def depth1_kernel(got, out):
    total = summed(got)
    value = jnp.concatenate([coded(decoded(total[: 2 * RHS])), total[2 * RHS :]], axis=0).astype(BF16)
    for q in range(8):
        out[q] = value


def sum_kernel(got, out):
    total = summed(got)
    out[: 2 * RHS] = decoded(total[: 2 * RHS])
    out[2 * RHS :] = total[2 * RHS :]


def store_kernel(stack, basis_hbm, basis, sem):
    for level in range(BLOCKS - 1):
        basis[level] = stack[level * RHS : (level + 1) * RHS].reshape(RHS, 1, 1, 2 * FACE)
    copy = pltpu.make_async_copy(basis, basis_hbm.at[: BLOCKS - 1], sem)
    copy.start()
    copy.wait()


def final_kernel(
    coef, own, got, coarse, matrix, w0, w1, w2, known4, spread, wide_in, stored,
    basis_hbm, gram_hbm, block4, gram, square, sems,
):
    centre, _, alpha = terms_in(coef, NCO)
    zero = lax.axis_index("core") == 0
    w3 = jnp.where(zero, own[:RHS], got[:RHS])
    second = jnp.where(zero, got[: 2 * RHS], own[: 2 * RHS])
    g3, packed = second[:RHS], second[RHS:]
    row = own[2 * RHS :] + got[2 * RHS :]
    row = jnp.concatenate([row[:, :128], row[:, 128:]], axis=0)
    z3 = hdot(w3, coarse[...])
    lift = lifted(z3, wide_in[...], spread[:, :SLOTS])
    value = jnp.concatenate(
        [known4[:, :FACE] + alpha * lift[:, SEG[0]], known4[:, FACE:] + alpha * lift[:, SEG[2]]], axis=1
    )
    block4[...] = value.reshape(RHS, 1, 1, 2 * FACE)
    late = pltpu.make_async_copy(block4, basis_hbm.at[BLOCKS - 1], sems.at[0])
    late.start()
    wk = alpha * (g3 - centre * w3) - w2[...]
    z_row = jnp.concatenate([jnp.zeros((64, NCO), F32), z3, jnp.zeros((48, NCO), F32)], axis=0)
    rows = jnp.concatenate([w0[...], w1[...], w2[...], w3, wk, dot2(z3, matrix[...])], axis=0)
    cross = hdot(rows, z_row, NT)
    alpha = alpha[:, :128]
    h0, h1 = packed[:, :128], packed[:, 128:]
    parts = [h0, pltpu.roll(h0, 80, 1), pltpu.roll(h1, 32, 1), pltpu.roll(h1, 16, 1)]
    lane = lax.broadcasted_iota(jnp.int32, (RHS, 128), 1)
    for i in range(BLOCKS - 1):
        rows = slice(i * RHS, (i + 1) * RHS)
        square[rows] = jnp.where(lane < 64, parts[i], 0.0) + alpha * cross[rows]
    last = slice(4 * RHS, 5 * RHS)
    square[last] = alpha * alpha * cross[5 * RHS :] + jnp.where(lane < 64, 0.0, row)
    square[5 * RHS :] = jnp.zeros((48, 128), F32)
    own4 = jnp.where(lane < 64, row, alpha * cross[last])
    column = jnp.concatenate([jnp.zeros((64, 128), F32), own4, jnp.zeros((48, 128), F32)], axis=0)
    up = square[...]
    r = lax.broadcasted_iota(jnp.int32, (128, 128), 0) // RHS
    c = lax.broadcasted_iota(jnp.int32, (128, 128), 1) // RHS
    sided = jnp.where(r < c, up, 0.0) + column
    whole = jnp.where(r == c, up, 0.0) + sided + sided.T
    gram[...] = (whole * (1.0 / (2 * FACE * 64)))[: BLOCKS * RHS, : BLOCKS * RHS]
    result = pltpu.make_async_copy(gram, gram_hbm, sems.at[1])
    result.start()
    late.wait()
    result.wait()


def body(residual, bounds, local_inverse, corner_basis, corner_map, coarse_inverse):
    inverse = local_inverse.reshape(WIDTH, WIDTH)
    corners = corner_basis.reshape(-1, WIDTH)
    count = corners.shape[0]
    face = ((RHS, FACE), F32)
    load = ((RHS, WIDTH), F32)
    small = ((RHS, NCO), F32)
    half = ((RHS, 2 * FACE), F32)
    square = ((NCO, NCO), F32)
    blocks = ((BLOCKS, RHS, 1, 1, 2 * FACE), F32)
    smem, hbm = pltpu.SMEM, pltpu.HBM

    *packs, labels, block, corners = call(
        pack_kernel,
        [((64, FACE), BF16)] * 4 + [((1, 256), jnp.int32), half, ((count, WIDTH), BF16)],
        [residual, corners, corner_map.reshape(1, count)],
        [hbm] * 3,
        [pltpu.VMEM((RHS, 1, 1, 2 * FACE), F32), pltpu.VMEM((1, count), jnp.int32), pltpu.VMEM((4, 64, FACE), BF16),
         pltpu.SemaphoreType.DMA((3,))],
    )
    near = neighbours(packs)
    inverse, coef, own_row = call(
        fetch_kernel,
        [((WIDTH, WIDTH), BF16), ((8, WIDTH), F32), ((8, NCO), F32)],
        [bounds, inverse, coarse_inverse],
        [smem, hbm, hbm],
        [pltpu.VMEM((1, NCO), F32), pltpu.SemaphoreType.DMA((2,))],
    )
    load0, wide, spread, image0, *sends = call(
        start_kernel,
        [load, ((SLOTS, WIDTH), BF16), ((NCO, 256), BF16), load, face, face, face, face],
        [block, *near, corners, labels, inverse],
    )
    near0 = neighbours(sends)
    keep, send = call(
        moment_kernel,
        [((272, NCO), F32), ((272, NCO), F32)],
        [load0, image0, wide, spread, inverse],
    )
    got = swapped(send)
    base1, g2 = call(join_kernel, [load, small], [coef, load0, *near0, image0, wide, spread, inverse])
    (v,) = call(plane0_kernel, [((16, 24, NCO), BF16)], [keep, got, g2])
    (v,) = call(depth0_kernel, [((8, 24, NCO), BF16)], [exchange(v, PLANE), own_row])
    (v,) = call(spread0_kernel, [((16, 40, NCO), BF16)], [exchange(v, "z")])
    (own,) = call(collect0_kernel, [((576, NCO), BF16)], [exchange(v, PLANE)])

    got = swapped(own)
    coarse, w0, z0, load1, image1, *sends = call(
        block1_kernel,
        [square, small, small, load, load, face, face, face, face],
        [own, got, base1, coef, spread, wide, inverse],
    )
    near1 = neighbours(sends)
    w1, w2, lift1, lift2, m0 = call(
        solve_kernel,
        [small, small, load, load, ((NCO, NCO), BF16)],
        [coef, own, got, z0, w0, coarse, spread, wide],
        scratch=[pltpu.VMEM((NCO, NCO), BF16), pltpu.VMEM((RHS, NCO), F32), pltpu.VMEM((RHS, NCO), F32)],
    )
    load2, image2, *sends = call(
        next_kernel,
        [load, load, face, face, face, face],
        [coef, lift1, *near1, image1, load0, load1, inverse],
    )
    near2 = neighbours(sends)
    load3, image3, low_sub, low_grp = call(
        last_kernel,
        [load, load, face, face],
        [coef, lift2, *near2, image2, load1, load2, inverse],
    )
    n0 = along(low_sub, SUB, -1)
    n2 = along(low_grp, "x", -1)
    stack, partial4, keep, send = call(
        terms_kernel,
        [((4 * RHS, 2 * FACE), F32), half, ((32, NCO), F32), ((32, NCO), F32)],
        [coef, block, load1, load2, load3, image3, spread, wide],
    )
    got = swapped(send)
    known4, v = call(
        gram_kernel,
        [half, ((16, 40, NCO), BF16)],
        [coef, stack, partial4, n0, n2, keep, got],
    )
    (stored,) = call(
        store_kernel,
        [blocks],
        [stack],
        scratch=[pltpu.VMEM((BLOCKS - 1, RHS, 1, 1, 2 * FACE), F32), pltpu.SemaphoreType.DMA(())],
        out_space=hbm,
    )
    (v,) = call(depth1_kernel, [((8, 40, NCO), BF16)], [exchange(v, PLANE)])
    (own,) = call(sum_kernel, [((40, NCO), F32)], [exchange(v, "z")])
    basis, gram = call(
        final_kernel,
        [blocks, ((BLOCKS * RHS, BLOCKS * RHS), F32)],
        [coef, own, swapped(own), coarse, m0, w0, w1, w2, known4, spread, wide, stored],
        [None] * 11 + [hbm],
        [pltpu.VMEM((RHS, 1, 1, 2 * FACE), F32), pltpu.VMEM((BLOCKS * RHS, BLOCKS * RHS), F32),
         pltpu.VMEM((128, 128), F32), pltpu.SemaphoreType.DMA((2,))],
        out_space=hbm,
        aliases={11: 0},
    )
    return basis, gram


def solution(mesh):
    split = Mesh(mesh.devices.reshape(8, 4, 2, mesh.shape["grp"]), ("z", "y", "core", "x"))
    in_specs = (
        P(None, SUB, "x", None),
        P(),
        P(SUB, "x", None, None),
        P(SUB, "x", None, None),
        P(SUB, "x", None),
        P(("z", "y", "core", "x"), None),
    )
    out_specs = (P(None, None, SUB, "x", None), P())
    return jax.shard_map(body, mesh=split, in_specs=in_specs, out_specs=out_specs, check_vma=False)
```

```python
import functools

import jax
import jax.numpy as jnp
from jax import lax
from jax.experimental import pallas as pl
from jax.experimental.pallas import tpu as pltpu
from jax.sharding import Mesh
from jax.sharding import PartitionSpec as P


BLOCKS = 5
RHS = 16
FACE = 256
WIDTH = 4 * FACE
NCO = 256
SLOT = 32
SLOTS = 5 * SLOT
SUB = ("z", "y", "core")
PLANE = ("y", "x")
HIGH = lax.Precision.HIGHEST
F32, BF16 = jnp.float32, jnp.bfloat16
SEG = [slice(i * FACE, (i + 1) * FACE) for i in range(4)]


NN = (((1,), (0,)), ((), ()))
NT = (((1,), (1,)), ((), ()))


def hdot(a, b, dims=NN):
    return lax.dot_general(a, b, dims, precision=HIGH, preferred_element_type=F32)


def bdot(a, b, dims=NN):
    return lax.dot_general(a, b, dims, preferred_element_type=F32)


def halves_of(a):
    top = a.astype(BF16)
    return top, (a - top.astype(F32)).astype(BF16)


def dot_halves(a, table):
    rows = table.shape[0] // 2
    return dot2(a, table[:rows]) + bdot(a.astype(BF16), table[rows:])


def dot2(a, exact, dims=NN):
    rows = a.shape[0]
    top = a.astype(BF16)
    low = (a - top.astype(F32)).astype(BF16)
    got = bdot(jnp.concatenate([top, low], axis=0), exact, dims)
    return got[:rows] + got[rows:]


def call(kernel, outs, args, spaces=None, scratch=(), limit=20, out_space=None, aliases=None):
    vmem = pl.BlockSpec(memory_space=pltpu.VMEM)
    out_spaces = out_space if isinstance(out_space, list) else [out_space] * len(outs)
    out_specs = [vmem if s is None else pl.BlockSpec(memory_space=s) for s in out_spaces]
    specs = [vmem if s is None else pl.BlockSpec(memory_space=s) for s in (spaces or [None] * len(args))]
    if spaces:
        args = [
            pltpu.with_memory_space_constraint(a, pltpu.HBM) if s is pltpu.HBM else a for a, s in zip(args, spaces)
        ]
    run = pl.pallas_call(
        kernel,
        out_shape=[
            pltpu.HBM(s, d) if space is pltpu.HBM else jax.ShapeDtypeStruct(s, d)
            for (s, d), space in zip(outs, out_spaces)
        ],
        in_specs=specs,
        out_specs=out_specs,
        scratch_shapes=list(scratch),
        input_output_aliases=aliases or {},
        compiler_params=pltpu.CompilerParams(vmem_limit_bytes=limit << 20),
    )
    return run(*args)


def along(x, axis, by):
    count = lax.axis_size(axis)
    return lax.ppermute(x, axis, [(i, (i + by) % count) for i in range(count)])


def exchange(x, axis):
    return lax.all_to_all(x, axis, split_axis=0, concat_axis=0, tiled=True)


def swapped(v):
    return along(v, "core", 1)


def in_pairs(v, axis, first):
    count = lax.axis_size(axis)
    pairs = []
    for i in range(first, first + count, 2):
        a, b = i % count, (i + 1) % count
        pairs += [(a, b), (b, a)]
    return lax.ppermute(v, axis, pairs)


def neighbours(sends):
    return [in_pairs(sends[0], SUB, 1), in_pairs(sends[1], "x", 1), in_pairs(sends[2], "x", 0), swapped(sends[3])]


def label_of(n):
    return ((n // 4) % 2) * 128 + ((n // 8) % 4 * 4 + n % 4) * 8 + n // 32


def pack_kernel(
    block_hbm, corners_hbm, ids_hbm,
    s0, s1, s2, s3, labels, block, corners, wide_block, given, packs, sems,
):
    copies = [
        pltpu.make_async_copy(src, dst, sems.at[i])
        for i, (src, dst) in enumerate(
            ((block_hbm, wide_block), (corners_hbm, corners), (ids_hbm, given))
        )
    ]
    for copy in copies:
        copy.start()
    for copy in copies:
        copy.wait()
    count = corners.shape[0]
    labels[...] = jnp.full((1, 256), -1, jnp.int32)
    labels[:, :count] = label_of(given[...])
    text = labels[...].astype(F32).astype(BF16)
    x = wide_block[...].reshape(RHS, 2 * FACE)
    block[...] = x
    top = x.astype(BF16)
    rest = (x - top.astype(F32)).astype(BF16)
    for i, s in enumerate(SEG):
        if i % 2 == 0:
            packs[i, :RHS] = top[:, SEG[i // 2]]
            packs[i, RHS : 2 * RHS] = rest[:, SEG[i // 2]]
        else:
            packs[i, : 2 * RHS] = jnp.zeros((2 * RHS, FACE), BF16)
        packs[i, 2 * RHS : 2 * RHS + count] = corners[:, s]
        packs[i, 2 * RHS + count :] = jnp.broadcast_to(text, (8, FACE))
    put_sends([packs[i] for i in range(4)], (s0, s1, s2, s3))


def terms_of(load, u, wide, spread_t):
    both = dot2(dot2(jnp.concatenate([load * 0.5, u], axis=0), wide, NT), spread_t, NT)
    return both[:RHS], both[RHS:]


def lifted(z, wide, spread_t):
    return dot2(dot2(z, spread_t), wide)


def either(axis, even_branch, odd_branch):
    even = lax.axis_index(axis) % 2 == 0
    pl.when(even)(even_branch)
    pl.when(jnp.logical_not(even))(odd_branch)


def on_core(zero_branch, other_branch):
    either("core", zero_branch, other_branch)


def put_pair(axis, up, low, first, second):
    def even():
        first[...] = up
        second[...] = low

    def odd():
        first[...] = low
        second[...] = up

    either(axis, even, odd)


def put_sends(faces, outs):
    put_pair("core", faces[0], faces[1], outs[3], outs[0])
    put_pair("x", faces[2], faces[3], outs[2], outs[1])


def put_image(u, out, sends):
    out[...] = u
    put_sends([u[:, s] for s in SEG], sends)


def arrived(refs):
    values = [r[...] for r in refs]
    if values[0].dtype != F32:
        values = [v.astype(F32) for v in values]
    zero, even = lax.axis_index("core") == 0, lax.axis_index("x") % 2 == 0
    return [
        jnp.where(zero, values[3], values[0]),
        jnp.where(zero, values[0], values[3]),
        jnp.where(even, values[2], values[1]),
        jnp.where(even, values[1], values[2]),
    ]


def split_by_core(first, second, keep, send):
    def zero():
        keep[...] = first
        send[...] = second

    def one():
        keep[...] = second
        send[...] = first

    on_core(zero, one)


def high_low(x):
    top = x.astype(BF16).astype(F32)
    return top, x - top


def start_kernel(
    block, r0, r1, r2, r3, corners, labels, inverse, load_out, wide_out, spread_out, image, s0, s1, s2, s3,
):
    count = corners.shape[0]
    k = 2 * RHS
    next_sub, prev_sub, next_grp, prev_grp = arrived((r0, r1, r2, r3))
    load_out[:, SEG[0]] = block[:, :FACE]
    load_out[:, SEG[1]] = -(prev_sub[:RHS] + prev_sub[RHS:k])
    load_out[:, SEG[2]] = block[:, FACE:]
    load_out[:, SEG[3]] = -(prev_grp[:RHS] + prev_grp[RHS:k])
    put_image(dot2(load_out[...], inverse[...]), image, (s0, s1, s2, s3))
    wide_out[...] = jnp.zeros((SLOTS, WIDTH), BF16)
    wide_out[:count] = corners[...]
    others = (next_sub, prev_sub, next_grp, prev_grp)
    for i, other in enumerate(others):
        wide_out[SLOT * (i + 1) : SLOT * (i + 1) + count, SEG[i]] = (-other[k : k + count]).astype(BF16)
    lane = lax.broadcasted_iota(jnp.int32, (8, 256), 1)
    ids = jnp.where(lane < SLOT, jnp.broadcast_to(labels[...], (8, 256)).astype(F32), -1.0)
    for i, other in enumerate(others):
        moved = pltpu.roll(other[k + count :], SLOT * (i + 1), 1)
        mine = jnp.logical_and(lane >= SLOT * (i + 1), lane < SLOT * (i + 2))
        ids = jnp.where(mine, moved, ids)
    number = lax.broadcasted_iota(jnp.int32, (NCO, 256), 0).astype(F32)
    spread_out[...] = (number == ids[:1]).astype(F32).astype(BF16)


def fetch_kernel(bounds, inverse_hbm, row_hbm, out, coef, own_row, row, sems):
    fetch = pltpu.make_async_copy(inverse_hbm, out, sems.at[0])
    fetch.start()
    copy = pltpu.make_async_copy(row_hbm, row, sems.at[1])
    copy.start()
    low, high = bounds[0], bounds[1]
    centre = jnp.full((1, WIDTH), (low + high) * 0.5, F32)
    inv = 1.0 / jnp.full((1, WIDTH), (high - low) * 0.5, F32)
    coef[...] = jnp.concatenate([centre, inv, 2.0 * inv, jnp.zeros((5, WIDTH), F32)], axis=0)
    n = lax.broadcasted_iota(jnp.int32, (NCO, NCO), 0)
    m = lax.broadcasted_iota(jnp.int32, (NCO, NCO), 1)
    order = (label_of(n) == m).astype(F32).astype(BF16)
    copy.wait()
    own_row[...] = dot2(jnp.broadcast_to(row[...], (RHS, NCO)), order)[:8]
    fetch.wait()


def moment_kernel(load0, image, wide_in, spread, inverse, keep, send, lifted_image):
    wide, spread_t = wide_in[...], spread[:, :SLOTS]
    pairs0 = bdot(wide, wide, NT) * 0.5
    wide_image = bdot(wide, inverse[...])
    top, low = halves_of(wide_image)
    top, low = halves_of(bdot(spread_t, top) + bdot(spread_t, low))
    lifted_image[:NCO] = top
    lifted_image[NCO:] = low
    pairs1 = dot2(wide_image, wide, NT)
    half = dot2(jnp.concatenate([pairs0, pairs1], axis=0), spread_t, NT)
    half = jnp.concatenate([half[:SLOTS], half[SLOTS:]], axis=1)
    top = half.astype(BF16)
    low = (half - top.astype(F32)).astype(BF16)
    both = bdot(spread_t, jnp.concatenate([top, low], axis=1))
    both = both[:, : 2 * NCO] + both[:, 2 * NCO :]
    w, g = terms_of(load0[...], image[...], wide, spread_t)

    def put(first, second):
        first[:NCO] = both[:, :NCO]
        first[NCO:] = w
        second[:NCO] = both[:, NCO:]
        second[NCO:] = g

    on_core(lambda: put(keep, send), lambda: put(send, keep))


def jumped(image, near):
    return [image[:, s] - n for s, n in zip(SEG, arrived(near), strict=True)]


def put_chain(u, lifts, sends):
    top = u.astype(BF16)
    low = (u - top.astype(F32)).astype(BF16)
    put_sends([jnp.concatenate([top[:, s], low[:, s], lifts[:, s]], axis=0) for s in SEG], sends)


def chain_jumps(u, own_lift, near):
    far = arrived(near)
    jump = jnp.concatenate([u[:, s] - (n[:RHS] + n[RHS : 2 * RHS]) for s, n in zip(SEG, far, strict=True)], axis=1)
    lift = [own_lift(s) - n[2 * RHS :] for s, n in zip(SEG, far, strict=True)]
    return jump, jnp.concatenate(lift, axis=1)


def join_kernel(
    coef, load0, n0, n1, n2, n3, image, wide_in, spread, inverse, lifted_image, base1, jump0, g2, image_x, s0, s1, s2, s3
):
    centre, inv, _ = terms_in(coef, WIDTH)
    jump = jnp.concatenate(jumped(image, (n0, n1, n2, n3)), axis=1)
    jump0[...] = jump
    base1[...] = (jump - centre * load0[...]) * inv
    u = dot2(jump, inverse[...])
    image_x[...] = u
    g2[...] = dot2(dot2(u, wide_in[...], NT), spread[:, :SLOTS], NT)
    put_chain(u, lifted_image[:NCO], (s0, s1, s2, s3))


def chain1_kernel(
    n0, n1, n2, n3, image_x, lifted_image, inverse_hbm,
    jump1, lift1_hbm, image_x2, lifted2, s0, s1, s2, s3, inverse, lift1, sems,
):
    fetch = pltpu.make_async_copy(inverse_hbm, inverse, sems.at[0])
    fetch.start()

    def own_lift(s):
        return lifted_image[:NCO, s].astype(F32) + lifted_image[NCO:, s].astype(F32)

    jump, lift = chain_jumps(image_x[...], own_lift, (n0, n1, n2, n3))
    jump1[...] = jump
    top, low = halves_of(lift)
    lift1[:NCO] = top
    lift1[NCO:] = low
    store = pltpu.make_async_copy(lift1, lift1_hbm, sems.at[1])
    store.start()
    fetch.wait()
    u = dot2(jump, inverse[...])
    image_x2[...] = u
    both = bdot(lift1[...], inverse[...])
    lifts = (both[:NCO] + both[NCO:]).astype(BF16)
    lifted2[...] = lifts
    put_chain(u, lifts, (s0, s1, s2, s3))
    store.wait()


def chain2_kernel(n0, n1, n2, n3, image_x2, lifted2, jump2, lift2):
    jump, lift = chain_jumps(image_x2[...], lambda s: lifted2[:, s].astype(F32), (n0, n1, n2, n3))
    jump2[...] = jump
    top, low = halves_of(lift)
    lift2[:NCO] = top
    lift2[NCO:] = low


def plane0_kernel(keep, got, g2, out):
    pieces = [high_low(keep[NCO:] + got[NCO:]), high_low(g2[...])]
    zero = jnp.zeros((4, NCO), F32)
    for p in range(16):
        rows = slice(16 * p, 16 * p + 16)
        small = [piece[part][p : p + 1] for part in range(2) for piece in pieces]
        out[p] = jnp.concatenate([keep[rows] + got[rows], *small, zero], axis=0).astype(BF16)


def summed(got):
    total = got[0].astype(F32)
    for p in range(1, got.shape[0]):
        total = total + got[p].astype(F32)
    return total


def depth0_kernel(got, own_row, out):
    total = summed(got)
    g = total[16:18] + total[18:20]
    rows = [total[:16], *high_low(g), *high_low(own_row[:1]), jnp.zeros((2, NCO), F32)]
    value = jnp.concatenate(rows, axis=0).astype(BF16)
    for q in range(8):
        out[q] = value


def spread0_kernel(got, out):
    every = [got[q].astype(F32) for q in range(8)]
    total = functools.reduce(jnp.add, every)
    g = total[16:18] + total[18:20]
    rows = [total[:16], *high_low(g), jnp.zeros((4, NCO), F32)]
    rows += [r[20:21] for r in every] + [r[21:22] for r in every]
    value = jnp.concatenate(rows, axis=0).astype(BF16)
    for p in range(16):
        out[p] = value


def collect0_kernel(got, out):
    g = []
    for p in range(16):
        out[16 * p : 16 * p + 16] = got[p, :16]
        g.append(got[p, 16:24].astype(F32))
        out[320 + 8 * p : 328 + 8 * p] = got[p, 24:32]
        out[448 + 8 * p : 456 + 8 * p] = got[p, 32:40]
    out[256:320] = jnp.concatenate([r[i : i + 1] for i in range(4) for r in g], axis=0).astype(BF16)


def terms_in(coef, width):
    return coef[0:1, :width], coef[1:2, :width], coef[2:3, :width]


def march_kernel(
    coef, own, got, load0, base1, jump0, jump1, jump2, chain2, spread, wide_in, chain1_hbm, inverse_hbm,
    coarse, m0, w0, w1, w2, load1, load2, load3, image3, low_sub, low_grp, m1, g1, g2, chain1, inverse, sems,
):
    table = pltpu.make_async_copy(chain1_hbm, chain1, sems.at[0])
    table.start()
    fetch = pltpu.make_async_copy(inverse_hbm, inverse, sems.at[1])
    fetch.start()

    def put(first, second):
        for half, part in ((slice(0, 128), first), (slice(128, 256), second)):
            coarse[half] = part[320:448].astype(F32) + part[448:576].astype(F32)
        m0[...] = first[:NCO]
        m1[...] = second[:NCO]
        w0[...] = first[256:272].astype(F32) + first[288:304].astype(F32)
        g1[...] = second[256:272].astype(F32) + second[288:304].astype(F32)
        parts = [part[i : i + RHS].astype(F32) for part in (first, second) for i in (272, 304)]
        g2[...] = functools.reduce(jnp.add, parts)

    on_core(lambda: put(own, got), lambda: put(got, own))
    centre, inv, alpha = terms_in(coef, NCO)
    w = w0[...]
    z = hdot(w, coarse[...])
    after = (g1[...] + dot2(z, m0[...]) - centre * w) * inv
    w1[...] = after
    z1 = hdot(after, coarse[...])
    image = (g2[...] + dot2(z, m1[...]) - centre * g1[...]) * inv
    last = alpha * (image + dot2(z1, m0[...]) - centre * after) - w
    w2[...] = last
    z2 = hdot(last, coarse[...])
    both = jnp.concatenate([z, z1, z2], axis=0)
    lift = lifted(both, wide_in[...], spread[:, :SLOTS])
    far = dot_halves(z, chain2[...])
    table.wait()
    near = dot_halves(both[: 2 * RHS], chain1[...])
    centre, inv, alpha = terms_in(coef, WIDTH)
    x1 = base1[...] + inv * lift[:RHS]
    load1[...] = x1
    j1 = inv * (jump1[...] + near[:RHS] - centre * jump0[...])
    x2 = alpha * (j1 + lift[RHS : 2 * RHS] - centre * x1) - load0[...]
    load2[...] = x2
    jj1 = inv * (jump2[...] + far - centre * jump1[...])
    j2 = alpha * (jj1 + near[RHS:] - centre * j1) - jump0[...]
    x3 = alpha * (j2 + lift[2 * RHS :] - centre * x2) - x1
    load3[...] = x3
    fetch.wait()
    u = bdot(x3.astype(BF16), inverse[...])
    image3[...] = u
    low_sub[...] = u[:, SEG[1]]
    low_grp[...] = u[:, SEG[3]]


def terms_kernel(coef, block, load1, load2, load3, image, spread, wide_in, stack, partial4, keep, send):
    centre, _, alpha = terms_in(coef, FACE)
    w, g = terms_of(load3[...], image[...], wide_in[...], spread[:, :SLOTS])
    left, right = slice(0, FACE), slice(FACE, 2 * FACE)
    stack[:RHS] = block[...]
    for level, load in ((1, load1), (2, load2), (3, load3)):
        stack[level * RHS : (level + 1) * RHS, left] = load[:, SEG[0]]
        stack[level * RHS : (level + 1) * RHS, right] = load[:, SEG[2]]
    for half, s in ((left, SEG[0]), (right, SEG[2])):
        partial4[:, half] = alpha * (image[:, s] - centre * load3[:, s]) - load2[:, s]
    known = jnp.concatenate([stack[...], jnp.zeros((64, 2 * FACE), F32)], axis=0)
    terms = hdot(stack[...], known, NT)
    t = [terms[i * RHS : (i + 1) * RHS] for i in range(BLOCKS - 1)]
    lane = lax.broadcasted_iota(jnp.int32, (RHS, 128), 1)
    first = jnp.where(lane < 64, t[0], pltpu.roll(t[1], 48, 1))
    second = jnp.where(lane < 32, pltpu.roll(t[2], 96, 1), pltpu.roll(t[3], 112, 1))
    split_by_core(
        jnp.concatenate([w, jnp.zeros((RHS, NCO), F32)], axis=0),
        jnp.concatenate([g, jnp.concatenate([first, second], axis=1)], axis=0),
        keep,
        send,
    )


def coded(total):
    zero = lax.axis_index("core") == 0
    return jnp.where(zero, jnp.concatenate(high_low(total[:RHS]), axis=0), total)


def decoded(total):
    zero = lax.axis_index("core") == 0
    whole = jnp.concatenate([total[:RHS] + total[RHS:], jnp.zeros((RHS, NCO), F32)], axis=0)
    return jnp.where(zero, whole, total)


def gram_kernel(coef, stack, partial4, n0, n2, keep, got, known4, out):
    _, _, alpha = terms_in(coef, FACE)
    known4[:, :FACE] = partial4[:, :FACE] - alpha * n0[...]
    known4[:, FACE:] = partial4[:, FACE:] - alpha * n2[...]
    q = known4[...]
    row = hdot(q, jnp.concatenate([stack[...], q, jnp.zeros((48, 2 * FACE), F32)], axis=0), NT)
    row = jnp.concatenate([row[:8], row[8:]], axis=1)
    value = jnp.concatenate([coded(keep[...] + got[...]), row], axis=0).astype(BF16)
    for p in range(16):
        out[p] = value


def depth1_kernel(got, out):
    total = summed(got)
    value = jnp.concatenate([coded(decoded(total[: 2 * RHS])), total[2 * RHS :]], axis=0).astype(BF16)
    for q in range(8):
        out[q] = value


def sum_kernel(got, out):
    total = summed(got)
    out[: 2 * RHS] = decoded(total[: 2 * RHS])
    out[2 * RHS :] = total[2 * RHS :]


def store_kernel(stack, basis_hbm, basis, sem):
    for level in range(BLOCKS - 1):
        basis[level] = stack[level * RHS : (level + 1) * RHS].reshape(RHS, 1, 1, 2 * FACE)
    copy = pltpu.make_async_copy(basis, basis_hbm.at[: BLOCKS - 1], sem)
    copy.start()
    copy.wait()


def final_kernel(
    coef, own, got, coarse, matrix, w0, w1, w2, known4, spread, wide_in, stored,
    basis_hbm, gram_hbm, block4, gram, square, sems,
):
    centre, _, alpha = terms_in(coef, NCO)
    zero = lax.axis_index("core") == 0
    w3 = jnp.where(zero, own[:RHS], got[:RHS])
    second = jnp.where(zero, got[: 2 * RHS], own[: 2 * RHS])
    g3, packed = second[:RHS], second[RHS:]
    row = own[2 * RHS :] + got[2 * RHS :]
    row = jnp.concatenate([row[:, :128], row[:, 128:]], axis=0)
    z3 = hdot(w3, coarse[...])
    lift = lifted(z3, wide_in[...], spread[:, :SLOTS])
    value = jnp.concatenate(
        [known4[:, :FACE] + alpha * lift[:, SEG[0]], known4[:, FACE:] + alpha * lift[:, SEG[2]]], axis=1
    )
    block4[...] = value.reshape(RHS, 1, 1, 2 * FACE)
    late = pltpu.make_async_copy(block4, basis_hbm.at[BLOCKS - 1], sems.at[0])
    late.start()
    wk = alpha * (g3 - centre * w3) - w2[...]
    z_row = jnp.concatenate([jnp.zeros((64, NCO), F32), z3, jnp.zeros((48, NCO), F32)], axis=0)
    rows = jnp.concatenate([w0[...], w1[...], w2[...], w3, wk, dot2(z3, matrix[...])], axis=0)
    cross = hdot(rows, z_row, NT)
    alpha = alpha[:, :128]
    h0, h1 = packed[:, :128], packed[:, 128:]
    parts = [h0, pltpu.roll(h0, 80, 1), pltpu.roll(h1, 32, 1), pltpu.roll(h1, 16, 1)]
    lane = lax.broadcasted_iota(jnp.int32, (RHS, 128), 1)
    for i in range(BLOCKS - 1):
        rows = slice(i * RHS, (i + 1) * RHS)
        square[rows] = jnp.where(lane < 64, parts[i], 0.0) + alpha * cross[rows]
    last = slice(4 * RHS, 5 * RHS)
    square[last] = alpha * alpha * cross[5 * RHS :] + jnp.where(lane < 64, 0.0, row)
    square[5 * RHS :] = jnp.zeros((48, 128), F32)
    own4 = jnp.where(lane < 64, row, alpha * cross[last])
    column = jnp.concatenate([jnp.zeros((64, 128), F32), own4, jnp.zeros((48, 128), F32)], axis=0)
    up = square[...]
    r = lax.broadcasted_iota(jnp.int32, (128, 128), 0) // RHS
    c = lax.broadcasted_iota(jnp.int32, (128, 128), 1) // RHS
    sided = jnp.where(r < c, up, 0.0) + column
    whole = jnp.where(r == c, up, 0.0) + sided + sided.T
    gram[...] = (whole * (1.0 / (2 * FACE * 64)))[: BLOCKS * RHS, : BLOCKS * RHS]
    result = pltpu.make_async_copy(gram, gram_hbm, sems.at[1])
    result.start()
    late.wait()
    result.wait()


def body(residual, bounds, local_inverse, corner_basis, corner_map, coarse_inverse):
    inverse = local_inverse.reshape(WIDTH, WIDTH)
    corners = corner_basis.reshape(-1, WIDTH)
    count = corners.shape[0]
    face = ((RHS, FACE), F32)
    load = ((RHS, WIDTH), F32)
    small = ((RHS, NCO), F32)
    half = ((RHS, 2 * FACE), F32)
    square = ((NCO, NCO), F32)
    blocks = ((BLOCKS, RHS, 1, 1, 2 * FACE), F32)
    smem, hbm = pltpu.SMEM, pltpu.HBM

    *packs, labels, block, corners = call(
        pack_kernel,
        [((64, FACE), BF16)] * 4 + [((1, 256), jnp.int32), half, ((count, WIDTH), BF16)],
        [residual, corners, corner_map.reshape(1, count)],
        [hbm] * 3,
        [pltpu.VMEM((RHS, 1, 1, 2 * FACE), F32), pltpu.VMEM((1, count), jnp.int32), pltpu.VMEM((4, 64, FACE), BF16),
         pltpu.SemaphoreType.DMA((3,))],
    )
    near = neighbours(packs)
    inverse, coef, own_row = call(
        fetch_kernel,
        [((WIDTH, WIDTH), BF16), ((8, WIDTH), F32), ((8, NCO), F32)],
        [bounds, inverse, coarse_inverse],
        [smem, hbm, hbm],
        [pltpu.VMEM((1, NCO), F32), pltpu.SemaphoreType.DMA((2,))],
    )
    load0, wide, spread, image0, *sends = call(
        start_kernel,
        [load, ((SLOTS, WIDTH), BF16), ((NCO, 256), BF16), load, face, face, face, face],
        [block, *near, corners, labels, inverse],
    )
    near0 = neighbours(sends)
    keep, send, lifted_image = call(
        moment_kernel,
        [((272, NCO), F32), ((272, NCO), F32), ((2 * NCO, WIDTH), BF16)],
        [load0, image0, wide, spread, inverse],
    )
    got = swapped(send)
    chain = ((2 * RHS + NCO, FACE), BF16)
    table = ((2 * NCO, WIDTH), BF16)
    base1, jump0, g2, image_x, *sends = call(
        join_kernel,
        [load, load, small, load, chain, chain, chain, chain],
        [coef, load0, *near0, image0, wide, spread, inverse, lifted_image],
    )
    (v,) = call(plane0_kernel, [((16, 24, NCO), BF16)], [keep, got, g2])
    near1 = neighbours(sends)
    (v,) = call(depth0_kernel, [((8, 24, NCO), BF16)], [exchange(v, PLANE), own_row])
    jump1, chain1, image_x2, lifted2, *sends = call(
        chain1_kernel,
        [load, table, load, ((NCO, WIDTH), BF16), chain, chain, chain, chain],
        [*near1, image_x, lifted_image, local_inverse.reshape(WIDTH, WIDTH)],
        [None] * 6 + [hbm],
        [pltpu.VMEM((WIDTH, WIDTH), BF16), pltpu.VMEM((2 * NCO, WIDTH), BF16), pltpu.SemaphoreType.DMA((2,))],
        out_space=[None, hbm] + [None] * 6,
    )
    near2 = neighbours(sends)
    (v,) = call(spread0_kernel, [((16, 40, NCO), BF16)], [exchange(v, "z")])
    (own,) = call(collect0_kernel, [((576, NCO), BF16)], [exchange(v, PLANE)])
    jump2, chain2 = call(chain2_kernel, [load, table], [*near2, image_x2, lifted2])

    coarse, m0, w0, w1, w2, load1, load2, load3, image3, low_sub, low_grp = call(
        march_kernel,
        [square, ((NCO, NCO), BF16), small, small, small, load, load, load, load, face, face],
        [coef, own, swapped(own), load0, base1, jump0, jump1, jump2, chain2, spread, wide, chain1,
         local_inverse.reshape(WIDTH, WIDTH)],
        [None] * 11 + [hbm, hbm],
        [pltpu.VMEM((NCO, NCO), BF16), pltpu.VMEM((RHS, NCO), F32), pltpu.VMEM((RHS, NCO), F32),
         pltpu.VMEM((2 * NCO, WIDTH), BF16), pltpu.VMEM((WIDTH, WIDTH), BF16), pltpu.SemaphoreType.DMA((2,))],
    )
    n0 = along(low_sub, SUB, -1)
    n2 = along(low_grp, "x", -1)
    stack, partial4, keep, send = call(
        terms_kernel,
        [((4 * RHS, 2 * FACE), F32), half, ((32, NCO), F32), ((32, NCO), F32)],
        [coef, block, load1, load2, load3, image3, spread, wide],
    )
    got = swapped(send)
    known4, v = call(
        gram_kernel,
        [half, ((16, 40, NCO), BF16)],
        [coef, stack, partial4, n0, n2, keep, got],
    )
    (stored,) = call(
        store_kernel,
        [blocks],
        [stack],
        scratch=[pltpu.VMEM((BLOCKS - 1, RHS, 1, 1, 2 * FACE), F32), pltpu.SemaphoreType.DMA(())],
        out_space=hbm,
    )
    (v,) = call(depth1_kernel, [((8, 40, NCO), BF16)], [exchange(v, PLANE)])
    (own,) = call(sum_kernel, [((40, NCO), F32)], [exchange(v, "z")])
    basis, gram = call(
        final_kernel,
        [blocks, ((BLOCKS * RHS, BLOCKS * RHS), F32)],
        [coef, own, swapped(own), coarse, m0, w0, w1, w2, known4, spread, wide, stored],
        [None] * 11 + [hbm],
        [pltpu.VMEM((RHS, 1, 1, 2 * FACE), F32), pltpu.VMEM((BLOCKS * RHS, BLOCKS * RHS), F32),
         pltpu.VMEM((128, 128), F32), pltpu.SemaphoreType.DMA((2,))],
        out_space=hbm,
        aliases={11: 0},
    )
    return basis, gram


def solution(mesh):
    split = Mesh(mesh.devices.reshape(8, 4, 2, mesh.shape["grp"]), ("z", "y", "core", "x"))
    in_specs = (
        P(None, SUB, "x", None),
        P(),
        P(SUB, "x", None, None),
        P(SUB, "x", None, None),
        P(SUB, "x", None),
        P(("z", "y", "core", "x"), None),
    )
    out_specs = (P(None, None, SUB, "x", None), P())
    return jax.shard_map(body, mesh=split, in_specs=in_specs, out_specs=out_specs, check_vma=False)
```

```python
import functools

import jax
import jax.numpy as jnp
from jax import lax
from jax.experimental import pallas as pl
from jax.experimental.pallas import tpu as pltpu
from jax.sharding import Mesh
from jax.sharding import PartitionSpec as P


BLOCKS = 5
RHS = 16
FACE = 256
WIDTH = 4 * FACE
NCO = 256
SLOT = 32
SLOTS = 5 * SLOT
SUB = ("z", "y", "core")
PLANE = ("y", "x")
HIGH = lax.Precision.HIGHEST
F32, BF16 = jnp.float32, jnp.bfloat16
SEG = [slice(i * FACE, (i + 1) * FACE) for i in range(4)]


NN = (((1,), (0,)), ((), ()))
NT = (((1,), (1,)), ((), ()))


def hdot(a, b, dims=NN):
    return lax.dot_general(a, b, dims, precision=HIGH, preferred_element_type=F32)


def bdot(a, b, dims=NN):
    return lax.dot_general(a, b, dims, preferred_element_type=F32)


def halves_of(a):
    top = a.astype(BF16)
    return top, (a - top.astype(F32)).astype(BF16)


def dot_halves(a, table):
    rows = table.shape[0] // 2
    return dot2(a, table[:rows]) + bdot(a.astype(BF16), table[rows:])


def dot2(a, exact, dims=NN):
    rows = a.shape[0]
    top = a.astype(BF16)
    low = (a - top.astype(F32)).astype(BF16)
    got = bdot(jnp.concatenate([top, low], axis=0), exact, dims)
    return got[:rows] + got[rows:]


def call(kernel, outs, args, spaces=None, scratch=(), limit=20, out_space=None, aliases=None):
    vmem = pl.BlockSpec(memory_space=pltpu.VMEM)
    out_spaces = out_space if isinstance(out_space, list) else [out_space] * len(outs)
    out_specs = [vmem if s is None else pl.BlockSpec(memory_space=s) for s in out_spaces]
    specs = [vmem if s is None else pl.BlockSpec(memory_space=s) for s in (spaces or [None] * len(args))]
    if spaces:
        args = [
            pltpu.with_memory_space_constraint(a, pltpu.HBM) if s is pltpu.HBM else a for a, s in zip(args, spaces)
        ]
    run = pl.pallas_call(
        kernel,
        out_shape=[
            pltpu.HBM(s, d) if space is pltpu.HBM else jax.ShapeDtypeStruct(s, d)
            for (s, d), space in zip(outs, out_spaces)
        ],
        in_specs=specs,
        out_specs=out_specs,
        scratch_shapes=list(scratch),
        input_output_aliases=aliases or {},
        compiler_params=pltpu.CompilerParams(vmem_limit_bytes=limit << 20),
    )
    return run(*args)


def along(x, axis, by):
    count = lax.axis_size(axis)
    return lax.ppermute(x, axis, [(i, (i + by) % count) for i in range(count)])


def exchange(x, axis):
    return lax.all_to_all(x, axis, split_axis=0, concat_axis=0, tiled=True)


def swapped(v):
    return along(v, "core", 1)


def in_pairs(v, axis, first):
    count = lax.axis_size(axis)
    pairs = []
    for i in range(first, first + count, 2):
        a, b = i % count, (i + 1) % count
        pairs += [(a, b), (b, a)]
    return lax.ppermute(v, axis, pairs)


def neighbours(sends):
    return [in_pairs(sends[0], SUB, 1), in_pairs(sends[1], "x", 1), in_pairs(sends[2], "x", 0), swapped(sends[3])]


def label_of(n):
    return ((n // 4) % 2) * 128 + ((n // 8) % 4 * 4 + n % 4) * 8 + n // 32


def pack_kernel(
    block_hbm, corners_hbm, ids_hbm,
    s0, s1, s2, s3, labels, block, corners, wide_block, given, packs, sems,
):
    copies = [
        pltpu.make_async_copy(src, dst, sems.at[i])
        for i, (src, dst) in enumerate(
            ((block_hbm, wide_block), (corners_hbm, corners), (ids_hbm, given))
        )
    ]
    for copy in copies:
        copy.start()
    for copy in copies:
        copy.wait()
    count = corners.shape[0]
    labels[...] = jnp.full((1, 256), -1, jnp.int32)
    labels[:, :count] = label_of(given[...])
    text = labels[...].astype(F32).astype(BF16)
    x = wide_block[...].reshape(RHS, 2 * FACE)
    block[...] = x
    top = x.astype(BF16)
    rest = (x - top.astype(F32)).astype(BF16)
    for i, s in enumerate(SEG):
        if i % 2 == 0:
            packs[i, :RHS] = top[:, SEG[i // 2]]
            packs[i, RHS : 2 * RHS] = rest[:, SEG[i // 2]]
        else:
            packs[i, : 2 * RHS] = jnp.zeros((2 * RHS, FACE), BF16)
        packs[i, 2 * RHS : 2 * RHS + count] = corners[:, s]
        packs[i, 2 * RHS + count :] = jnp.broadcast_to(text, (8, FACE))
    put_sends([packs[i] for i in range(4)], (s0, s1, s2, s3))


def terms_of(load, u, wide, spread_t):
    both = dot2(dot2(jnp.concatenate([load * 0.5, u], axis=0), wide, NT), spread_t, NT)
    return both[:RHS], both[RHS:]


def lifted(z, wide, spread_t):
    return dot2(dot2(z, spread_t), wide)


def either(axis, even_branch, odd_branch):
    even = lax.axis_index(axis) % 2 == 0
    pl.when(even)(even_branch)
    pl.when(jnp.logical_not(even))(odd_branch)


def on_core(zero_branch, other_branch):
    either("core", zero_branch, other_branch)


def put_pair(axis, up, low, first, second):
    def even():
        first[...] = up
        second[...] = low

    def odd():
        first[...] = low
        second[...] = up

    either(axis, even, odd)


def put_sends(faces, outs):
    put_pair("core", faces[0], faces[1], outs[3], outs[0])
    put_pair("x", faces[2], faces[3], outs[2], outs[1])


def put_image(u, out, sends):
    out[...] = u
    put_sends([u[:, s] for s in SEG], sends)


def arrived(refs):
    values = [r[...] for r in refs]
    if values[0].dtype != F32:
        values = [v.astype(F32) for v in values]
    zero, even = lax.axis_index("core") == 0, lax.axis_index("x") % 2 == 0
    return [
        jnp.where(zero, values[3], values[0]),
        jnp.where(zero, values[0], values[3]),
        jnp.where(even, values[2], values[1]),
        jnp.where(even, values[1], values[2]),
    ]


def split_by_core(first, second, keep, send):
    def zero():
        keep[...] = first
        send[...] = second

    def one():
        keep[...] = second
        send[...] = first

    on_core(zero, one)


def high_low(x):
    top = x.astype(BF16).astype(F32)
    return top, x - top


def start_kernel(
    block, r0, r1, r2, r3, corners, labels, inverse, load_out, wide_out, spread_out, image, s0, s1, s2, s3,
):
    count = corners.shape[0]
    k = 2 * RHS
    next_sub, prev_sub, next_grp, prev_grp = arrived((r0, r1, r2, r3))
    load_out[:, SEG[0]] = block[:, :FACE]
    load_out[:, SEG[1]] = -(prev_sub[:RHS] + prev_sub[RHS:k])
    load_out[:, SEG[2]] = block[:, FACE:]
    load_out[:, SEG[3]] = -(prev_grp[:RHS] + prev_grp[RHS:k])
    put_image(dot2(load_out[...], inverse[...]), image, (s0, s1, s2, s3))
    wide_out[...] = jnp.zeros((SLOTS, WIDTH), BF16)
    wide_out[:count] = corners[...]
    others = (next_sub, prev_sub, next_grp, prev_grp)
    for i, other in enumerate(others):
        wide_out[SLOT * (i + 1) : SLOT * (i + 1) + count, SEG[i]] = (-other[k : k + count]).astype(BF16)
    lane = lax.broadcasted_iota(jnp.int32, (8, 256), 1)
    ids = jnp.where(lane < SLOT, jnp.broadcast_to(labels[...], (8, 256)).astype(F32), -1.0)
    for i, other in enumerate(others):
        moved = pltpu.roll(other[k + count :], SLOT * (i + 1), 1)
        mine = jnp.logical_and(lane >= SLOT * (i + 1), lane < SLOT * (i + 2))
        ids = jnp.where(mine, moved, ids)
    number = lax.broadcasted_iota(jnp.int32, (NCO, 256), 0).astype(F32)
    spread_out[...] = (number == ids[:1]).astype(F32).astype(BF16)


def fetch_kernel(bounds_hbm, inverse_hbm, row_hbm, out, coef, own_row, bounds, row, sems):
    limits = pltpu.make_async_copy(bounds_hbm, bounds, sems.at[2])
    limits.start()
    copy = pltpu.make_async_copy(row_hbm, row, sems.at[1])
    copy.start()
    fetch = pltpu.make_async_copy(inverse_hbm, out, sems.at[0])
    fetch.start()
    limits.wait()
    low, high = bounds[:, 0:1], bounds[:, 1:2]
    centre = jnp.broadcast_to((low + high) * 0.5, (1, WIDTH))
    inv = 1.0 / jnp.broadcast_to((high - low) * 0.5, (1, WIDTH))
    coef[...] = jnp.concatenate([centre, inv, 2.0 * inv, jnp.zeros((5, WIDTH), F32)], axis=0)
    n = lax.broadcasted_iota(jnp.int32, (NCO, NCO), 0)
    m = lax.broadcasted_iota(jnp.int32, (NCO, NCO), 1)
    order = (label_of(n) == m).astype(F32).astype(BF16)
    copy.wait()
    own_row[...] = dot2(jnp.broadcast_to(row[...], (RHS, NCO)), order)[:8]
    fetch.wait()


def moment_kernel(load0, image, wide_in, spread, inverse, keep, send, lifted_image):
    wide, spread_t = wide_in[...], spread[:, :SLOTS]
    pairs0 = bdot(wide, wide, NT) * 0.5
    wide_image = bdot(wide, inverse[...])
    top, low = halves_of(wide_image)
    top, low = halves_of(bdot(spread_t, top) + bdot(spread_t, low))
    lifted_image[:NCO] = top
    lifted_image[NCO:] = low
    pairs1 = dot2(wide_image, wide, NT)
    half = dot2(jnp.concatenate([pairs0, pairs1], axis=0), spread_t, NT)
    half = jnp.concatenate([half[:SLOTS], half[SLOTS:]], axis=1)
    top = half.astype(BF16)
    low = (half - top.astype(F32)).astype(BF16)
    both = bdot(spread_t, jnp.concatenate([top, low], axis=1))
    both = both[:, : 2 * NCO] + both[:, 2 * NCO :]
    w, g = terms_of(load0[...], image[...], wide, spread_t)

    def put(first, second):
        first[:NCO] = both[:, :NCO]
        first[NCO:] = w
        second[:NCO] = both[:, NCO:]
        second[NCO:] = g

    on_core(lambda: put(keep, send), lambda: put(send, keep))


def jumped(image, near):
    return [image[:, s] - n for s, n in zip(SEG, arrived(near), strict=True)]


def put_chain(u, lifts, sends):
    top = u.astype(BF16)
    low = (u - top.astype(F32)).astype(BF16)
    put_sends([jnp.concatenate([top[:, s], low[:, s], lifts[:, s]], axis=0) for s in SEG], sends)


def chain_jumps(u, own_lift, near):
    far = arrived(near)
    jump = jnp.concatenate([u[:, s] - (n[:RHS] + n[RHS : 2 * RHS]) for s, n in zip(SEG, far, strict=True)], axis=1)
    lift = [own_lift(s) - n[2 * RHS :] for s, n in zip(SEG, far, strict=True)]
    return jump, jnp.concatenate(lift, axis=1)


def join_kernel(
    coef, load0, n0, n1, n2, n3, image, wide_in, spread, inverse, lifted_image, base1, jump0, g2, image_x, s0, s1, s2, s3
):
    centre, inv, _ = terms_in(coef, WIDTH)
    jump = jnp.concatenate(jumped(image, (n0, n1, n2, n3)), axis=1)
    jump0[...] = jump
    base1[...] = (jump - centre * load0[...]) * inv
    u = dot2(jump, inverse[...])
    image_x[...] = u
    g2[...] = dot2(dot2(u, wide_in[...], NT), spread[:, :SLOTS], NT)
    put_chain(u, lifted_image[:NCO], (s0, s1, s2, s3))


def chain1_kernel(
    n0, n1, n2, n3, image_x, lifted_image, inverse_hbm,
    jump1, lift1_hbm, image_x2, lifted2, s0, s1, s2, s3, inverse, lift1, sends, sems,
):
    fetch = pltpu.make_async_copy(inverse_hbm, inverse, sems.at[0])
    fetch.start()

    def own_lift(s):
        return lifted_image[:NCO, s].astype(F32) + lifted_image[NCO:, s].astype(F32)

    jump, lift = chain_jumps(image_x[...], own_lift, (n0, n1, n2, n3))
    jump1[...] = jump
    top, low = halves_of(lift)
    lift1[:NCO] = top
    lift1[NCO:] = low
    store = pltpu.make_async_copy(lift1, lift1_hbm, sems.at[1])
    store.start()
    fetch.wait()
    u = dot2(jump, inverse[...])
    image_x2[...] = u
    lifts = bdot(top, inverse[...]).astype(BF16)
    put_chain(u, lifts, [sends.at[i] for i in range(4)])
    copies = [pltpu.make_async_copy(sends.at[i], s, sems.at[i + 2]) for i, s in enumerate((s0, s1, s2, s3))]
    for copy in copies:
        copy.start()
    lifted2[...] = lifts
    store.wait()
    for copy in copies:
        copy.wait()


def chain2_kernel(n0, n1, n2, n3, image_x2, lifted2, jump2, lift2):
    jump, lift = chain_jumps(image_x2[...], lambda s: lifted2[:, s].astype(F32), (n0, n1, n2, n3))
    jump2[...] = jump
    top, low = halves_of(lift)
    lift2[:NCO] = top
    lift2[NCO:] = low


def plane0_kernel(keep, got, g2, out):
    pieces = [high_low(keep[NCO:] + got[NCO:]), high_low(g2[...])]
    zero = jnp.zeros((4, NCO), F32)
    for p in range(16):
        rows = slice(16 * p, 16 * p + 16)
        small = [piece[part][p : p + 1] for part in range(2) for piece in pieces]
        out[p] = jnp.concatenate([keep[rows] + got[rows], *small, zero], axis=0).astype(BF16)


def summed(got):
    total = got[0].astype(F32)
    for p in range(1, got.shape[0]):
        total = total + got[p].astype(F32)
    return total


def depth0_kernel(got, own_row, out):
    total = summed(got)
    g = total[16:18] + total[18:20]
    rows = [total[:16], *high_low(g), *high_low(own_row[:1]), jnp.zeros((2, NCO), F32)]
    value = jnp.concatenate(rows, axis=0).astype(BF16)
    for q in range(8):
        out[q] = value


def spread0_kernel(got, out):
    every = [got[q].astype(F32) for q in range(8)]
    total = functools.reduce(jnp.add, every)
    g = total[16:18] + total[18:20]
    rows = [total[:16], *high_low(g), jnp.zeros((4, NCO), F32)]
    rows += [r[20:21] for r in every] + [r[21:22] for r in every]
    value = jnp.concatenate(rows, axis=0).astype(BF16)
    for p in range(16):
        out[p] = value


def collect0_kernel(got, out):
    g = []
    for p in range(16):
        out[16 * p : 16 * p + 16] = got[p, :16]
        g.append(got[p, 16:24].astype(F32))
        out[320 + 8 * p : 328 + 8 * p] = got[p, 24:32]
        out[448 + 8 * p : 456 + 8 * p] = got[p, 32:40]
    out[256:320] = jnp.concatenate([r[i : i + 1] for i in range(4) for r in g], axis=0).astype(BF16)


def terms_in(coef, width):
    return coef[0:1, :width], coef[1:2, :width], coef[2:3, :width]


def march_kernel(
    coef, own, got, load0, base1, jump0, jump1, jump2, chain2, spread, wide_in, chain1_hbm, inverse_hbm,
    coarse, m0, w0, w1, w2, load1, load2, load3, image3, low_sub, low_grp, m1, g1, g2, chain1, inverse, sems,
):
    table = pltpu.make_async_copy(chain1_hbm, chain1, sems.at[0])
    table.start()
    fetch = pltpu.make_async_copy(inverse_hbm, inverse, sems.at[1])
    fetch.start()

    def put(first, second):
        for half, part in ((slice(0, 128), first), (slice(128, 256), second)):
            coarse[half] = part[320:448].astype(F32) + part[448:576].astype(F32)
        m0[...] = first[:NCO]
        m1[...] = second[:NCO]
        w0[...] = first[256:272].astype(F32) + first[288:304].astype(F32)
        g1[...] = second[256:272].astype(F32) + second[288:304].astype(F32)
        parts = [part[i : i + RHS].astype(F32) for part in (first, second) for i in (272, 304)]
        g2[...] = functools.reduce(jnp.add, parts)

    on_core(lambda: put(own, got), lambda: put(got, own))
    centre, inv, alpha = terms_in(coef, NCO)
    w = w0[...]
    z = hdot(w, coarse[...])
    after = (g1[...] + dot2(z, m0[...]) - centre * w) * inv
    w1[...] = after
    z1 = hdot(after, coarse[...])
    image = (g2[...] + dot2(z, m1[...]) - centre * g1[...]) * inv
    last = alpha * (image + dot2(z1, m0[...]) - centre * after) - w
    w2[...] = last
    z2 = hdot(last, coarse[...])
    both = jnp.concatenate([z, z1, z2], axis=0)
    lift = lifted(both, wide_in[...], spread[:, :SLOTS])
    far = dot_halves(z, chain2[...])
    table.wait()
    near = dot_halves(both[: 2 * RHS], chain1[...])
    centre, inv, alpha = terms_in(coef, WIDTH)
    x1 = base1[...] + inv * lift[:RHS]
    load1[...] = x1
    j1 = inv * (jump1[...] + near[:RHS] - centre * jump0[...])
    x2 = alpha * (j1 + lift[RHS : 2 * RHS] - centre * x1) - load0[...]
    load2[...] = x2
    jj1 = inv * (jump2[...] + far - centre * jump1[...])
    j2 = alpha * (jj1 + near[RHS:] - centre * j1) - jump0[...]
    x3 = alpha * (j2 + lift[2 * RHS :] - centre * x2) - x1
    load3[...] = x3
    fetch.wait()
    u = bdot(x3.astype(BF16), inverse[...])
    image3[...] = u
    low_sub[...] = u[:, SEG[1]]
    low_grp[...] = u[:, SEG[3]]


def terms_kernel(coef, block, load1, load2, load3, image, spread, wide_in, stack, partial4, keep, send):
    centre, _, alpha = terms_in(coef, FACE)
    w, g = terms_of(load3[...], image[...], wide_in[...], spread[:, :SLOTS])
    left, right = slice(0, FACE), slice(FACE, 2 * FACE)
    stack[:RHS] = block[...]
    for level, load in ((1, load1), (2, load2), (3, load3)):
        stack[level * RHS : (level + 1) * RHS, left] = load[:, SEG[0]]
        stack[level * RHS : (level + 1) * RHS, right] = load[:, SEG[2]]
    for half, s in ((left, SEG[0]), (right, SEG[2])):
        partial4[:, half] = alpha * (image[:, s] - centre * load3[:, s]) - load2[:, s]
    known = jnp.concatenate([stack[...], jnp.zeros((64, 2 * FACE), F32)], axis=0)
    terms = hdot(stack[...], known, NT)
    t = [terms[i * RHS : (i + 1) * RHS] for i in range(BLOCKS - 1)]
    lane = lax.broadcasted_iota(jnp.int32, (RHS, 128), 1)
    first = jnp.where(lane < 64, t[0], pltpu.roll(t[1], 48, 1))
    second = jnp.where(lane < 32, pltpu.roll(t[2], 96, 1), pltpu.roll(t[3], 112, 1))
    split_by_core(
        jnp.concatenate([w, jnp.zeros((RHS, NCO), F32)], axis=0),
        jnp.concatenate([g, jnp.concatenate([first, second], axis=1)], axis=0),
        keep,
        send,
    )


def coded(total):
    zero = lax.axis_index("core") == 0
    return jnp.where(zero, jnp.concatenate(high_low(total[:RHS]), axis=0), total)


def decoded(total):
    zero = lax.axis_index("core") == 0
    whole = jnp.concatenate([total[:RHS] + total[RHS:], jnp.zeros((RHS, NCO), F32)], axis=0)
    return jnp.where(zero, whole, total)


def gram_kernel(coef, stack, partial4, n0, n2, keep, got, known4, out):
    _, _, alpha = terms_in(coef, FACE)
    known4[:, :FACE] = partial4[:, :FACE] - alpha * n0[...]
    known4[:, FACE:] = partial4[:, FACE:] - alpha * n2[...]
    q = known4[...]
    row = hdot(q, jnp.concatenate([stack[...], q, jnp.zeros((48, 2 * FACE), F32)], axis=0), NT)
    row = jnp.concatenate([row[:8], row[8:]], axis=1)
    value = jnp.concatenate([coded(keep[...] + got[...]), row], axis=0).astype(BF16)
    for p in range(16):
        out[p] = value


def depth1_kernel(got, out):
    total = summed(got)
    value = jnp.concatenate([coded(decoded(total[: 2 * RHS])), total[2 * RHS :]], axis=0).astype(BF16)
    for q in range(8):
        out[q] = value


def sum_kernel(got, out):
    total = summed(got)
    out[: 2 * RHS] = decoded(total[: 2 * RHS])
    out[2 * RHS :] = total[2 * RHS :]


def store_kernel(stack, basis_hbm, basis, sem):
    for level in range(BLOCKS - 1):
        basis[level] = stack[level * RHS : (level + 1) * RHS].reshape(RHS, 1, 1, 2 * FACE)
    copy = pltpu.make_async_copy(basis, basis_hbm.at[: BLOCKS - 1], sem)
    copy.start()
    copy.wait()


def final_kernel(
    coef, own, got, coarse, matrix, w0, w1, w2, known4, spread, wide_in, stored,
    basis_hbm, gram_hbm, block4, gram, square, sems,
):
    centre, _, alpha = terms_in(coef, NCO)
    zero = lax.axis_index("core") == 0
    w3 = jnp.where(zero, own[:RHS], got[:RHS])
    second = jnp.where(zero, got[: 2 * RHS], own[: 2 * RHS])
    g3, packed = second[:RHS], second[RHS:]
    row = own[2 * RHS :] + got[2 * RHS :]
    row = jnp.concatenate([row[:, :128], row[:, 128:]], axis=0)
    z3 = hdot(w3, coarse[...])
    lift = lifted(z3, wide_in[...], spread[:, :SLOTS])
    value = jnp.concatenate(
        [known4[:, :FACE] + alpha * lift[:, SEG[0]], known4[:, FACE:] + alpha * lift[:, SEG[2]]], axis=1
    )
    block4[...] = value.reshape(RHS, 1, 1, 2 * FACE)
    late = pltpu.make_async_copy(block4, basis_hbm.at[BLOCKS - 1], sems.at[0])
    late.start()
    wk = alpha * (g3 - centre * w3) - w2[...]
    z_row = jnp.concatenate([jnp.zeros((64, NCO), F32), z3, jnp.zeros((48, NCO), F32)], axis=0)
    rows = jnp.concatenate([w0[...], w1[...], w2[...], w3, wk, dot2(z3, matrix[...])], axis=0)
    cross = hdot(rows, z_row, NT)
    alpha = alpha[:, :128]
    h0, h1 = packed[:, :128], packed[:, 128:]
    parts = [h0, pltpu.roll(h0, 80, 1), pltpu.roll(h1, 32, 1), pltpu.roll(h1, 16, 1)]
    lane = lax.broadcasted_iota(jnp.int32, (RHS, 128), 1)
    for i in range(BLOCKS - 1):
        rows = slice(i * RHS, (i + 1) * RHS)
        square[rows] = jnp.where(lane < 64, parts[i], 0.0) + alpha * cross[rows]
    last = slice(4 * RHS, 5 * RHS)
    square[last] = alpha * alpha * cross[5 * RHS :] + jnp.where(lane < 64, 0.0, row)
    square[5 * RHS :] = jnp.zeros((48, 128), F32)
    own4 = jnp.where(lane < 64, row, alpha * cross[last])
    column = jnp.concatenate([jnp.zeros((64, 128), F32), own4, jnp.zeros((48, 128), F32)], axis=0)
    up = square[...]
    r = lax.broadcasted_iota(jnp.int32, (128, 128), 0) // RHS
    c = lax.broadcasted_iota(jnp.int32, (128, 128), 1) // RHS
    sided = jnp.where(r < c, up, 0.0) + column
    whole = jnp.where(r == c, up, 0.0) + sided + sided.T
    gram[...] = (whole * (1.0 / (2 * FACE * 64)))[: BLOCKS * RHS, : BLOCKS * RHS]
    result = pltpu.make_async_copy(gram, gram_hbm, sems.at[1])
    result.start()
    late.wait()
    result.wait()


def body(residual, bounds, local_inverse, corner_basis, corner_map, coarse_inverse):
    inverse = local_inverse.reshape(WIDTH, WIDTH)
    corners = corner_basis.reshape(-1, WIDTH)
    count = corners.shape[0]
    face = ((RHS, FACE), F32)
    load = ((RHS, WIDTH), F32)
    small = ((RHS, NCO), F32)
    half = ((RHS, 2 * FACE), F32)
    square = ((NCO, NCO), F32)
    blocks = ((BLOCKS, RHS, 1, 1, 2 * FACE), F32)
    hbm = pltpu.HBM

    *packs, labels, block, corners = call(
        pack_kernel,
        [((64, FACE), BF16)] * 4 + [((1, 256), jnp.int32), half, ((count, WIDTH), BF16)],
        [residual, corners, corner_map.reshape(1, count)],
        [hbm] * 3,
        [pltpu.VMEM((RHS, 1, 1, 2 * FACE), F32), pltpu.VMEM((1, count), jnp.int32), pltpu.VMEM((4, 64, FACE), BF16),
         pltpu.SemaphoreType.DMA((3,))],
    )
    near = neighbours(packs)
    inverse, coef, own_row = call(
        fetch_kernel,
        [((WIDTH, WIDTH), BF16), ((8, WIDTH), F32), ((8, NCO), F32)],
        [bounds.reshape(1, 2), inverse, coarse_inverse],
        [hbm, hbm, hbm],
        [pltpu.VMEM((1, 2), F32), pltpu.VMEM((1, NCO), F32), pltpu.SemaphoreType.DMA((3,))],
    )
    load0, wide, spread, image0, *sends = call(
        start_kernel,
        [load, ((SLOTS, WIDTH), BF16), ((NCO, 256), BF16), load, face, face, face, face],
        [block, *near, corners, labels, inverse],
    )
    near0 = neighbours(sends)
    keep, send, lifted_image = call(
        moment_kernel,
        [((272, NCO), F32), ((272, NCO), F32), ((2 * NCO, WIDTH), BF16)],
        [load0, image0, wide, spread, inverse],
    )
    got = swapped(send)
    chain = ((2 * RHS + NCO, FACE), BF16)
    table = ((2 * NCO, WIDTH), BF16)
    base1, jump0, g2, image_x, *sends = call(
        join_kernel,
        [load, load, small, load, chain, chain, chain, chain],
        [coef, load0, *near0, image0, wide, spread, inverse, lifted_image],
    )
    (v,) = call(plane0_kernel, [((16, 24, NCO), BF16)], [keep, got, g2])
    near1 = neighbours(sends)
    (v,) = call(depth0_kernel, [((8, 24, NCO), BF16)], [exchange(v, PLANE), own_row])
    jump1, chain1, image_x2, lifted2, *sends = call(
        chain1_kernel,
        [load, table, load, ((NCO, WIDTH), BF16), chain, chain, chain, chain],
        [*near1, image_x, lifted_image, local_inverse.reshape(WIDTH, WIDTH)],
        [None] * 6 + [hbm],
        [pltpu.VMEM((WIDTH, WIDTH), BF16), pltpu.VMEM((2 * NCO, WIDTH), BF16), pltpu.VMEM((4, *chain[0]), BF16),
         pltpu.SemaphoreType.DMA((6,))],
        out_space=[None, hbm, None, None] + [hbm] * 4,
    )
    near2 = neighbours(sends)
    (v,) = call(spread0_kernel, [((16, 40, NCO), BF16)], [exchange(v, "z")])
    (own,) = call(collect0_kernel, [((576, NCO), BF16)], [exchange(v, PLANE)])
    jump2, chain2 = call(chain2_kernel, [load, table], [*near2, image_x2, lifted2])

    coarse, m0, w0, w1, w2, load1, load2, load3, image3, low_sub, low_grp = call(
        march_kernel,
        [square, ((NCO, NCO), BF16), small, small, small, load, load, load, load, face, face],
        [coef, own, swapped(own), load0, base1, jump0, jump1, jump2, chain2, spread, wide, chain1,
         local_inverse.reshape(WIDTH, WIDTH)],
        [None] * 11 + [hbm, hbm],
        [pltpu.VMEM((NCO, NCO), BF16), pltpu.VMEM((RHS, NCO), F32), pltpu.VMEM((RHS, NCO), F32),
         pltpu.VMEM((2 * NCO, WIDTH), BF16), pltpu.VMEM((WIDTH, WIDTH), BF16), pltpu.SemaphoreType.DMA((2,))],
    )
    n0 = along(low_sub, SUB, -1)
    n2 = along(low_grp, "x", -1)
    stack, partial4, keep, send = call(
        terms_kernel,
        [((4 * RHS, 2 * FACE), F32), half, ((32, NCO), F32), ((32, NCO), F32)],
        [coef, block, load1, load2, load3, image3, spread, wide],
    )
    got = swapped(send)
    known4, v = call(
        gram_kernel,
        [half, ((16, 40, NCO), BF16)],
        [coef, stack, partial4, n0, n2, keep, got],
    )
    (stored,) = call(
        store_kernel,
        [blocks],
        [stack],
        scratch=[pltpu.VMEM((BLOCKS - 1, RHS, 1, 1, 2 * FACE), F32), pltpu.SemaphoreType.DMA(())],
        out_space=hbm,
    )
    (v,) = call(depth1_kernel, [((8, 40, NCO), BF16)], [exchange(v, PLANE)])
    (own,) = call(sum_kernel, [((40, NCO), F32)], [exchange(v, "z")])
    basis, gram = call(
        final_kernel,
        [blocks, ((BLOCKS * RHS, BLOCKS * RHS), F32)],
        [coef, own, swapped(own), coarse, m0, w0, w1, w2, known4, spread, wide, stored],
        [None] * 11 + [hbm],
        [pltpu.VMEM((RHS, 1, 1, 2 * FACE), F32), pltpu.VMEM((BLOCKS * RHS, BLOCKS * RHS), F32),
         pltpu.VMEM((128, 128), F32), pltpu.SemaphoreType.DMA((2,))],
        out_space=hbm,
        aliases={11: 0},
    )
    return basis, gram


def solution(mesh):
    split = Mesh(mesh.devices.reshape(8, 4, 2, mesh.shape["grp"]), ("z", "y", "core", "x"))
    in_specs = (
        P(None, SUB, "x", None),
        P(),
        P(SUB, "x", None, None),
        P(SUB, "x", None, None),
        P(SUB, "x", None),
        P(("z", "y", "core", "x"), None),
    )
    out_specs = (P(None, None, SUB, "x", None), P())
    return jax.shard_map(body, mesh=split, in_specs=in_specs, out_specs=out_specs, check_vma=False)
```

```python
import functools

import jax
import jax.numpy as jnp
from jax import lax
from jax.experimental import pallas as pl
from jax.experimental.pallas import tpu as pltpu
from jax.sharding import Mesh
from jax.sharding import PartitionSpec as P


BLOCKS = 5
RHS = 16
FACE = 256
WIDTH = 4 * FACE
NCO = 256
SLOT = 32
SLOTS = 5 * SLOT
SUB = ("z", "y", "core")
PLANE = ("y", "x")
HIGH = lax.Precision.HIGHEST
F32, BF16 = jnp.float32, jnp.bfloat16
SEG = [slice(i * FACE, (i + 1) * FACE) for i in range(4)]


NN = (((1,), (0,)), ((), ()))
NT = (((1,), (1,)), ((), ()))


def hdot(a, b, dims=NN):
    return lax.dot_general(a, b, dims, precision=HIGH, preferred_element_type=F32)


def bdot(a, b, dims=NN):
    return lax.dot_general(a, b, dims, preferred_element_type=F32)


def halves_of(a):
    top = a.astype(BF16)
    return top, (a - top.astype(F32)).astype(BF16)


def dot_halves(a, table):
    rows = table.shape[0] // 2
    return dot2(a, table[:rows]) + bdot(a.astype(BF16), table[rows:])


def dot2(a, exact, dims=NN):
    rows = a.shape[0]
    top = a.astype(BF16)
    low = (a - top.astype(F32)).astype(BF16)
    got = bdot(jnp.concatenate([top, low], axis=0), exact, dims)
    return got[:rows] + got[rows:]


def call(kernel, outs, args, spaces=None, scratch=(), limit=20, out_space=None, aliases=None):
    vmem = pl.BlockSpec(memory_space=pltpu.VMEM)
    out_spaces = out_space if isinstance(out_space, list) else [out_space] * len(outs)
    out_specs = [vmem if s is None else pl.BlockSpec(memory_space=s) for s in out_spaces]
    specs = [vmem if s is None else pl.BlockSpec(memory_space=s) for s in (spaces or [None] * len(args))]
    if spaces:
        args = [
            pltpu.with_memory_space_constraint(a, pltpu.HBM) if s is pltpu.HBM else a for a, s in zip(args, spaces)
        ]
    run = pl.pallas_call(
        kernel,
        out_shape=[
            pltpu.HBM(s, d) if space is pltpu.HBM else jax.ShapeDtypeStruct(s, d)
            for (s, d), space in zip(outs, out_spaces)
        ],
        in_specs=specs,
        out_specs=out_specs,
        scratch_shapes=list(scratch),
        input_output_aliases=aliases or {},
        compiler_params=pltpu.CompilerParams(vmem_limit_bytes=limit << 20),
    )
    return run(*args)


def along(x, axis, by):
    count = lax.axis_size(axis)
    return lax.ppermute(x, axis, [(i, (i + by) % count) for i in range(count)])


def exchange(x, axis):
    return lax.all_to_all(x, axis, split_axis=0, concat_axis=0, tiled=True)


def swapped(v):
    return along(v, "core", 1)


def in_pairs(v, axis, first):
    count = lax.axis_size(axis)
    pairs = []
    for i in range(first, first + count, 2):
        a, b = i % count, (i + 1) % count
        pairs += [(a, b), (b, a)]
    return lax.ppermute(v, axis, pairs)


def neighbours(sends):
    return [in_pairs(sends[0], SUB, 1), in_pairs(sends[1], "x", 1), in_pairs(sends[2], "x", 0), swapped(sends[3])]


def label_of(n):
    return ((n // 4) % 2) * 128 + ((n // 8) % 4 * 4 + n % 4) * 8 + n // 32


def pack_kernel(
    block_hbm, corners_hbm, ids_hbm,
    s0, s1, s2, s3, labels, block, corners, wide_block, given, packs, sems,
):
    copies = [
        pltpu.make_async_copy(src, dst, sems.at[i])
        for i, (src, dst) in enumerate(
            ((block_hbm, wide_block), (corners_hbm, corners), (ids_hbm, given))
        )
    ]
    for copy in copies:
        copy.start()
    for copy in copies:
        copy.wait()
    count = corners.shape[0]
    labels[...] = jnp.full((1, 256), -1, jnp.int32)
    labels[:, :count] = label_of(given[...])
    text = labels[...].astype(F32).astype(BF16)
    x = wide_block[...].reshape(RHS, 2 * FACE)
    block[...] = x
    top = x.astype(BF16)
    rest = (x - top.astype(F32)).astype(BF16)
    for i, s in enumerate(SEG):
        if i % 2 == 0:
            packs[i, :RHS] = top[:, SEG[i // 2]]
            packs[i, RHS : 2 * RHS] = rest[:, SEG[i // 2]]
        else:
            packs[i, : 2 * RHS] = jnp.zeros((2 * RHS, FACE), BF16)
        packs[i, 2 * RHS : 2 * RHS + count] = corners[:, s]
        packs[i, 2 * RHS + count :] = jnp.broadcast_to(text, (8, FACE))
    put_sends([packs[i] for i in range(4)], (s0, s1, s2, s3))


def terms_of(load, u, wide, spread_t):
    both = dot2(dot2(jnp.concatenate([load * 0.5, u], axis=0), wide, NT), spread_t, NT)
    return both[:RHS], both[RHS:]


def lifted(z, wide, spread_t):
    return dot2(dot2(z, spread_t), wide)


def either(axis, even_branch, odd_branch):
    even = lax.axis_index(axis) % 2 == 0
    pl.when(even)(even_branch)
    pl.when(jnp.logical_not(even))(odd_branch)


def on_core(zero_branch, other_branch):
    either("core", zero_branch, other_branch)


def put_pair(axis, up, low, first, second):
    def even():
        first[...] = up
        second[...] = low

    def odd():
        first[...] = low
        second[...] = up

    either(axis, even, odd)


def put_sends(faces, outs):
    put_pair("core", faces[0], faces[1], outs[3], outs[0])
    put_pair("x", faces[2], faces[3], outs[2], outs[1])


def put_image(u, out, sends):
    out[...] = u
    put_sends([u[:, s] for s in SEG], sends)


def arrived(refs):
    values = [r[...] for r in refs]
    if values[0].dtype != F32:
        values = [v.astype(F32) for v in values]
    zero, even = lax.axis_index("core") == 0, lax.axis_index("x") % 2 == 0
    return [
        jnp.where(zero, values[3], values[0]),
        jnp.where(zero, values[0], values[3]),
        jnp.where(even, values[2], values[1]),
        jnp.where(even, values[1], values[2]),
    ]


def split_by_core(first, second, keep, send):
    def zero():
        keep[...] = first
        send[...] = second

    def one():
        keep[...] = second
        send[...] = first

    on_core(zero, one)


def high_low(x):
    top = x.astype(BF16).astype(F32)
    return top, x - top


def start_kernel(
    block, r0, r1, r2, r3, corners, labels, inverse, load_out, wide_out, spread_out, image, s0, s1, s2, s3,
):
    count = corners.shape[0]
    k = 2 * RHS
    next_sub, prev_sub, next_grp, prev_grp = arrived((r0, r1, r2, r3))
    load_out[:, SEG[0]] = block[:, :FACE]
    load_out[:, SEG[1]] = -(prev_sub[:RHS] + prev_sub[RHS:k])
    load_out[:, SEG[2]] = block[:, FACE:]
    load_out[:, SEG[3]] = -(prev_grp[:RHS] + prev_grp[RHS:k])
    put_image(dot2(load_out[...], inverse[...]), image, (s0, s1, s2, s3))
    wide_out[...] = jnp.zeros((SLOTS, WIDTH), BF16)
    wide_out[:count] = corners[...]
    others = (next_sub, prev_sub, next_grp, prev_grp)
    for i, other in enumerate(others):
        wide_out[SLOT * (i + 1) : SLOT * (i + 1) + count, SEG[i]] = (-other[k : k + count]).astype(BF16)
    lane = lax.broadcasted_iota(jnp.int32, (8, 256), 1)
    ids = jnp.where(lane < SLOT, jnp.broadcast_to(labels[...], (8, 256)).astype(F32), -1.0)
    for i, other in enumerate(others):
        moved = pltpu.roll(other[k + count :], SLOT * (i + 1), 1)
        mine = jnp.logical_and(lane >= SLOT * (i + 1), lane < SLOT * (i + 2))
        ids = jnp.where(mine, moved, ids)
    number = lax.broadcasted_iota(jnp.int32, (NCO, 256), 0).astype(F32)
    spread_out[...] = (number == ids[:1]).astype(F32).astype(BF16)


def fetch_kernel(bounds_hbm, inverse_hbm, row_hbm, out, coef, own_row, bounds, row, sems):
    limits = pltpu.make_async_copy(bounds_hbm, bounds, sems.at[2])
    limits.start()
    copy = pltpu.make_async_copy(row_hbm, row, sems.at[1])
    copy.start()
    fetch = pltpu.make_async_copy(inverse_hbm, out, sems.at[0])
    fetch.start()
    limits.wait()
    low, high = bounds[:, 0:1], bounds[:, 1:2]
    centre = jnp.broadcast_to((low + high) * 0.5, (1, WIDTH))
    inv = 1.0 / jnp.broadcast_to((high - low) * 0.5, (1, WIDTH))
    coef[...] = jnp.concatenate([centre, inv, 2.0 * inv, jnp.zeros((5, WIDTH), F32)], axis=0)
    n = lax.broadcasted_iota(jnp.int32, (NCO, NCO), 0)
    m = lax.broadcasted_iota(jnp.int32, (NCO, NCO), 1)
    order = (label_of(n) == m).astype(F32).astype(BF16)
    copy.wait()
    own_row[...] = dot2(jnp.broadcast_to(row[...], (RHS, NCO)), order)[:8]
    fetch.wait()


def moment_kernel(load0, image, wide_in, spread, inverse, keep, send, lifted_image):
    wide, spread_t = wide_in[...], spread[:, :SLOTS]
    pairs0 = bdot(wide, wide, NT) * 0.5
    wide_image = bdot(wide, inverse[...])
    top, low = halves_of(wide_image)
    top, low = halves_of(bdot(spread_t, top) + bdot(spread_t, low))
    lifted_image[:NCO] = top
    lifted_image[NCO:] = low
    pairs1 = dot2(wide_image, wide, NT)
    half = dot2(jnp.concatenate([pairs0, pairs1], axis=0), spread_t, NT)
    half = jnp.concatenate([half[:SLOTS], half[SLOTS:]], axis=1)
    top = half.astype(BF16)
    low = (half - top.astype(F32)).astype(BF16)
    both = bdot(spread_t, jnp.concatenate([top, low], axis=1))
    both = both[:, : 2 * NCO] + both[:, 2 * NCO :]
    w, g = terms_of(load0[...], image[...], wide, spread_t)

    def put(first, second):
        first[:NCO] = both[:, :NCO]
        first[NCO:] = w
        second[:NCO] = both[:, NCO:]
        second[NCO:] = g

    on_core(lambda: put(keep, send), lambda: put(send, keep))


def jumped(image, near):
    return [image[:, s] - n for s, n in zip(SEG, arrived(near), strict=True)]


def put_chain(u, lifts, sends):
    top = u.astype(BF16)
    low = (u - top.astype(F32)).astype(BF16)
    put_sends([jnp.concatenate([top[:, s], low[:, s], lifts[:, s]], axis=0) for s in SEG], sends)


def chain_jumps(u, own_lift, near):
    far = arrived(near)
    jump = jnp.concatenate([u[:, s] - (n[:RHS] + n[RHS : 2 * RHS]) for s, n in zip(SEG, far, strict=True)], axis=1)
    lift = [own_lift(s) - n[2 * RHS :] for s, n in zip(SEG, far, strict=True)]
    return jump, jnp.concatenate(lift, axis=1)


def join_kernel(
    coef, load0, n0, n1, n2, n3, image, wide_in, spread, inverse, lifted_image, keep, got,
    base1, jump0, image_x, s0, s1, s2, s3, out_hbm, out, sem,
):
    centre, inv, _ = terms_in(coef, WIDTH)
    jump = jnp.concatenate(jumped(image, (n0, n1, n2, n3)), axis=1)
    u = dot2(jump, inverse[...])
    g2 = dot2(dot2(u, wide_in[...], NT), spread[:, :SLOTS], NT)
    pieces = [high_low(keep[NCO:] + got[NCO:]), high_low(g2)]
    zero = jnp.zeros((4, NCO), F32)
    for p in range(16):
        rows = slice(16 * p, 16 * p + 16)
        small = [piece[part][p : p + 1] for part in range(2) for piece in pieces]
        out[p] = jnp.concatenate([keep[rows] + got[rows], *small, zero], axis=0).astype(BF16)
    copy = pltpu.make_async_copy(out, out_hbm, sem)
    copy.start()
    jump0[...] = jump
    base1[...] = (jump - centre * load0[...]) * inv
    image_x[...] = u
    put_chain(u, lifted_image[:NCO], (s0, s1, s2, s3))
    copy.wait()


def chain1_kernel(
    n0, n1, n2, n3, image_x, lifted_image, inverse_hbm,
    jump1, lift1_hbm, image_x2, lifted2, s0, s1, s2, s3, inverse, lift1, sends, sems,
):
    fetch = pltpu.make_async_copy(inverse_hbm, inverse, sems.at[0])
    fetch.start()

    def own_lift(s):
        return lifted_image[:NCO, s].astype(F32) + lifted_image[NCO:, s].astype(F32)

    jump, lift = chain_jumps(image_x[...], own_lift, (n0, n1, n2, n3))
    jump1[...] = jump
    top, low = halves_of(lift)
    lift1[:NCO] = top
    lift1[NCO:] = low
    store = pltpu.make_async_copy(lift1, lift1_hbm, sems.at[1])
    store.start()
    fetch.wait()
    u = dot2(jump, inverse[...])
    image_x2[...] = u
    lifts = bdot(top, inverse[...]).astype(BF16)
    put_chain(u, lifts, [sends.at[i] for i in range(4)])
    copies = [pltpu.make_async_copy(sends.at[i], s, sems.at[i + 2]) for i, s in enumerate((s0, s1, s2, s3))]
    for copy in copies:
        copy.start()
    lifted2[...] = lifts
    store.wait()
    for copy in copies:
        copy.wait()


def chain2_kernel(n0, n1, n2, n3, image_x2, lifted2, jump2, lift2):
    jump, lift = chain_jumps(image_x2[...], lambda s: lifted2[:, s].astype(F32), (n0, n1, n2, n3))
    jump2[...] = jump
    top, low = halves_of(lift)
    lift2[:NCO] = top
    lift2[NCO:] = low


def summed(got):
    total = got[0].astype(F32)
    for p in range(1, got.shape[0]):
        total = total + got[p].astype(F32)
    return total


def depth0_kernel(got, own_row, out):
    total = summed(got)
    g = total[16:18] + total[18:20]
    rows = [total[:16], *high_low(g), *high_low(own_row[:1]), jnp.zeros((2, NCO), F32)]
    value = jnp.concatenate(rows, axis=0).astype(BF16)
    for q in range(8):
        out[q] = value


def spread0_kernel(got, out):
    every = [got[q].astype(F32) for q in range(8)]
    total = functools.reduce(jnp.add, every)
    g = total[16:18] + total[18:20]
    rows = [total[:16], *high_low(g), jnp.zeros((4, NCO), F32)]
    rows += [r[20:21] for r in every] + [r[21:22] for r in every]
    value = jnp.concatenate(rows, axis=0).astype(BF16)
    for p in range(16):
        out[p] = value


def collect0_kernel(got, out):
    g = []
    for p in range(16):
        out[16 * p : 16 * p + 16] = got[p, :16]
        g.append(got[p, 16:24].astype(F32))
        out[320 + 8 * p : 328 + 8 * p] = got[p, 24:32]
        out[448 + 8 * p : 456 + 8 * p] = got[p, 32:40]
    out[256:320] = jnp.concatenate([r[i : i + 1] for i in range(4) for r in g], axis=0).astype(BF16)


def terms_in(coef, width):
    return coef[0:1, :width], coef[1:2, :width], coef[2:3, :width]


def march_kernel(
    coef, own, got, load0, base1, jump0, jump1, jump2, chain2, spread, wide_in, chain1_hbm, inverse_hbm,
    coarse, m0, w0, w1, w2, load1, load2, load3, image3, low_sub, low_grp, m1, g1, g2, chain1, inverse, sems,
):
    table = pltpu.make_async_copy(chain1_hbm, chain1, sems.at[0])
    table.start()
    fetch = pltpu.make_async_copy(inverse_hbm, inverse, sems.at[1])
    fetch.start()

    def put(first, second):
        for row, part in ((0, first), (128, second)):
            coarse[row : row + 128] = part[320:448]
            coarse[NCO + row : NCO + row + 128] = part[448:576]
        m0[...] = first[:NCO]
        m1[...] = second[:NCO]
        w0[...] = first[256:272].astype(F32) + first[288:304].astype(F32)
        g1[...] = second[256:272].astype(F32) + second[288:304].astype(F32)
        parts = [part[i : i + RHS].astype(F32) for part in (first, second) for i in (272, 304)]
        g2[...] = functools.reduce(jnp.add, parts)

    on_core(lambda: put(own, got), lambda: put(got, own))
    centre, inv, alpha = terms_in(coef, NCO)
    w = w0[...]
    z = dot_halves(w, coarse[...])
    after = (g1[...] + dot2(z, m0[...]) - centre * w) * inv
    w1[...] = after
    z1 = dot_halves(after, coarse[...])
    image = (g2[...] + dot2(z, m1[...]) - centre * g1[...]) * inv
    last = alpha * (image + dot2(z1, m0[...]) - centre * after) - w
    w2[...] = last
    z2 = dot_halves(last, coarse[...])
    both = jnp.concatenate([z, z1, z2], axis=0)
    lift = lifted(both, wide_in[...], spread[:, :SLOTS])
    far = dot_halves(z, chain2[...])
    table.wait()
    near = dot_halves(both[: 2 * RHS], chain1[...])
    centre, inv, alpha = terms_in(coef, WIDTH)
    x1 = base1[...] + inv * lift[:RHS]
    load1[...] = x1
    j1 = inv * (jump1[...] + near[:RHS] - centre * jump0[...])
    x2 = alpha * (j1 + lift[RHS : 2 * RHS] - centre * x1) - load0[...]
    load2[...] = x2
    jj1 = inv * (jump2[...] + far - centre * jump1[...])
    j2 = alpha * (jj1 + near[RHS:] - centre * j1) - jump0[...]
    x3 = alpha * (j2 + lift[2 * RHS :] - centre * x2) - x1
    load3[...] = x3
    fetch.wait()
    u = bdot(x3.astype(BF16), inverse[...])
    image3[...] = u
    low_sub[...] = u[:, SEG[1]]
    low_grp[...] = u[:, SEG[3]]


def terms_kernel(coef, block, load1, load2, load3, image, spread, wide_in, stack, partial4, keep, send):
    centre, _, alpha = terms_in(coef, FACE)
    w, g = terms_of(load3[...], image[...], wide_in[...], spread[:, :SLOTS])
    left, right = slice(0, FACE), slice(FACE, 2 * FACE)
    stack[:RHS] = block[...]
    for level, load in ((1, load1), (2, load2), (3, load3)):
        stack[level * RHS : (level + 1) * RHS, left] = load[:, SEG[0]]
        stack[level * RHS : (level + 1) * RHS, right] = load[:, SEG[2]]
    for half, s in ((left, SEG[0]), (right, SEG[2])):
        partial4[:, half] = alpha * (image[:, s] - centre * load3[:, s]) - load2[:, s]
    known = jnp.concatenate([stack[...], jnp.zeros((64, 2 * FACE), F32)], axis=0)
    terms = hdot(stack[...], known, NT)
    t = [terms[i * RHS : (i + 1) * RHS] for i in range(BLOCKS - 1)]
    lane = lax.broadcasted_iota(jnp.int32, (RHS, 128), 1)
    first = jnp.where(lane < 64, t[0], pltpu.roll(t[1], 48, 1))
    second = jnp.where(lane < 32, pltpu.roll(t[2], 96, 1), pltpu.roll(t[3], 112, 1))
    split_by_core(
        jnp.concatenate([w, jnp.zeros((RHS, NCO), F32)], axis=0),
        jnp.concatenate([g, jnp.concatenate([first, second], axis=1)], axis=0),
        keep,
        send,
    )


def coded(total):
    zero = lax.axis_index("core") == 0
    return jnp.where(zero, jnp.concatenate(high_low(total[:RHS]), axis=0), total)


def decoded(total):
    zero = lax.axis_index("core") == 0
    whole = jnp.concatenate([total[:RHS] + total[RHS:], jnp.zeros((RHS, NCO), F32)], axis=0)
    return jnp.where(zero, whole, total)


def gram_kernel(coef, stack, partial4, n0, n2, keep, got, known4, out):
    _, _, alpha = terms_in(coef, FACE)
    known4[:, :FACE] = partial4[:, :FACE] - alpha * n0[...]
    known4[:, FACE:] = partial4[:, FACE:] - alpha * n2[...]
    q = known4[...]
    row = hdot(q, jnp.concatenate([stack[...], q, jnp.zeros((48, 2 * FACE), F32)], axis=0), NT)
    row = jnp.concatenate([row[:8], row[8:]], axis=1)
    value = jnp.concatenate([coded(keep[...] + got[...]), row], axis=0).astype(BF16)
    for p in range(16):
        out[p] = value


def depth1_kernel(got, out):
    total = summed(got)
    value = jnp.concatenate([coded(decoded(total[: 2 * RHS])), total[2 * RHS :]], axis=0).astype(BF16)
    for q in range(8):
        out[q] = value


def sum_kernel(got, out):
    total = summed(got)
    out[: 2 * RHS] = decoded(total[: 2 * RHS])
    out[2 * RHS :] = total[2 * RHS :]


def store_kernel(stack, basis_hbm, basis, sem):
    for level in range(BLOCKS - 1):
        basis[level] = stack[level * RHS : (level + 1) * RHS].reshape(RHS, 1, 1, 2 * FACE)
    copy = pltpu.make_async_copy(basis, basis_hbm.at[: BLOCKS - 1], sem)
    copy.start()
    copy.wait()


def final_kernel(
    coef, own, got, coarse, matrix, w0, w1, w2, known4, spread, wide_in, stored,
    basis_hbm, gram_hbm, block4, gram, square, sems,
):
    centre, _, alpha = terms_in(coef, NCO)
    zero = lax.axis_index("core") == 0
    w3 = jnp.where(zero, own[:RHS], got[:RHS])
    second = jnp.where(zero, got[: 2 * RHS], own[: 2 * RHS])
    g3, packed = second[:RHS], second[RHS:]
    row = own[2 * RHS :] + got[2 * RHS :]
    row = jnp.concatenate([row[:, :128], row[:, 128:]], axis=0)
    z3 = dot_halves(w3, coarse[...])
    lift = lifted(z3, wide_in[...], spread[:, :SLOTS])
    value = jnp.concatenate(
        [known4[:, :FACE] + alpha * lift[:, SEG[0]], known4[:, FACE:] + alpha * lift[:, SEG[2]]], axis=1
    )
    block4[...] = value.reshape(RHS, 1, 1, 2 * FACE)
    late = pltpu.make_async_copy(block4, basis_hbm.at[BLOCKS - 1], sems.at[0])
    late.start()
    wk = alpha * (g3 - centre * w3) - w2[...]
    z_row = jnp.concatenate([jnp.zeros((64, NCO), F32), z3, jnp.zeros((48, NCO), F32)], axis=0)
    rows = jnp.concatenate([w0[...], w1[...], w2[...], w3, wk, dot2(z3, matrix[...])], axis=0)
    cross = hdot(rows, z_row, NT)
    alpha = alpha[:, :128]
    h0, h1 = packed[:, :128], packed[:, 128:]
    parts = [h0, pltpu.roll(h0, 80, 1), pltpu.roll(h1, 32, 1), pltpu.roll(h1, 16, 1)]
    lane = lax.broadcasted_iota(jnp.int32, (RHS, 128), 1)
    for i in range(BLOCKS - 1):
        rows = slice(i * RHS, (i + 1) * RHS)
        square[rows] = jnp.where(lane < 64, parts[i], 0.0) + alpha * cross[rows]
    last = slice(4 * RHS, 5 * RHS)
    square[last] = alpha * alpha * cross[5 * RHS :] + jnp.where(lane < 64, 0.0, row)
    square[5 * RHS :] = jnp.zeros((48, 128), F32)
    own4 = jnp.where(lane < 64, row, alpha * cross[last])
    column = jnp.concatenate([jnp.zeros((64, 128), F32), own4, jnp.zeros((48, 128), F32)], axis=0)
    up = square[...]
    r = lax.broadcasted_iota(jnp.int32, (128, 128), 0) // RHS
    c = lax.broadcasted_iota(jnp.int32, (128, 128), 1) // RHS
    sided = jnp.where(r < c, up, 0.0) + column
    whole = jnp.where(r == c, up, 0.0) + sided + sided.T
    gram[...] = (whole * (1.0 / (2 * FACE * 64)))[: BLOCKS * RHS, : BLOCKS * RHS]
    result = pltpu.make_async_copy(gram, gram_hbm, sems.at[1])
    result.start()
    late.wait()
    result.wait()


def body(residual, bounds, local_inverse, corner_basis, corner_map, coarse_inverse):
    inverse = local_inverse.reshape(WIDTH, WIDTH)
    corners = corner_basis.reshape(-1, WIDTH)
    count = corners.shape[0]
    face = ((RHS, FACE), F32)
    load = ((RHS, WIDTH), F32)
    small = ((RHS, NCO), F32)
    half = ((RHS, 2 * FACE), F32)
    blocks = ((BLOCKS, RHS, 1, 1, 2 * FACE), F32)
    hbm = pltpu.HBM

    *packs, labels, block, corners = call(
        pack_kernel,
        [((64, FACE), BF16)] * 4 + [((1, 256), jnp.int32), half, ((count, WIDTH), BF16)],
        [residual, corners, corner_map.reshape(1, count)],
        [hbm] * 3,
        [pltpu.VMEM((RHS, 1, 1, 2 * FACE), F32), pltpu.VMEM((1, count), jnp.int32), pltpu.VMEM((4, 64, FACE), BF16),
         pltpu.SemaphoreType.DMA((3,))],
    )
    near = neighbours(packs)
    inverse, coef, own_row = call(
        fetch_kernel,
        [((WIDTH, WIDTH), BF16), ((8, WIDTH), F32), ((8, NCO), F32)],
        [bounds.reshape(1, 2), inverse, coarse_inverse],
        [hbm, hbm, hbm],
        [pltpu.VMEM((1, 2), F32), pltpu.VMEM((1, NCO), F32), pltpu.SemaphoreType.DMA((3,))],
    )
    load0, wide, spread, image0, *sends = call(
        start_kernel,
        [load, ((SLOTS, WIDTH), BF16), ((NCO, 256), BF16), load, face, face, face, face],
        [block, *near, corners, labels, inverse],
    )
    near0 = neighbours(sends)
    keep, send, lifted_image = call(
        moment_kernel,
        [((272, NCO), F32), ((272, NCO), F32), ((2 * NCO, WIDTH), BF16)],
        [load0, image0, wide, spread, inverse],
    )
    got = swapped(send)
    chain = ((2 * RHS + NCO, FACE), BF16)
    table = ((2 * NCO, WIDTH), BF16)
    base1, jump0, image_x, *sends, v = call(
        join_kernel,
        [load, load, load, chain, chain, chain, chain, ((16, 24, NCO), BF16)],
        [coef, load0, *near0, image0, wide, spread, inverse, lifted_image, keep, got],
        scratch=[pltpu.VMEM((16, 24, NCO), BF16), pltpu.SemaphoreType.DMA(())],
        out_space=[None] * 7 + [hbm],
    )
    near1 = neighbours(sends)
    (v,) = call(depth0_kernel, [((8, 24, NCO), BF16)], [exchange(v, PLANE), own_row])
    jump1, chain1, image_x2, lifted2, *sends = call(
        chain1_kernel,
        [load, table, load, ((NCO, WIDTH), BF16), chain, chain, chain, chain],
        [*near1, image_x, lifted_image, local_inverse.reshape(WIDTH, WIDTH)],
        [None] * 6 + [hbm],
        [pltpu.VMEM((WIDTH, WIDTH), BF16), pltpu.VMEM((2 * NCO, WIDTH), BF16), pltpu.VMEM((4, *chain[0]), BF16),
         pltpu.SemaphoreType.DMA((6,))],
        out_space=[None, hbm, None, None] + [hbm] * 4,
    )
    near2 = neighbours(sends)
    (v,) = call(spread0_kernel, [((16, 40, NCO), BF16)], [exchange(v, "z")])
    (own,) = call(collect0_kernel, [((576, NCO), BF16)], [exchange(v, PLANE)])
    jump2, chain2 = call(chain2_kernel, [load, table], [*near2, image_x2, lifted2])

    coarse, m0, w0, w1, w2, load1, load2, load3, image3, low_sub, low_grp = call(
        march_kernel,
        [((2 * NCO, NCO), BF16), ((NCO, NCO), BF16), small, small, small, load, load, load, load, face, face],
        [coef, own, swapped(own), load0, base1, jump0, jump1, jump2, chain2, spread, wide, chain1,
         local_inverse.reshape(WIDTH, WIDTH)],
        [None] * 11 + [hbm, hbm],
        [pltpu.VMEM((NCO, NCO), BF16), pltpu.VMEM((RHS, NCO), F32), pltpu.VMEM((RHS, NCO), F32),
         pltpu.VMEM((2 * NCO, WIDTH), BF16), pltpu.VMEM((WIDTH, WIDTH), BF16), pltpu.SemaphoreType.DMA((2,))],
    )
    n0 = along(low_sub, SUB, -1)
    n2 = along(low_grp, "x", -1)
    stack, partial4, keep, send = call(
        terms_kernel,
        [((4 * RHS, 2 * FACE), F32), half, ((32, NCO), F32), ((32, NCO), F32)],
        [coef, block, load1, load2, load3, image3, spread, wide],
    )
    got = swapped(send)
    known4, v = call(
        gram_kernel,
        [half, ((16, 40, NCO), BF16)],
        [coef, stack, partial4, n0, n2, keep, got],
    )
    (stored,) = call(
        store_kernel,
        [blocks],
        [stack],
        scratch=[pltpu.VMEM((BLOCKS - 1, RHS, 1, 1, 2 * FACE), F32), pltpu.SemaphoreType.DMA(())],
        out_space=hbm,
    )
    (v,) = call(depth1_kernel, [((8, 40, NCO), BF16)], [exchange(v, PLANE)])
    (own,) = call(sum_kernel, [((40, NCO), F32)], [exchange(v, "z")])
    basis, gram = call(
        final_kernel,
        [blocks, ((BLOCKS * RHS, BLOCKS * RHS), F32)],
        [coef, own, swapped(own), coarse, m0, w0, w1, w2, known4, spread, wide, stored],
        [None] * 11 + [hbm],
        [pltpu.VMEM((RHS, 1, 1, 2 * FACE), F32), pltpu.VMEM((BLOCKS * RHS, BLOCKS * RHS), F32),
         pltpu.VMEM((128, 128), F32), pltpu.SemaphoreType.DMA((2,))],
        out_space=hbm,
        aliases={11: 0},
    )
    return basis, gram


def solution(mesh):
    split = Mesh(mesh.devices.reshape(8, 4, 2, mesh.shape["grp"]), ("z", "y", "core", "x"))
    in_specs = (
        P(None, SUB, "x", None),
        P(),
        P(SUB, "x", None, None),
        P(SUB, "x", None, None),
        P(SUB, "x", None),
        P(("z", "y", "core", "x"), None),
    )
    out_specs = (P(None, None, SUB, "x", None), P())
    return jax.shard_map(body, mesh=split, in_specs=in_specs, out_specs=out_specs, check_vma=False)
```

```python
import functools

import jax
import jax.numpy as jnp
from jax import lax
from jax.experimental import pallas as pl
from jax.experimental.pallas import tpu as pltpu
from jax.sharding import Mesh
from jax.sharding import PartitionSpec as P


BLOCKS = 5
RHS = 16
FACE = 256
WIDTH = 4 * FACE
NCO = 256
SLOT = 32
SLOTS = 5 * SLOT
SUB = ("z", "y", "core")
PLANE = ("y", "x")
HIGH = lax.Precision.HIGHEST
F32, BF16 = jnp.float32, jnp.bfloat16
SEG = [slice(i * FACE, (i + 1) * FACE) for i in range(4)]


NN = (((1,), (0,)), ((), ()))
NT = (((1,), (1,)), ((), ()))


def hdot(a, b, dims=NN):
    return lax.dot_general(a, b, dims, precision=HIGH, preferred_element_type=F32)


def bdot(a, b, dims=NN):
    return lax.dot_general(a, b, dims, preferred_element_type=F32)


def halves_of(a):
    top = a.astype(BF16)
    return top, (a - top.astype(F32)).astype(BF16)


def dot_halves(a, table):
    rows = table.shape[0] // 2
    return dot2(a, table[:rows]) + bdot(a.astype(BF16), table[rows:])


def dot2(a, exact, dims=NN):
    rows = a.shape[0]
    top = a.astype(BF16)
    low = (a - top.astype(F32)).astype(BF16)
    got = bdot(jnp.concatenate([top, low], axis=0), exact, dims)
    return got[:rows] + got[rows:]


def call(kernel, outs, args, spaces=None, scratch=(), limit=20, out_space=None, aliases=None):
    vmem = pl.BlockSpec(memory_space=pltpu.VMEM)
    out_spaces = out_space if isinstance(out_space, list) else [out_space] * len(outs)
    out_specs = [vmem if s is None else pl.BlockSpec(memory_space=s) for s in out_spaces]
    specs = [vmem if s is None else pl.BlockSpec(memory_space=s) for s in (spaces or [None] * len(args))]
    if spaces:
        args = [
            pltpu.with_memory_space_constraint(a, pltpu.HBM) if s is pltpu.HBM else a for a, s in zip(args, spaces)
        ]
    run = pl.pallas_call(
        kernel,
        out_shape=[
            pltpu.HBM(s, d) if space is pltpu.HBM else jax.ShapeDtypeStruct(s, d)
            for (s, d), space in zip(outs, out_spaces)
        ],
        in_specs=specs,
        out_specs=out_specs,
        scratch_shapes=list(scratch),
        input_output_aliases=aliases or {},
        compiler_params=pltpu.CompilerParams(vmem_limit_bytes=limit << 20),
    )
    return run(*args)


def along(x, axis, by):
    count = lax.axis_size(axis)
    return lax.ppermute(x, axis, [(i, (i + by) % count) for i in range(count)])


def exchange(x, axis):
    return lax.all_to_all(x, axis, split_axis=0, concat_axis=0, tiled=True)


def swapped(v):
    return along(v, "core", 1)


def in_pairs(v, axis, first):
    count = lax.axis_size(axis)
    pairs = []
    for i in range(first, first + count, 2):
        a, b = i % count, (i + 1) % count
        pairs += [(a, b), (b, a)]
    return lax.ppermute(v, axis, pairs)


def neighbours(sends):
    return [in_pairs(sends[0], SUB, 1), in_pairs(sends[1], "x", 1), in_pairs(sends[2], "x", 0), swapped(sends[3])]


def label_of(n):
    return ((n // 4) % 2) * 128 + ((n // 8) % 4 * 4 + n % 4) * 8 + n // 32


def pack_kernel(
    block_hbm, corners_hbm, ids_hbm,
    s0, s1, s2, s3, labels, block, corners, wide_block, given, packs, sems,
):
    copies = [
        pltpu.make_async_copy(src, dst, sems.at[i])
        for i, (src, dst) in enumerate(
            ((block_hbm, wide_block), (corners_hbm, corners), (ids_hbm, given))
        )
    ]
    for copy in copies:
        copy.start()
    for copy in copies:
        copy.wait()
    count = corners.shape[0]
    labels[...] = jnp.full((1, 256), -1, jnp.int32)
    labels[:, :count] = label_of(given[...])
    text = labels[...].astype(F32).astype(BF16)
    x = wide_block[...].reshape(RHS, 2 * FACE)
    block[...] = x
    top = x.astype(BF16)
    rest = (x - top.astype(F32)).astype(BF16)
    for i, s in enumerate(SEG):
        if i % 2 == 0:
            packs[i, :RHS] = top[:, SEG[i // 2]]
            packs[i, RHS : 2 * RHS] = rest[:, SEG[i // 2]]
        else:
            packs[i, : 2 * RHS] = jnp.zeros((2 * RHS, FACE), BF16)
        packs[i, 2 * RHS : 2 * RHS + count] = corners[:, s]
        packs[i, 2 * RHS + count :] = jnp.broadcast_to(text, (8, FACE))
    put_sends([packs[i] for i in range(4)], (s0, s1, s2, s3))


def terms_of(load, u, wide, spread_t):
    both = dot2(dot2(jnp.concatenate([load * 0.5, u], axis=0), wide, NT), spread_t, NT)
    return both[:RHS], both[RHS:]


def lifted(z, wide, spread_t):
    return dot2(dot2(z, spread_t), wide)


def either(axis, even_branch, odd_branch):
    even = lax.axis_index(axis) % 2 == 0
    pl.when(even)(even_branch)
    pl.when(jnp.logical_not(even))(odd_branch)


def on_core(zero_branch, other_branch):
    either("core", zero_branch, other_branch)


def put_pair(axis, up, low, first, second):
    def even():
        first[...] = up
        second[...] = low

    def odd():
        first[...] = low
        second[...] = up

    either(axis, even, odd)


def put_sends(faces, outs):
    put_pair("core", faces[0], faces[1], outs[3], outs[0])
    put_pair("x", faces[2], faces[3], outs[2], outs[1])


def put_image(u, out, sends):
    out[...] = u
    put_sends([u[:, s] for s in SEG], sends)


def arrived(refs):
    values = [r[...] for r in refs]
    if values[0].dtype != F32:
        values = [v.astype(F32) for v in values]
    zero, even = lax.axis_index("core") == 0, lax.axis_index("x") % 2 == 0
    return [
        jnp.where(zero, values[3], values[0]),
        jnp.where(zero, values[0], values[3]),
        jnp.where(even, values[2], values[1]),
        jnp.where(even, values[1], values[2]),
    ]


def split_by_core(first, second, keep, send):
    def zero():
        keep[...] = first
        send[...] = second

    def one():
        keep[...] = second
        send[...] = first

    on_core(zero, one)


def high_low(x):
    top = x.astype(BF16).astype(F32)
    return top, x - top


def start_kernel(
    block, r0, r1, r2, r3, corners, labels, inverse, load_out, wide_out, spread_out, image, s0, s1, s2, s3,
):
    count = corners.shape[0]
    k = 2 * RHS
    next_sub, prev_sub, next_grp, prev_grp = arrived((r0, r1, r2, r3))
    load_out[:, SEG[0]] = block[:, :FACE]
    load_out[:, SEG[1]] = -(prev_sub[:RHS] + prev_sub[RHS:k])
    load_out[:, SEG[2]] = block[:, FACE:]
    load_out[:, SEG[3]] = -(prev_grp[:RHS] + prev_grp[RHS:k])
    put_image(dot2(load_out[...], inverse[...]), image, (s0, s1, s2, s3))
    wide_out[...] = jnp.zeros((SLOTS, WIDTH), BF16)
    wide_out[:count] = corners[...]
    others = (next_sub, prev_sub, next_grp, prev_grp)
    for i, other in enumerate(others):
        wide_out[SLOT * (i + 1) : SLOT * (i + 1) + count, SEG[i]] = (-other[k : k + count]).astype(BF16)
    lane = lax.broadcasted_iota(jnp.int32, (8, 256), 1)
    ids = jnp.where(lane < SLOT, jnp.broadcast_to(labels[...], (8, 256)).astype(F32), -1.0)
    for i, other in enumerate(others):
        moved = pltpu.roll(other[k + count :], SLOT * (i + 1), 1)
        mine = jnp.logical_and(lane >= SLOT * (i + 1), lane < SLOT * (i + 2))
        ids = jnp.where(mine, moved, ids)
    number = lax.broadcasted_iota(jnp.int32, (NCO, 256), 0).astype(F32)
    spread_out[...] = (number == ids[:1]).astype(F32).astype(BF16)


def fetch_kernel(bounds_hbm, inverse_hbm, row_hbm, out, coef, own_row, bounds, row, sems):
    limits = pltpu.make_async_copy(bounds_hbm, bounds, sems.at[2])
    limits.start()
    copy = pltpu.make_async_copy(row_hbm, row, sems.at[1])
    copy.start()
    fetch = pltpu.make_async_copy(inverse_hbm, out, sems.at[0])
    fetch.start()
    limits.wait()
    low, high = bounds[:, 0:1], bounds[:, 1:2]
    centre = jnp.broadcast_to((low + high) * 0.5, (1, WIDTH))
    inv = 1.0 / jnp.broadcast_to((high - low) * 0.5, (1, WIDTH))
    coef[...] = jnp.concatenate([centre, inv, 2.0 * inv, jnp.zeros((5, WIDTH), F32)], axis=0)
    n = lax.broadcasted_iota(jnp.int32, (NCO, NCO), 0)
    m = lax.broadcasted_iota(jnp.int32, (NCO, NCO), 1)
    order = (label_of(n) == m).astype(F32).astype(BF16)
    copy.wait()
    own_row[...] = dot2(jnp.broadcast_to(row[...], (RHS, NCO)), order)[:8]
    fetch.wait()


def moment_kernel(load0, image, wide_in, spread, inverse, keep, send, lifted_image):
    wide, spread_t = wide_in[...], spread[:, :SLOTS]
    pairs0 = bdot(wide, wide, NT) * 0.5
    wide_image = bdot(wide, inverse[...])
    top, low = halves_of(wide_image)
    top, low = halves_of(bdot(spread_t, top))
    lifted_image[:NCO] = top
    lifted_image[NCO:] = low
    pairs1 = dot2(wide_image, wide, NT)
    half = dot2(jnp.concatenate([pairs0, pairs1], axis=0), spread_t, NT)
    half = jnp.concatenate([half[:SLOTS], half[SLOTS:]], axis=1)
    top = half.astype(BF16)
    low = (half - top.astype(F32)).astype(BF16)
    both = bdot(spread_t, jnp.concatenate([top, low], axis=1))
    both = both[:, : 2 * NCO] + both[:, 2 * NCO :]
    w, g = terms_of(load0[...], image[...], wide, spread_t)

    def put(first, second):
        first[:NCO] = both[:, :NCO]
        first[NCO:] = w
        second[:NCO] = both[:, NCO:]
        second[NCO:] = g

    on_core(lambda: put(keep, send), lambda: put(send, keep))


def jumped(image, near):
    return [image[:, s] - n for s, n in zip(SEG, arrived(near), strict=True)]


def put_chain(u, lifts, sends):
    top = u.astype(BF16)
    low = (u - top.astype(F32)).astype(BF16)
    put_sends([jnp.concatenate([top[:, s], low[:, s], lifts[:, s]], axis=0) for s in SEG], sends)


def chain_jumps(u, own_lift, near):
    far = arrived(near)
    jump = jnp.concatenate([u[:, s] - (n[:RHS] + n[RHS : 2 * RHS]) for s, n in zip(SEG, far, strict=True)], axis=1)
    lift = [own_lift(s) - n[2 * RHS :] for s, n in zip(SEG, far, strict=True)]
    return jump, jnp.concatenate(lift, axis=1)


def join_kernel(
    coef, load0, n0, n1, n2, n3, image, wide_in, spread, inverse, lifted_image, keep, got,
    base1, jump0, image_x, s0, s1, s2, s3, out_hbm, out, sem,
):
    centre, inv, _ = terms_in(coef, WIDTH)
    jump = jnp.concatenate(jumped(image, (n0, n1, n2, n3)), axis=1)
    u = dot2(jump, inverse[...])
    g2 = dot2(dot2(u, wide_in[...], NT), spread[:, :SLOTS], NT)
    pieces = [high_low(keep[NCO:] + got[NCO:]), high_low(g2)]
    zero = jnp.zeros((4, NCO), F32)
    for p in range(16):
        rows = slice(16 * p, 16 * p + 16)
        small = [piece[part][p : p + 1] for part in range(2) for piece in pieces]
        out[p] = jnp.concatenate([keep[rows] + got[rows], *small, zero], axis=0).astype(BF16)
    copy = pltpu.make_async_copy(out, out_hbm, sem)
    copy.start()
    jump0[...] = jump
    base1[...] = (jump - centre * load0[...]) * inv
    image_x[...] = u
    put_chain(u, lifted_image[:NCO], (s0, s1, s2, s3))
    copy.wait()


def chain1_kernel(
    n0, n1, n2, n3, image_x, lifted_image, inverse_hbm,
    jump1, lift1_hbm, image_x2, lifted2, s0, s1, s2, s3, inverse, lift1, sends, sems,
):
    fetch = pltpu.make_async_copy(inverse_hbm, inverse, sems.at[0])
    fetch.start()

    def own_lift(s):
        return lifted_image[:NCO, s].astype(F32) + lifted_image[NCO:, s].astype(F32)

    jump, lift = chain_jumps(image_x[...], own_lift, (n0, n1, n2, n3))
    jump1[...] = jump
    top, low = halves_of(lift)
    lift1[:NCO] = top
    lift1[NCO:] = low
    store = pltpu.make_async_copy(lift1, lift1_hbm, sems.at[1])
    store.start()
    fetch.wait()
    u = dot2(jump, inverse[...])
    image_x2[...] = u
    lifts = bdot(top, inverse[...]).astype(BF16)
    put_chain(u, lifts, [sends.at[i] for i in range(4)])
    copies = [pltpu.make_async_copy(sends.at[i], s, sems.at[i + 2]) for i, s in enumerate((s0, s1, s2, s3))]
    for copy in copies:
        copy.start()
    lifted2[...] = lifts
    store.wait()
    for copy in copies:
        copy.wait()


def chain2_kernel(n0, n1, n2, n3, image_x2, lifted2, jump2, lift2):
    jump, lift = chain_jumps(image_x2[...], lambda s: lifted2[:, s].astype(F32), (n0, n1, n2, n3))
    jump2[...] = jump
    top, low = halves_of(lift)
    lift2[:NCO] = top
    lift2[NCO:] = low


def summed(got):
    total = got[0].astype(F32)
    for p in range(1, got.shape[0]):
        total = total + got[p].astype(F32)
    return total


def depth0_kernel(got, own_row, out):
    total = summed(got)
    g = total[16:18] + total[18:20]
    rows = [total[:16], *high_low(g), *high_low(own_row[:1]), jnp.zeros((2, NCO), F32)]
    value = jnp.concatenate(rows, axis=0).astype(BF16)
    for q in range(8):
        out[q] = value


def spread0_kernel(got, out):
    every = [got[q].astype(F32) for q in range(8)]
    total = functools.reduce(jnp.add, every)
    g = total[16:18] + total[18:20]
    rows = [total[:16], *high_low(g), jnp.zeros((4, NCO), F32)]
    rows += [r[20:21] for r in every] + [r[21:22] for r in every]
    value = jnp.concatenate(rows, axis=0).astype(BF16)
    for p in range(16):
        out[p] = value


def collect0_kernel(got, out):
    g = []
    for p in range(16):
        out[16 * p : 16 * p + 16] = got[p, :16]
        g.append(got[p, 16:24].astype(F32))
        out[320 + 8 * p : 328 + 8 * p] = got[p, 24:32]
        out[448 + 8 * p : 456 + 8 * p] = got[p, 32:40]
    out[256:320] = jnp.concatenate([r[i : i + 1] for i in range(4) for r in g], axis=0).astype(BF16)


def terms_in(coef, width):
    return coef[0:1, :width], coef[1:2, :width], coef[2:3, :width]


def fetch2_kernel(after, chain1_hbm, inverse_hbm, chain1, inverse, sems):
    copies = [
        pltpu.make_async_copy(chain1_hbm, chain1, sems.at[0]),
        pltpu.make_async_copy(inverse_hbm, inverse, sems.at[1]),
    ]
    for copy in copies:
        copy.start()
    for copy in copies:
        copy.wait()


def march_kernel(
    coef, own, got, load0, base1, jump0, jump1, jump2, chain2, spread, wide_in, chain1, inverse,
    coarse, m0, w0, w1, w2, load1, load2, load3, image3, low_sub, low_grp, m1, g1, g2,
):

    def put(first, second):
        for row, part in ((0, first), (128, second)):
            coarse[row : row + 128] = part[320:448]
            coarse[NCO + row : NCO + row + 128] = part[448:576]
        m0[...] = first[:NCO]
        m1[...] = second[:NCO]
        w0[...] = first[256:272].astype(F32) + first[288:304].astype(F32)
        g1[...] = second[256:272].astype(F32) + second[288:304].astype(F32)
        parts = [part[i : i + RHS].astype(F32) for part in (first, second) for i in (272, 304)]
        g2[...] = functools.reduce(jnp.add, parts)

    on_core(lambda: put(own, got), lambda: put(got, own))
    centre, inv, alpha = terms_in(coef, NCO)
    w = w0[...]
    z = dot_halves(w, coarse[...])
    after = (g1[...] + dot2(z, m0[...]) - centre * w) * inv
    w1[...] = after
    z1 = dot_halves(after, coarse[...])
    image = (g2[...] + dot2(z, m1[...]) - centre * g1[...]) * inv
    last = alpha * (image + dot2(z1, m0[...]) - centre * after) - w
    w2[...] = last
    z2 = dot_halves(last, coarse[...])
    both = jnp.concatenate([z, z1, z2], axis=0)
    lift = lifted(both, wide_in[...], spread[:, :SLOTS])
    far = dot_halves(z, chain2[...])
    near = dot_halves(both[: 2 * RHS], chain1[...])
    centre, inv, alpha = terms_in(coef, WIDTH)
    x1 = base1[...] + inv * lift[:RHS]
    load1[...] = x1
    j1 = inv * (jump1[...] + near[:RHS] - centre * jump0[...])
    x2 = alpha * (j1 + lift[RHS : 2 * RHS] - centre * x1) - load0[...]
    load2[...] = x2
    jj1 = inv * (jump2[...] + far - centre * jump1[...])
    j2 = alpha * (jj1 + near[RHS:] - centre * j1) - jump0[...]
    x3 = alpha * (j2 + lift[2 * RHS :] - centre * x2) - x1
    load3[...] = x3
    u = bdot(x3.astype(BF16), inverse[...])
    image3[...] = u
    low_sub[...] = u[:, SEG[1]]
    low_grp[...] = u[:, SEG[3]]


def terms_kernel(coef, block, load1, load2, load3, image, spread, wide_in, stack, partial4, keep, send):
    centre, _, alpha = terms_in(coef, FACE)
    w, g = terms_of(load3[...], image[...], wide_in[...], spread[:, :SLOTS])
    left, right = slice(0, FACE), slice(FACE, 2 * FACE)
    stack[:RHS] = block[...]
    for level, load in ((1, load1), (2, load2), (3, load3)):
        stack[level * RHS : (level + 1) * RHS, left] = load[:, SEG[0]]
        stack[level * RHS : (level + 1) * RHS, right] = load[:, SEG[2]]
    for half, s in ((left, SEG[0]), (right, SEG[2])):
        partial4[:, half] = alpha * (image[:, s] - centre * load3[:, s]) - load2[:, s]
    known = jnp.concatenate([stack[...], jnp.zeros((64, 2 * FACE), F32)], axis=0)
    terms = hdot(stack[...], known, NT)
    t = [terms[i * RHS : (i + 1) * RHS] for i in range(BLOCKS - 1)]
    lane = lax.broadcasted_iota(jnp.int32, (RHS, 128), 1)
    first = jnp.where(lane < 64, t[0], pltpu.roll(t[1], 48, 1))
    second = jnp.where(lane < 32, pltpu.roll(t[2], 96, 1), pltpu.roll(t[3], 112, 1))
    split_by_core(
        jnp.concatenate([w, jnp.zeros((RHS, NCO), F32)], axis=0),
        jnp.concatenate([g, jnp.concatenate([first, second], axis=1)], axis=0),
        keep,
        send,
    )


def coded(total):
    zero = lax.axis_index("core") == 0
    return jnp.where(zero, jnp.concatenate(high_low(total[:RHS]), axis=0), total)


def decoded(total):
    zero = lax.axis_index("core") == 0
    whole = jnp.concatenate([total[:RHS] + total[RHS:], jnp.zeros((RHS, NCO), F32)], axis=0)
    return jnp.where(zero, whole, total)


def gram_kernel(coef, stack, partial4, n0, n2, keep, got, known4, out):
    _, _, alpha = terms_in(coef, FACE)
    known4[:, :FACE] = partial4[:, :FACE] - alpha * n0[...]
    known4[:, FACE:] = partial4[:, FACE:] - alpha * n2[...]
    q = known4[...]
    row = hdot(q, jnp.concatenate([stack[...], q, jnp.zeros((48, 2 * FACE), F32)], axis=0), NT)
    row = jnp.concatenate([row[:8], row[8:]], axis=1)
    value = jnp.concatenate([coded(keep[...] + got[...]), row], axis=0).astype(BF16)
    for p in range(16):
        out[p] = value


def depth1_kernel(got, out):
    total = summed(got)
    value = jnp.concatenate([coded(decoded(total[: 2 * RHS])), total[2 * RHS :]], axis=0).astype(BF16)
    for q in range(8):
        out[q] = value


def sum_kernel(got, out):
    total = summed(got)
    out[: 2 * RHS] = decoded(total[: 2 * RHS])
    out[2 * RHS :] = total[2 * RHS :]


def store_kernel(stack, basis_hbm, basis, sem):
    for level in range(BLOCKS - 1):
        basis[level] = stack[level * RHS : (level + 1) * RHS].reshape(RHS, 1, 1, 2 * FACE)
    copy = pltpu.make_async_copy(basis, basis_hbm.at[: BLOCKS - 1], sem)
    copy.start()
    copy.wait()


def final_kernel(
    coef, own, got, coarse, matrix, w0, w1, w2, known4, spread, wide_in, stored,
    basis_hbm, gram_hbm, block4, gram, square, sems,
):
    centre, _, alpha = terms_in(coef, NCO)
    zero = lax.axis_index("core") == 0
    w3 = jnp.where(zero, own[:RHS], got[:RHS])
    second = jnp.where(zero, got[: 2 * RHS], own[: 2 * RHS])
    g3, packed = second[:RHS], second[RHS:]
    row = own[2 * RHS :] + got[2 * RHS :]
    row = jnp.concatenate([row[:, :128], row[:, 128:]], axis=0)
    z3 = dot_halves(w3, coarse[...])
    lift = lifted(z3, wide_in[...], spread[:, :SLOTS])
    value = jnp.concatenate(
        [known4[:, :FACE] + alpha * lift[:, SEG[0]], known4[:, FACE:] + alpha * lift[:, SEG[2]]], axis=1
    )
    block4[...] = value.reshape(RHS, 1, 1, 2 * FACE)
    late = pltpu.make_async_copy(block4, basis_hbm.at[BLOCKS - 1], sems.at[0])
    late.start()
    wk = alpha * (g3 - centre * w3) - w2[...]
    z_row = jnp.concatenate([jnp.zeros((64, NCO), F32), z3, jnp.zeros((48, NCO), F32)], axis=0)
    rows = jnp.concatenate([w0[...], w1[...], w2[...], w3, wk, dot2(z3, matrix[...])], axis=0)
    cross = hdot(rows, z_row, NT)
    alpha = alpha[:, :128]
    h0, h1 = packed[:, :128], packed[:, 128:]
    parts = [h0, pltpu.roll(h0, 80, 1), pltpu.roll(h1, 32, 1), pltpu.roll(h1, 16, 1)]
    lane = lax.broadcasted_iota(jnp.int32, (RHS, 128), 1)
    for i in range(BLOCKS - 1):
        rows = slice(i * RHS, (i + 1) * RHS)
        square[rows] = jnp.where(lane < 64, parts[i], 0.0) + alpha * cross[rows]
    last = slice(4 * RHS, 5 * RHS)
    square[last] = alpha * alpha * cross[5 * RHS :] + jnp.where(lane < 64, 0.0, row)
    square[5 * RHS :] = jnp.zeros((48, 128), F32)
    own4 = jnp.where(lane < 64, row, alpha * cross[last])
    column = jnp.concatenate([jnp.zeros((64, 128), F32), own4, jnp.zeros((48, 128), F32)], axis=0)
    up = square[...]
    r = lax.broadcasted_iota(jnp.int32, (128, 128), 0) // RHS
    c = lax.broadcasted_iota(jnp.int32, (128, 128), 1) // RHS
    sided = jnp.where(r < c, up, 0.0) + column
    whole = jnp.where(r == c, up, 0.0) + sided + sided.T
    gram[...] = (whole * (1.0 / (2 * FACE * 64)))[: BLOCKS * RHS, : BLOCKS * RHS]
    result = pltpu.make_async_copy(gram, gram_hbm, sems.at[1])
    result.start()
    late.wait()
    result.wait()


def body(residual, bounds, local_inverse, corner_basis, corner_map, coarse_inverse):
    inverse = local_inverse.reshape(WIDTH, WIDTH)
    corners = corner_basis.reshape(-1, WIDTH)
    count = corners.shape[0]
    face = ((RHS, FACE), F32)
    load = ((RHS, WIDTH), F32)
    small = ((RHS, NCO), F32)
    half = ((RHS, 2 * FACE), F32)
    blocks = ((BLOCKS, RHS, 1, 1, 2 * FACE), F32)
    hbm = pltpu.HBM

    *packs, labels, block, corners = call(
        pack_kernel,
        [((64, FACE), BF16)] * 4 + [((1, 256), jnp.int32), half, ((count, WIDTH), BF16)],
        [residual, corners, corner_map.reshape(1, count)],
        [hbm] * 3,
        [pltpu.VMEM((RHS, 1, 1, 2 * FACE), F32), pltpu.VMEM((1, count), jnp.int32), pltpu.VMEM((4, 64, FACE), BF16),
         pltpu.SemaphoreType.DMA((3,))],
    )
    near = neighbours(packs)
    inverse, coef, own_row = call(
        fetch_kernel,
        [((WIDTH, WIDTH), BF16), ((8, WIDTH), F32), ((8, NCO), F32)],
        [bounds.reshape(1, 2), inverse, coarse_inverse],
        [hbm, hbm, hbm],
        [pltpu.VMEM((1, 2), F32), pltpu.VMEM((1, NCO), F32), pltpu.SemaphoreType.DMA((3,))],
    )
    load0, wide, spread, image0, *sends = call(
        start_kernel,
        [load, ((SLOTS, WIDTH), BF16), ((NCO, 256), BF16), load, face, face, face, face],
        [block, *near, corners, labels, inverse],
    )
    near0 = neighbours(sends)
    keep, send, lifted_image = call(
        moment_kernel,
        [((272, NCO), F32), ((272, NCO), F32), ((2 * NCO, WIDTH), BF16)],
        [load0, image0, wide, spread, inverse],
    )
    got = swapped(send)
    chain = ((2 * RHS + NCO, FACE), BF16)
    table = ((2 * NCO, WIDTH), BF16)
    base1, jump0, image_x, *sends, v = call(
        join_kernel,
        [load, load, load, chain, chain, chain, chain, ((16, 24, NCO), BF16)],
        [coef, load0, *near0, image0, wide, spread, inverse, lifted_image, keep, got],
        scratch=[pltpu.VMEM((16, 24, NCO), BF16), pltpu.SemaphoreType.DMA(())],
        out_space=[None] * 7 + [hbm],
    )
    near1 = neighbours(sends)
    (v,) = call(depth0_kernel, [((8, 24, NCO), BF16)], [exchange(v, PLANE), own_row])
    jump1, chain1, image_x2, lifted2, *sends = call(
        chain1_kernel,
        [load, table, load, ((NCO, WIDTH), BF16), chain, chain, chain, chain],
        [*near1, image_x, lifted_image, local_inverse.reshape(WIDTH, WIDTH)],
        [None] * 6 + [hbm],
        [pltpu.VMEM((WIDTH, WIDTH), BF16), pltpu.VMEM((2 * NCO, WIDTH), BF16), pltpu.VMEM((4, *chain[0]), BF16),
         pltpu.SemaphoreType.DMA((6,))],
        out_space=[None, hbm, None, None] + [hbm] * 4,
    )
    near2 = neighbours(sends)
    (v,) = call(spread0_kernel, [((16, 40, NCO), BF16)], [exchange(v, "z")])
    (own,) = call(collect0_kernel, [((576, NCO), BF16)], [exchange(v, PLANE)])
    got = swapped(own)
    chain1, inverse = call(
        fetch2_kernel,
        [table, ((WIDTH, WIDTH), BF16)],
        [own, chain1, local_inverse.reshape(WIDTH, WIDTH)],
        [None, hbm, hbm],
        [pltpu.SemaphoreType.DMA((2,))],
    )
    jump2, chain2 = call(chain2_kernel, [load, table], [*near2, image_x2, lifted2])

    coarse, m0, w0, w1, w2, load1, load2, load3, image3, low_sub, low_grp = call(
        march_kernel,
        [((2 * NCO, NCO), BF16), ((NCO, NCO), BF16), small, small, small, load, load, load, load, face, face],
        [coef, own, got, load0, base1, jump0, jump1, jump2, chain2, spread, wide, chain1, inverse],
        scratch=[pltpu.VMEM((NCO, NCO), BF16), pltpu.VMEM((RHS, NCO), F32), pltpu.VMEM((RHS, NCO), F32)],
    )
    n0 = along(low_sub, SUB, -1)
    n2 = along(low_grp, "x", -1)
    stack, partial4, keep, send = call(
        terms_kernel,
        [((4 * RHS, 2 * FACE), F32), half, ((32, NCO), F32), ((32, NCO), F32)],
        [coef, block, load1, load2, load3, image3, spread, wide],
    )
    got = swapped(send)
    known4, v = call(
        gram_kernel,
        [half, ((16, 40, NCO), BF16)],
        [coef, stack, partial4, n0, n2, keep, got],
    )
    (stored,) = call(
        store_kernel,
        [blocks],
        [stack],
        scratch=[pltpu.VMEM((BLOCKS - 1, RHS, 1, 1, 2 * FACE), F32), pltpu.SemaphoreType.DMA(())],
        out_space=hbm,
    )
    (v,) = call(depth1_kernel, [((8, 40, NCO), BF16)], [exchange(v, PLANE)])
    (own,) = call(sum_kernel, [((40, NCO), F32)], [exchange(v, "z")])
    basis, gram = call(
        final_kernel,
        [blocks, ((BLOCKS * RHS, BLOCKS * RHS), F32)],
        [coef, own, swapped(own), coarse, m0, w0, w1, w2, known4, spread, wide, stored],
        [None] * 11 + [hbm],
        [pltpu.VMEM((RHS, 1, 1, 2 * FACE), F32), pltpu.VMEM((BLOCKS * RHS, BLOCKS * RHS), F32),
         pltpu.VMEM((128, 128), F32), pltpu.SemaphoreType.DMA((2,))],
        out_space=hbm,
        aliases={11: 0},
    )
    return basis, gram


def solution(mesh):
    split = Mesh(mesh.devices.reshape(8, 4, 2, mesh.shape["grp"]), ("z", "y", "core", "x"))
    in_specs = (
        P(None, SUB, "x", None),
        P(),
        P(SUB, "x", None, None),
        P(SUB, "x", None, None),
        P(SUB, "x", None),
        P(("z", "y", "core", "x"), None),
    )
    out_specs = (P(None, None, SUB, "x", None), P())
    return jax.shard_map(body, mesh=split, in_specs=in_specs, out_specs=out_specs, check_vma=False)
```
